32 devices in a mesh: gz: 2 (over core), gy: 8 (over z, y), gx: 2 (over x).
Axes of the slice: x: 2, y: 2, z: 4, core: 2. Of those that a mesh axis runs over, the one named last changes fastest.
Arguments:
- fixed: bfloat16 [32, 512, 256], P('gz', 'gy', 'gx'), may hold values from -6 to 6
- moving: bfloat16 [32, 512, 256], P('gz', 'gy', 'gx'), may hold values from -6 to 6
- owners: int32 [2, 8, 2, 256, 1], P('gz', 'gy', 'gx'), may hold values from 0 to 15; in each aligned block of 256 rows (0 to 255, 256 to 511, ..., all dimensions but the last counted through in order) at most 32 rows name the same one
- block_ids: int32 [2, 8, 2, 256], P('gz', 'gy', 'gx'), may hold values from 0 to 127
- counts: int32 [2, 8, 2, 128], P('gz', 'gy', 'gx'), may hold values from 1 to 2
- mix_yx: bfloat16 [2, 8, 2, 256, 128, 128], P('gz', 'gy', 'gx')
- mix_z: float32 [2, 8, 2, 256, 8, 8], P('gz', 'gy', 'gx')
Outputs:
- warped: float32 [32, 512, 256], P('gz', 'gy', 'gx')
- force: float32 [3, 32, 512, 256], P(None, 'gz', 'gy', 'gx')
The draws below stay inside these ranges and needn't reach their ends.
Inputs may be any that keep to these rules, and one draw needn't show every extreme that they name: `owners`: owner o names the device with the same gz index, gy index o // 2 and gx index o % 2; within one device's 256 requests no owner is named more than 32 times.
All inputs are finite; a program needn't handle non-finite values.
Results may differ from the reference program's by a relative error of at most 0.00035.
Values may be sent and summed in bfloat16 or wider, within the bound.
No kernel may reach another device: no remote copies, remote signals or barrier semaphores. Data moves between devices by JAX's collectives and lax.ppermute only.
A program may use at most 128 MiB of HBM per device.

```python
import math
import jax
import jax.numpy as jnp
import numpy as np
from jax import lax

VZ = 8
VY = 8
VX = 16
NBZ = 2
NBY = 8
NBX = 8
SOURCES = 2
RAD = 4
BV = 128
BLOCKS = 128
SLOTS = 256
CAP = 32
NZ = 32
NY = 512
NX = 256
N_GZ = 2
N_GY = 8
N_GX = 2


def dominant(key, side):
    shape = (N_GZ, N_GY, N_GX, SLOTS, side, side)
    first, second = jax.random.split(key)
    eye = (lax.broadcasted_iota(jnp.int32, (side, side), 0) == lax.broadcasted_iota(jnp.int32, (side, side), 1)).astype(jnp.float32)
    noise = 0.35 * jax.random.normal(first, shape, jnp.float32)
    diag = jax.random.uniform(second, shape[:-1] + (1,), jnp.float32, 0.5, 1.2)
    return eye * diag + (1.0 - eye) * noise / math.sqrt(side)


def draw_mix_yx(key, part):
    return dominant(jax.random.fold_in(key, 11), BV).astype(jnp.bfloat16)


def draw_mix_z(key, part):
    return dominant(jax.random.fold_in(key, 23), VZ).astype(jnp.float32)


def touch_ends(values, stream_key, smallest, high):
    place = [jax.random.randint(jax.random.fold_in(stream_key, axis), (), 0, length) for axis, length in enumerate(values.shape)]
    longest = values.shape.index(max(values.shape))
    next_to = place[:longest] + [(place[longest] + 1) % values.shape[longest]] + place[longest + 1:]
    return values.at[tuple(place)].set(smallest).at[tuple(next_to)].set(high)


def levels(own_key, extent, shards, low, largest):
    def one(position, parts):
        draws = jax.random.uniform(jax.random.fold_in(jax.random.fold_in(own_key, 6), position), (parts,), jnp.float32, low / len(shards), largest / len(shards))
        return jnp.repeat(jnp.exp(draws), extent[position] // parts).reshape((-1,) + (1,) * (len(extent) - position - 1))

    level = one(*shards[0])
    for cut in shards[1:]:
        level = level * one(*cut)
    return level


def deal_out(rng, own, number, rows, count, top, bound, slope):
    ranking = jax.random.permutation(rng, count)
    heavy_load, usual = portions_of(count, rows * top, bound, slope, True), portions_of(count, rows * top, bound, slope, False)
    places = jnp.arange(count)

    def named(sizes, offset_by):
        used = int((sizes > 0).sum())
        fixed = max(1, used // 4)
        moved = fixed + (places - fixed + offset_by * (used - fixed)) % max(1, count - fixed)
        return jnp.zeros((count,), jnp.int32).at[ranking[jnp.where(places < fixed, places, moved)]].set(jnp.asarray(sizes, jnp.int32))

    sizes = jnp.where(number % 4 == 0, named(heavy_load, number // 4), named(usual, number - number // 4 - 1))
    mixed = jax.random.permutation(jax.random.fold_in(own, 3), count)
    donor, sink = mixed[0:count // 2 * 2:2], mixed[1:count // 2 * 2:2]
    slack = jnp.minimum(sizes[donor] - 1, bound - sizes[sink]) // 2
    slack = jnp.where((donor == ranking[0]) | (sink == ranking[0]) | (sizes[sink] == 0), 0, jnp.maximum(slack, 0))
    moved = jax.random.randint(jax.random.fold_in(own, 4), (count // 2,), 0, 1 << 20) % (slack + 1)
    sizes = sizes.at[donor].add(-moved).at[sink].add(moved)
    labels = jnp.searchsorted(jnp.cumsum(sizes), jnp.arange(rows * top), side="right").astype(jnp.int32)
    table = labels.reshape(top, rows).T
    table = table[jax.random.permutation(jax.random.fold_in(own, 1), rows)]
    offset_by = jax.random.randint(jax.random.fold_in(own, 2), (rows, 1), 0, top)
    return jnp.take_along_axis(table, (jnp.arange(top)[None, :] + offset_by) % top, axis=1)


def portions_of(count, total, bound, skew, full):
    weights = [(1 << 20) // math.isqrt(grade ** skew) + 1 for grade in range(1, count + 1)]
    largest = bound if full else min(bound, max(-(-total // count), total * weights[0] // sum(weights)))
    least = 1 if total - largest >= count - 1 else 0
    given, surplus = [largest] + [least] * (count - 1), total - largest - least * (count - 1)
    while surplus > 0:
        candidates = [i for i in range(1, count) if given[i] < largest] or [i for i in range(1, count) if given[i] < bound]
        mass, remaining = sum([weights[i] for i in candidates]), surplus
        for i in candidates:
            more = min(bound - given[i], max(1, remaining * weights[i] // mass), surplus)
            given[i] = given[i] + more
            surplus = surplus - more
    return np.array(given)


def normal_values(rng, extent, deviation, most, shards=(), kind=jnp.bfloat16):
    loudness = levels(rng, extent, shards, -0.22, 0.18) if shards else 1.0
    array = jax.random.normal(rng, extent, jnp.float32) * deviation * loudness
    return jnp.minimum(jnp.maximum(array, -most), most).astype(kind)


def setup_inputs(seed: int = 0) -> dict:
    streams_of = jax.random.split(jax.random.key(seed), 8)
    fixed = normal_values(streams_of[0], (NZ, NY, NX), 1.0, 6.0, ((0, 2), (1, 8), (2, 2)))
    moving = normal_values(streams_of[1], (NZ, NY, NX), 1.0, 6.0, ((0, 2), (1, 8), (2, 2)))
    owners_keys = jax.random.split(jax.random.fold_in(streams_of[2], 1), N_GZ * N_GY * N_GX * SLOTS // SLOTS)
    owners_turns = jax.random.permutation(jax.random.fold_in(streams_of[2], 3), N_GZ * N_GY * N_GX * SLOTS // SLOTS)
    owners = jax.vmap(lambda own, number: deal_out(jax.random.fold_in(streams_of[2], 2), own, number, SLOTS, N_GY * N_GX, 1, CAP, 2))(owners_keys, owners_turns).reshape((N_GZ, N_GY, N_GX, SLOTS, 1))
    block_ids = touch_ends(jax.random.randint(streams_of[3], (N_GZ, N_GY, N_GX, SLOTS), 0, BLOCKS), jax.random.fold_in(streams_of[3], 1), 0, BLOCKS - 1).astype(jnp.int32)
    counts = touch_ends(jax.random.randint(streams_of[4], (N_GZ, N_GY, N_GX, BLOCKS), 1, SOURCES + 1), jax.random.fold_in(streams_of[4], 1), 1, SOURCES).astype(jnp.int32)
    mix_yx = draw_mix_yx(jax.random.fold_in(streams_of[7], 71), 0)
    mix_z = draw_mix_z(jax.random.fold_in(streams_of[7], 71), 0)
    return dict(fixed=fixed, moving=moving, owners=owners, block_ids=block_ids, counts=counts, mix_yx=mix_yx, mix_z=mix_z)


def box_along(padded, axis):
    length = padded.shape[axis] - 2 * RAD
    total = lax.slice_in_dim(padded, 0, length, axis=axis)
    for shift in range(1, 2 * RAD + 1):
        total = total + lax.slice_in_dim(padded, shift, shift + length, axis=axis)
    return total


def reference(fixed, moving, owners, block_ids, counts, mix_yx, mix_z):
    groups = N_GY * N_GX
    devices = N_GZ * groups
    order = (0, 3, 6, 1, 4, 7, 2, 5, 8)
    mblocks = moving.reshape(N_GZ, NBZ, VZ, N_GY, NBY, VY, N_GX, NBX, VX).transpose(order)
    mblocks = mblocks.reshape(N_GZ * groups, BLOCKS, VZ, BV)
    owner = owners.reshape(N_GZ, groups, SLOTS).astype(jnp.int32)
    ident = block_ids.reshape(N_GZ, groups, SLOTS).astype(jnp.int32)
    plane = (jnp.arange(N_GZ, dtype=jnp.int32) * groups)[:, None, None]
    source = mblocks[plane + owner, ident].reshape(devices, SLOTS, VZ, BV)
    weights_yx = mix_yx.reshape(devices, SLOTS, BV, BV)
    weights_z = mix_z.reshape(devices, SLOTS, VZ, VZ)
    used = counts.reshape(devices, BLOCKS).astype(jnp.int32)
    slot_pos = jnp.arange(SLOTS, dtype=jnp.int32)

    def one_device(items):
        src, wyx, wz, cnt = items
        inplane = jnp.einsum("szc,scd->szd", src.astype(jnp.float32), wyx.astype(jnp.float32))
        resampled = jnp.einsum("szy,syd->szd", wz, inplane, precision=lax.Precision.HIGHEST)
        keep = (slot_pos % SOURCES) < cnt[slot_pos // SOURCES]
        resampled = jnp.where(keep[:, None, None], resampled, jnp.float32(0.0))
        return resampled.reshape(BLOCKS, SOURCES, VZ, BV).sum(axis=1)

    wblocks = lax.map(one_device, (source, weights_yx, weights_z, used))
    warped = wblocks.reshape(N_GZ, N_GY, N_GX, NBZ, NBY, NBX, VZ, VY, VX).transpose(order).reshape(NZ, NY, NX)

    image = fixed.astype(jnp.float32)
    fields = jnp.stack([image, warped, image * image, warped * warped, image * warped])
    padded = jnp.pad(fields, ((0, 0), (RAD, RAD), (RAD, RAD), (RAD, RAD)))
    sums = box_along(box_along(box_along(padded, 1), 2), 3)
    count = float((2 * RAD + 1) ** 3)
    mean_f = sums[0] / count
    mean_w = sums[1] / count
    cov = sums[4] / count - mean_f * mean_w
    var_f = sums[2] / count - mean_f * mean_f
    var_w = sums[3] / count - mean_w * mean_w
    deriv = 2.0 * cov / ((var_f + 1e-5) * (var_w + 1e-5)) * ((image - mean_f) - cov / (var_w + 1e-5) * (warped - mean_w))
    wpad = jnp.pad(warped, 1)
    slope_z = (wpad[2:, 1:-1, 1:-1] - wpad[:-2, 1:-1, 1:-1]) * 0.5
    slope_y = (wpad[1:-1, 2:, 1:-1] - wpad[1:-1, :-2, 1:-1]) * 0.5
    slope_x = (wpad[1:-1, 1:-1, 2:] - wpad[1:-1, 1:-1, :-2]) * 0.5
    force = jnp.stack([deriv * slope_z, deriv * slope_y, deriv * slope_x])
    return warped, force
```

```python
import jax
import jax.numpy as jnp
from jax import lax
from jax.experimental import pallas as pl
from jax.experimental.pallas import tpu as pltpu
from jax.sharding import PartitionSpec as P

VZ = 8
VY = 8
VX = 16
NBZ = 2
NBY = 8
NBX = 8
SOURCES = 2
RAD = 4
BV = VY * VX
BLOCKS = NBZ * NBY * NBX
SLOTS = BLOCKS * SOURCES
NZ = NBZ * VZ
NY = NBY * VY
NX = NBX * VX
GROUPS = NBZ * NBY
PER = NBX * SOURCES
ROWS = PER * VZ
BRICKS = ("gy", "gx")
F32 = jnp.float32
BF16 = jnp.bfloat16

VMEM = pl.BlockSpec(memory_space=pltpu.VMEM)
SMEM = pl.BlockSpec(memory_space=pltpu.SMEM)


def iota(shape, dim):
    return lax.broadcasted_iota(jnp.int32, shape, dim)


def pieces(value, count):
    parts = []
    for _ in range(count - 1):
        part = value.astype(BF16)
        parts.append(part)
        value = value - part.astype(F32)
    parts.append(value.astype(BF16))
    return parts


def swap_chunks(rows):
    chunk = iota((VZ, BV), 1) // VX
    for k in (1, 2, 4):
        low = (chunk & k) == 0
        out = list(rows)
        for b in range(8):
            if b & k == 0:
                first, second = rows[b], rows[b + k]
                out[b] = jnp.where(low, first, pltpu.roll(second, k * VX, 1))
                out[b + k] = jnp.where(low, pltpu.roll(first, BV - k * VX, 1), second)
        rows = out
    return rows


def prepare_kernel(half_ref, moving_ref, owner_ref, ident_ref, blocks_ref, request_ref, flat_ref, wide):
    holders, _, width = request_ref.shape
    capacity = width // 2
    half = half_ref[0]
    owner = owner_ref[...]
    ident = ident_ref[...].astype(F32)
    groups = 2 * holders
    named = jnp.where(owner == iota((groups, SLOTS), 0), 1.0, 0.0)
    earlier = jnp.where(iota((SLOTS, SLOTS), 0) < iota((SLOTS, SLOTS), 1), 1.0, 0.0).astype(BF16)
    before = jnp.dot(named.astype(BF16), earlier, preferred_element_type=F32)
    rank = jnp.sum(named * before, axis=0, keepdims=True).astype(jnp.int32)
    upper = jnp.where(owner >= holders, 1, 0)
    holder = owner - upper * holders
    place = jnp.where(upper == half, 0, capacity) + rank
    flat_ref[...] = holder * width + place
    wanted = jnp.where(holder == iota((holders, SLOTS), 0), ident, 0.0).astype(BF16)
    at = jnp.where(place == iota((width, SLOTS), 0), 1.0, 0.0).astype(BF16)
    request = lax.dot_general(wanted, at, (((1,), (1,)), ((), ())), preferred_element_type=F32).astype(jnp.int32)
    for h in range(holders):
        request_ref[h] = request[h : h + 1, :]
    for z in range(NZ):
        wide[z * NY : (z + 1) * NY, :] = moving_ref[z].astype(F32)

    def group(g, _):
        start = (g // NBY) * (VZ * NY) + (g % NBY) * VY
        rows = [wide[pl.ds(start + y, VZ, stride=NY), :] for y in range(VY)]
        for x, block in enumerate(swap_chunks(rows)):
            blocks_ref[g * NBX + x] = block.astype(BF16)
        return 0

    lax.fori_loop(0, GROUPS, group, 0)


def prepare(half, moving, owner, ident, groups, capacity):
    holders = groups // 2
    return pl.pallas_call(
        prepare_kernel,
        out_shape=(
            jax.ShapeDtypeStruct((BLOCKS, VZ, BV), BF16),
            jax.ShapeDtypeStruct((holders, 1, 2 * capacity), jnp.int32),
            jax.ShapeDtypeStruct((1, SLOTS), jnp.int32),
        ),
        in_specs=[SMEM, VMEM, VMEM, VMEM],
        out_specs=(VMEM, VMEM, VMEM),
        scratch_shapes=[pltpu.VMEM((NZ * NY, NX), F32)],
        name="prepare",
    )(half, moving, owner, ident)


def pick_kernel(capacity, request_ref, near_ref, far_ref, out_ref):
    width = 2 * capacity

    def holder(h, _):
        for k in range(width):
            source = near_ref if k < capacity else far_ref
            out_ref[h * width + k] = source[request_ref[h * width + k]]
        return 0

    lax.fori_loop(0, out_ref.shape[0] // width, holder, 0)


def pick(request, near, far, capacity):
    return pl.pallas_call(
        lambda *refs: pick_kernel(capacity, *refs),
        out_shape=jax.ShapeDtypeStruct((request.shape[0], VZ, BV), BF16),
        in_specs=[SMEM, VMEM, VMEM],
        out_specs=VMEM,
        name="pick",
    )(request, near, far)


def spread_kernel(mix_ref, out_ref):
    pick_lane = jnp.where(iota((VZ, ROWS), 1) % VZ == iota((VZ, ROWS), 0), 1.0, 0.0).astype(BF16)
    same = iota((ROWS, ROWS), 0) // VZ == iota((ROWS, ROWS), 1) // VZ

    def group(g, _):
        weights = mix_ref[pl.ds(pl.multiple_of(g * ROWS, ROWS), ROWS), :]
        for k, part in enumerate(pieces(weights, 3)):
            tiled = jnp.dot(part, pick_lane, preferred_element_type=F32)
            out_ref[g, k * ROWS : (k + 1) * ROWS, :] = jnp.where(same, tiled, 0.0).astype(BF16)
        return 0

    lax.fori_loop(0, GROUPS, group, 0)


def spread(mix_z):
    return pl.pallas_call(
        spread_kernel,
        out_shape=jax.ShapeDtypeStruct((GROUPS, 3 * ROWS, ROWS), BF16),
        in_specs=[VMEM],
        out_specs=VMEM,
        name="spread",
    )(mix_z)


STEP = 2


def mix_kernel(flat_ref, received_ref, spread_ref, mix_ref, warped_ref, source):
    step = pl.program_id(0)
    for q in range(STEP):
        g = step * STEP + q
        for i in range(PER):
            source[i * VZ : (i + 1) * VZ, :] = received_ref[flat_ref[g * PER + i]].astype(F32)
        parts = jnp.dot(spread_ref[q], source[...].astype(BF16), preferred_element_type=F32)
        mixed = parts[:ROWS] + parts[ROWS : 2 * ROWS] + parts[2 * ROWS :]
        high = mixed.astype(BF16).astype(F32)
        low = mixed - high
        rows = []
        for j in range(NBX):
            a = slice(2 * j * VZ, (2 * j + 1) * VZ)
            b = slice((2 * j + 1) * VZ, (2 * j + 2) * VZ)
            left = jnp.concatenate(
                [jnp.concatenate([high[a], high[b]], 1), jnp.concatenate([low[a], low[b]], 1)], 0
            ).astype(BF16)
            right = mix_ref[q * PER + 2 * j : q * PER + 2 * j + 2].reshape(2 * BV, BV)
            both = jnp.dot(left, right, preferred_element_type=F32)
            rows.append(both[:VZ] + both[VZ:])
        start = (g // NBY) * (VZ * NY) + (g % NBY) * VY
        for y, row in enumerate(swap_chunks(rows)):
            warped_ref[pl.ds(start + y, VZ, stride=NY), :] = row


def mix(flat, received, spread_z, mix_yx):
    return pl.pallas_call(
        mix_kernel,
        grid_spec=pltpu.PrefetchScalarGridSpec(
            num_scalar_prefetch=1,
            grid=(GROUPS // STEP,),
            in_specs=[
                pl.BlockSpec(received.shape, lambda i, f: (0, 0, 0)),
                pl.BlockSpec((STEP, 3 * ROWS, ROWS), lambda i, f: (i, 0, 0)),
                pl.BlockSpec((STEP * PER, BV, BV), lambda i, f: (i, 0, 0)),
            ],
            out_specs=pl.BlockSpec((NZ * NY, NX), lambda i, f: (0, 0)),
            scratch_shapes=[pltpu.VMEM((ROWS, BV), F32)],
        ),
        out_shape=jax.ShapeDtypeStruct((NZ * NY, NX), F32),
        name="mix",
    )(flat, received, spread_z, mix_yx)


def fetch_and_mix(moving, owners, block_ids, counts, mix_yx, mix_z):
    rows_gy = lax.axis_size("gy")
    groups = rows_gy * lax.axis_size("gx")
    holders = groups // 2
    capacity = max(2, 2 * SLOTS // groups)
    halves = [list(range(holders)), list(range(holders, groups))]
    half = (lax.axis_index("gy") >= rows_gy // 2).astype(jnp.int32).reshape(1)
    near, request, flat = prepare(half, moving, owners.reshape(1, SLOTS), block_ids.reshape(1, SLOTS), groups, capacity)
    far = lax.ppermute(near, "gy", [(i, (i + rows_gy // 2) % rows_gy) for i in range(rows_gy)])
    request = lax.all_to_all(request, BRICKS, split_axis=0, concat_axis=0, tiled=True, axis_index_groups=halves)
    picked = pick(request.reshape(-1), near, far, capacity).reshape(holders, 2 * capacity, VZ, BV)
    received = lax.all_to_all(picked, BRICKS, split_axis=0, concat_axis=0, tiled=True, axis_index_groups=halves)
    slot_pos = jnp.arange(SLOTS, dtype=jnp.int32)
    keep = slot_pos % SOURCES < jnp.repeat(counts.reshape(-1), SOURCES)
    weights_z = jnp.where(keep[:, None, None], mix_z.reshape(SLOTS, VZ, VZ), 0.0).reshape(SLOTS * VZ, VZ)
    warped = mix(
        flat.reshape(-1),
        received.reshape(groups * capacity, VZ, BV),
        spread(weights_z),
        mix_yx.reshape(SLOTS, BV, BV),
    )
    return warped.reshape(NZ, NY, NX)


def padded_2(block, sides, width):
    for axis, dim in sides:
        count = lax.axis_size(axis)
        forward = [(i, i + 1) for i in range(count - 1)]
        backward = [(target, source) for source, target in forward]
        low = lax.ppermute(
            lax.slice_in_dim(block, block.shape[dim] - width, None, axis=dim), axis, forward
        )
        high = lax.ppermute(lax.slice_in_dim(block, 0, width, axis=dim), axis, backward)
        block = jnp.concatenate([low, block, high], axis=dim)
    return block


def box_along(padded, axis):
    length = padded.shape[axis] - 2 * RAD
    total = lax.slice_in_dim(padded, 0, length, axis=axis)
    for shift in range(1, 2 * RAD + 1):
        total = total + lax.slice_in_dim(padded, shift, shift + length, axis=axis)
    return total


def per_device(fixed, moving, owners, block_ids, counts, mix_yx, mix_z):
    warped = fetch_and_mix(moving, owners, block_ids, counts, mix_yx, mix_z)
    image = fixed.astype(jnp.float32)
    fields = jnp.stack([image, warped, image * image, warped * warped, image * warped])
    padded = padded_2(fields, (("gz", 1),), RAD)
    sums = box_along(padded, 1)
    padded = padded_2(sums, (("gy", 2),), RAD)
    sums = box_along(padded, 2)
    padded = padded_2(sums, (("gx", 3),), RAD)
    sums = box_along(padded, 3)
    wpad = padded_2(warped, (("gz", 0), ("gy", 1), ("gx", 2)), 1)
    count = float((2 * RAD + 1) ** 3)
    mean_f = sums[0] / count
    mean_w = sums[1] / count
    cov = sums[4] / count - mean_f * mean_w
    var_f = sums[2] / count - mean_f * mean_f
    var_w = sums[3] / count - mean_w * mean_w
    deriv = (
        2.0
        * cov
        / ((var_f + 1e-05) * (var_w + 1e-05))
        * (image - mean_f - cov / (var_w + 1e-05) * (warped - mean_w))
    )
    slope_z = (wpad[2:, 1:-1, 1:-1] - wpad[:-2, 1:-1, 1:-1]) * 0.5
    slope_y = (wpad[1:-1, 2:, 1:-1] - wpad[1:-1, :-2, 1:-1]) * 0.5
    slope_x = (wpad[1:-1, 1:-1, 2:] - wpad[1:-1, 1:-1, :-2]) * 0.5
    force = jnp.stack([deriv * slope_z, deriv * slope_y, deriv * slope_x])
    return (warped, force)


def solution(mesh):
    return jax.shard_map(
        per_device,
        mesh=mesh,
        in_specs=(
            P("gz", "gy", "gx"),
            P("gz", "gy", "gx"),
            P("gz", "gy", "gx", None, None),
            P("gz", "gy", "gx", None),
            P("gz", "gy", "gx", None),
            P("gz", "gy", "gx", None, None, None),
            P("gz", "gy", "gx", None, None, None),
        ),
        out_specs=(P("gz", "gy", "gx"), P(None, "gz", "gy", "gx")),
        check_vma=False,
    )
```

```python
import jax
import jax.numpy as jnp
from jax import lax
from jax.experimental import pallas as pl
from jax.experimental.pallas import tpu as pltpu
from jax.sharding import PartitionSpec as P

VZ = 8
VY = 8
VX = 16
NBZ = 2
NBY = 8
NBX = 8
SOURCES = 2
RAD = 4
BV = VY * VX
BLOCKS = NBZ * NBY * NBX
SLOTS = BLOCKS * SOURCES
NZ = NBZ * VZ
NY = NBY * VY
NX = NBX * VX
GROUPS = NBZ * NBY
PER = NBX * SOURCES
ROWS = PER * VZ
BRICKS = ("gy", "gx")
F32 = jnp.float32
BF16 = jnp.bfloat16

VMEM = pl.BlockSpec(memory_space=pltpu.VMEM)
SMEM = pl.BlockSpec(memory_space=pltpu.SMEM)


def iota(shape, dim):
    return lax.broadcasted_iota(jnp.int32, shape, dim)


def pieces(value, count):
    parts = []
    for _ in range(count - 1):
        part = value.astype(BF16)
        parts.append(part)
        value = value - part.astype(F32)
    parts.append(value.astype(BF16))
    return parts


def swap_chunks(rows):
    chunk = iota((VZ, BV), 1) // VX
    for k in (1, 2, 4):
        low = (chunk & k) == 0
        out = list(rows)
        for b in range(8):
            if b & k == 0:
                first, second = rows[b], rows[b + k]
                out[b] = jnp.where(low, first, pltpu.roll(second, k * VX, 1))
                out[b + k] = jnp.where(low, pltpu.roll(first, BV - k * VX, 1), second)
        rows = out
    return rows


def prepare_kernel(half_ref, moving_ref, owner_ref, ident_ref, blocks_ref, request_ref, flat_ref, wide):
    holders, _, width = request_ref.shape
    capacity = width // 2
    half = half_ref[0]
    owner = owner_ref[...]
    ident = ident_ref[...].astype(F32)
    groups = 2 * holders
    named = jnp.where(owner == iota((groups, SLOTS), 0), 1.0, 0.0)
    earlier = jnp.where(iota((SLOTS, SLOTS), 0) < iota((SLOTS, SLOTS), 1), 1.0, 0.0).astype(BF16)
    before = jnp.dot(named.astype(BF16), earlier, preferred_element_type=F32)
    rank = jnp.sum(named * before, axis=0, keepdims=True).astype(jnp.int32)
    upper = jnp.where(owner >= holders, 1, 0)
    holder = owner - upper * holders
    place = jnp.where(upper == half, 0, capacity) + rank
    flat_ref[...] = holder * width + place
    wanted = jnp.where(holder == iota((holders, SLOTS), 0), ident, 0.0).astype(BF16)
    at = jnp.where(place == iota((width, SLOTS), 0), 1.0, 0.0).astype(BF16)
    request = lax.dot_general(wanted, at, (((1,), (1,)), ((), ())), preferred_element_type=F32).astype(jnp.int32)
    for h in range(holders):
        request_ref[h] = request[h : h + 1, :]
    for z in range(NZ):
        wide[z * NY : (z + 1) * NY, :] = moving_ref[z].astype(F32)

    def group(g, _):
        start = (g // NBY) * (VZ * NY) + (g % NBY) * VY
        rows = [wide[pl.ds(start + y, VZ, stride=NY), :] for y in range(VY)]
        for x, block in enumerate(swap_chunks(rows)):
            blocks_ref[g * NBX + x] = block.astype(BF16)
        return 0

    lax.fori_loop(0, GROUPS, group, 0)


def prepare(half, moving, owner, ident, groups, capacity):
    holders = groups // 2
    return pl.pallas_call(
        prepare_kernel,
        out_shape=(
            jax.ShapeDtypeStruct((BLOCKS, VZ, BV), BF16),
            jax.ShapeDtypeStruct((holders, 1, 2 * capacity), jnp.int32),
            jax.ShapeDtypeStruct((1, SLOTS), jnp.int32),
        ),
        in_specs=[SMEM, VMEM, VMEM, VMEM],
        out_specs=(VMEM, VMEM, VMEM),
        scratch_shapes=[pltpu.VMEM((NZ * NY, NX), F32)],
        name="prepare",
    )(half, moving, owner, ident)


def pick_kernel(capacity, request_ref, near_ref, far_ref, out_ref):
    width = 2 * capacity

    def holder(h, _):
        for k in range(width):
            source = near_ref if k < capacity else far_ref
            out_ref[h * width + k] = source[request_ref[h * width + k]]
        return 0

    lax.fori_loop(0, out_ref.shape[0] // width, holder, 0)


def pick(request, near, far, capacity):
    return pl.pallas_call(
        lambda *refs: pick_kernel(capacity, *refs),
        out_shape=jax.ShapeDtypeStruct((request.shape[0], VZ, BV), BF16),
        in_specs=[SMEM, VMEM, VMEM],
        out_specs=VMEM,
        name="pick",
    )(request, near, far)


def spread_kernel(mix_ref, out_ref):
    pick_lane = jnp.where(iota((VZ, ROWS), 1) % VZ == iota((VZ, ROWS), 0), 1.0, 0.0).astype(BF16)
    same = iota((ROWS, ROWS), 0) // VZ == iota((ROWS, ROWS), 1) // VZ

    def group(g, _):
        weights = mix_ref[pl.ds(pl.multiple_of(g * ROWS, ROWS), ROWS), :]
        for k, part in enumerate(pieces(weights, 3)):
            tiled = jnp.dot(part, pick_lane, preferred_element_type=F32)
            out_ref[g, k * ROWS : (k + 1) * ROWS, :] = jnp.where(same, tiled, 0.0).astype(BF16)
        return 0

    lax.fori_loop(0, GROUPS, group, 0)


def spread(mix_z):
    return pl.pallas_call(
        spread_kernel,
        out_shape=jax.ShapeDtypeStruct((GROUPS, 3 * ROWS, ROWS), BF16),
        in_specs=[VMEM],
        out_specs=VMEM,
        name="spread",
    )(mix_z)


STEP = 2


def mix_kernel(flat_ref, place_ref, received_ref, spread_ref, mix_ref, warped_ref, side_ref, source):
    step = pl.program_id(0)
    for q in range(STEP):
        g = step * STEP + q
        for i in range(PER):
            source[i * VZ : (i + 1) * VZ, :] = received_ref[flat_ref[g * PER + i]].astype(F32)
        parts = jnp.dot(spread_ref[q], source[...].astype(BF16), preferred_element_type=F32)
        mixed = parts[:ROWS] + parts[ROWS : 2 * ROWS] + parts[2 * ROWS :]
        high = mixed.astype(BF16).astype(F32)
        low = mixed - high
        rows = []
        for j in range(NBX):
            a = slice(2 * j * VZ, (2 * j + 1) * VZ)
            b = slice((2 * j + 1) * VZ, (2 * j + 2) * VZ)
            left = jnp.concatenate(
                [jnp.concatenate([high[a], high[b]], 1), jnp.concatenate([low[a], low[b]], 1)], 0
            ).astype(BF16)
            right = mix_ref[q * PER + 2 * j : q * PER + 2 * j + 2].reshape(2 * BV, BV)
            both = jnp.dot(left, right, preferred_element_type=F32)
            rows.append(both[:VZ] + both[VZ:])
        start = (g // NBY) * (VZ * NY) + (g % NBY) * VY
        for y, row in enumerate(swap_chunks(rows)):
            warped_ref[pl.ds(start + y, VZ, stride=NY), :] = row

    @pl.when(step == pl.num_programs(0) - 1)
    def _():
        first = jnp.where(place_ref[0] == 0, (NZ - RAD) * NY, 0)
        side_ref[...] = warped_ref[pl.ds(pl.multiple_of(first, NY), RAD * NY), :]


def mix(flat, place, received, spread_z, mix_yx):
    return pl.pallas_call(
        mix_kernel,
        grid_spec=pltpu.PrefetchScalarGridSpec(
            num_scalar_prefetch=2,
            grid=(GROUPS // STEP,),
            in_specs=[
                pl.BlockSpec(received.shape, lambda i, f, p: (0, 0, 0)),
                pl.BlockSpec((STEP, 3 * ROWS, ROWS), lambda i, f, p: (i, 0, 0)),
                pl.BlockSpec((STEP * PER, BV, BV), lambda i, f, p: (i, 0, 0)),
            ],
            out_specs=(
                pl.BlockSpec((NZ * NY, NX), lambda i, f, p: (0, 0)),
                pl.BlockSpec((RAD * NY, NX), lambda i, f, p: (0, 0)),
            ),
            scratch_shapes=[pltpu.VMEM((ROWS, BV), F32)],
        ),
        out_shape=(
            jax.ShapeDtypeStruct((NZ * NY, NX), F32),
            jax.ShapeDtypeStruct((RAD * NY, NX), F32),
        ),
        name="mix",
    )(flat, place, received, spread_z, mix_yx)


def fetch_and_mix(place, moving, owners, block_ids, counts, mix_yx, mix_z):
    rows_gy = lax.axis_size("gy")
    groups = rows_gy * lax.axis_size("gx")
    holders = groups // 2
    capacity = max(2, 2 * SLOTS // groups)
    halves = [list(range(holders)), list(range(holders, groups))]
    half = (lax.axis_index("gy") >= rows_gy // 2).astype(jnp.int32).reshape(1)
    near, request, flat = prepare(half, moving, owners.reshape(1, SLOTS), block_ids.reshape(1, SLOTS), groups, capacity)
    far = lax.ppermute(near, "gy", [(i, (i + rows_gy // 2) % rows_gy) for i in range(rows_gy)])
    request = lax.all_to_all(request, BRICKS, split_axis=0, concat_axis=0, tiled=True, axis_index_groups=halves)
    picked = pick(request.reshape(-1), near, far, capacity).reshape(holders, 2 * capacity, VZ, BV)
    received = lax.all_to_all(picked, BRICKS, split_axis=0, concat_axis=0, tiled=True, axis_index_groups=halves)
    slot_pos = jnp.arange(SLOTS, dtype=jnp.int32)
    keep = slot_pos % SOURCES < jnp.repeat(counts.reshape(-1), SOURCES)
    weights_z = jnp.where(keep[:, None, None], mix_z.reshape(SLOTS, VZ, VZ), 0.0).reshape(SLOTS * VZ, VZ)
    return mix(
        flat.reshape(-1),
        place,
        received.reshape(groups * capacity, VZ, BV),
        spread(weights_z),
        mix_yx.reshape(SLOTS, BV, BV),
    )


REACH = 2 * RAD
EZ = NZ + REACH
EY = NY + REACH
COUNT = float((REACH + 1) ** 3)


def ysend_kernel(has_odd, place_ref, own_ref, side_ref, *outs):
    even = place_ref[1] == 0
    for p in range(NZ + RAD):
        source, start = (own_ref, p * NY) if p < NZ else (side_ref, (p - NZ) * NY)
        first = source[start : start + VY, :][:RAD]
        last = source[start + NY - VY : start + NY, :][VY - RAD :]
        outs[0][p] = jnp.where(even, last, first)
        if has_odd:
            outs[1][p] = jnp.where(even, first, last)


def ysend(place, own, side, has_odd):
    shape = jax.ShapeDtypeStruct((NZ + RAD, RAD, NX), F32)
    count = 2 if has_odd else 1
    return pl.pallas_call(
        lambda *refs: ysend_kernel(has_odd, *refs),
        out_shape=(shape,) * count,
        in_specs=[SMEM, VMEM, VMEM],
        out_specs=(VMEM,) * count,
        name="ysend",
    )(place, own, side)


def extend_kernel(y_count, x_count, place_ref, own_ref, side_ref, *refs):
    y_refs, ext_ref, x_refs = refs[:y_count], refs[y_count], refs[y_count + 1 :]
    low_z = place_ref[0] == 0
    even_y = place_ref[1] == 0
    even_x = place_ref[2] == 0
    nothing = jnp.zeros((EY, NX), F32)
    side_at = jnp.where(low_z, RAD + NZ, 0)
    none_at = jnp.where(low_z, 0, RAD + NZ)
    for p in range(NZ + RAD):
        if p < NZ:
            at, rows = RAD + p, own_ref[p * NY : (p + 1) * NY, :]
        else:
            at, rows = side_at + (p - NZ), side_ref[(p - NZ) * NY : (p - NZ + 1) * NY, :]
            ext_ref[none_at + (p - NZ)] = nothing
        first = y_refs[0][p]
        second = y_refs[1][p] if y_count == 2 else jnp.zeros_like(first)
        below = jnp.where(even_y, second, first)
        above = jnp.where(even_y, first, second)
        ext_ref[at] = jnp.concatenate([below, rows, above], 0)
    slot = iota((VY, NX), 1) // RAD
    for k in range(x_count):
        lift = jnp.where(even_x, RAD, 0) if k == 0 else jnp.where(even_x, 0, RAD)
        for q in range(EY // VY):
            packed = jnp.zeros((VY, NX), F32)
            for p in range(EZ):
                rows = pltpu.roll(ext_ref[p, q * VY : (q + 1) * VY, :], lift + p * RAD, 1)
                packed = jnp.where(slot == p, rows, packed)
            x_refs[k][q * VY : (q + 1) * VY, :] = packed


def extend(place, own, side, y_halos, x_count):
    packed = jax.ShapeDtypeStruct((EY, NX), F32)
    return pl.pallas_call(
        lambda *refs: extend_kernel(len(y_halos), x_count, *refs),
        out_shape=(jax.ShapeDtypeStruct((EZ, EY, NX), F32),) + (packed,) * x_count,
        in_specs=[SMEM] + [VMEM] * (2 + len(y_halos)),
        out_specs=(VMEM,) * (1 + x_count),
        name="extend",
    )(place, own, side, *y_halos)


def window(parts, length):
    two = [parts[i] + parts[i + 1] for i in range(len(parts) - 1)]
    four = [two[i] + two[i + 2] for i in range(len(two) - 2)]
    eight = [four[i] + four[i + 4] for i in range(len(four) - 4)]
    return [eight[i] + parts[i + 8] for i in range(length)]


def window_rows(value):
    two = value + pltpu.roll(value, EY - 1, 0)
    four = two + pltpu.roll(two, EY - 2, 0)
    eight = four + pltpu.roll(four, EY - 4, 0)
    return (eight + pltpu.roll(value, EY - 8, 0))[:NY]


def split_dot(value, table):
    total = None
    for part in pieces(value, 3):
        term = jnp.dot(part, table, preferred_element_type=F32)
        total = term if total is None else total + term
    return total


def brick_sums(kinds, fields, planes, out_ref):
    for q in range(EY // VY):
        for f, parts in enumerate(fields(q)):
            for z, total in enumerate(window(parts, NZ)):
                planes[f * NZ + z, q * VY : (q + 1) * VY, :] = total
    near = jnp.where(jnp.abs(iota((NX, NX), 0) - iota((NX, NX), 1)) <= RAD, 1.0, 0.0).astype(BF16)

    def one(i, _):
        out_ref[i] = split_dot(window_rows(planes[i]), near)
        return 0

    lax.fori_loop(0, kinds * NZ, one, 0, unroll=2)


def load_planes(ref, q):
    return [ref[p, q * VY : (q + 1) * VY, :] for p in range(EZ)]


def edge_table(right):
    row, col = iota((NX, NX), 0), iota((NX, NX), 1)
    plane, i = row // RAD, row % RAD
    z, j = col // RAD, col % RAD
    reach = jnp.where(right, j - i, i - j)
    inside = (plane >= z) & (plane <= z + REACH) & (z < NZ) & (plane < EZ) & (reach >= 0)
    return jnp.where(inside, 1.0, 0.0).astype(BF16)


def edge_sums(fields, table):
    return [split_dot(window_rows(field), table) for field in fields]


def at_edge(right):
    return iota((NY, NX), 1) // RAD == jnp.where(right, NX // RAD - 1, 0)


def edge_part(sums, z, right, mask):
    base = jnp.where(right, NX - RAD, 0)
    return jnp.where(mask, pltpu.roll(sums, lax.rem(base + NX - RAD * z, NX), 1), 0.0)


def side_is_right(place_ref, k):
    even = place_ref[2] == 0
    return even if k == 0 else jnp.logical_not(even)


def fixed_sums_kernel(x_count, place_ref, ext_ref, *refs):
    x_refs, out_ref, planes = refs[:x_count], refs[x_count], refs[x_count + 1]

    def fields(q):
        values = load_planes(ext_ref, q)
        return [values, [v * v for v in values]]

    brick_sums(2, fields, planes, out_ref)
    for k in range(x_count):
        right = side_is_right(place_ref, k)
        halo = x_refs[k][...]
        mask = at_edge(right)
        for f, sums in enumerate(edge_sums([halo, halo * halo], edge_table(right))):
            for z in range(NZ):
                out_ref[f * NZ + z] += edge_part(sums, z, right, mask)


def fixed_sums(place, ext, x_halos):
    return pl.pallas_call(
        lambda *refs: fixed_sums_kernel(len(x_halos), *refs),
        out_shape=jax.ShapeDtypeStruct((2 * NZ, NY, NX), F32),
        in_specs=[SMEM] + [VMEM] * (1 + len(x_halos)),
        out_specs=VMEM,
        scratch_shapes=[pltpu.VMEM((2 * NZ, EY, NX), F32)],
        name="fixed_sums",
    )(place, ext, *x_halos)


def warped_sums_kernel(warped_ref, fixed_ref, out_ref, planes):
    def fields(q):
        w, f = load_planes(warped_ref, q), load_planes(fixed_ref, q)
        return [w, [v * v for v in w], [u * v for u, v in zip(f, w)]]

    brick_sums(3, fields, planes, out_ref)


def warped_sums(warped_ext, fixed_ext):
    return pl.pallas_call(
        warped_sums_kernel,
        out_shape=jax.ShapeDtypeStruct((3 * NZ, NY, NX), F32),
        in_specs=[VMEM, VMEM],
        out_specs=VMEM,
        scratch_shapes=[pltpu.VMEM((3 * NZ, EY, NX), F32)],
        name="warped_sums",
    )(warped_ext, fixed_ext)


def force_kernel(x_count, place_ref, sums_ref, fixed_sums_ref, fixed_ref, ext_ref, *refs):
    warped_halos, fixed_halos = refs[:x_count], refs[x_count : 2 * x_count]
    force_ref, edges = refs[2 * x_count], refs[2 * x_count + 1]
    for k in range(x_count):
        right = side_is_right(place_ref, k)
        w, f = warped_halos[k][...], fixed_halos[k][...]
        for i, sums in enumerate(edge_sums([w, w * w, f * w], edge_table(right))):
            edges[4 * k + i] = sums
        edges[4 * k + 3] = w[RAD : RAD + NY]
    scale = 1.0 / COUNT
    lane = iota((NY, NX), 1)

    def plane(z, _):
        sums = [sums_ref[f * NZ + z] for f in range(3)]
        own = ext_ref[z + RAD, RAD : RAD + NY, :]
        after = jnp.where(lane == NX - 1, 0.0, pltpu.roll(own, NX - 1, 1))
        before = jnp.where(lane == 0, 0.0, pltpu.roll(own, 1, 1))
        for k in range(x_count):
            right = side_is_right(place_ref, k)
            mask = at_edge(right)
            sums = [total + edge_part(edges[4 * k + i], z, right, mask) for i, total in enumerate(sums)]
            turn = jnp.where(right, NX - 1, NX + 1 - RAD) + NX - RAD * (z + RAD)
            halo = pltpu.roll(edges[4 * k + 3], lax.rem(turn, NX), 1)
            after = jnp.where(lane == jnp.where(right, NX - 1, -1), halo, after)
            before = jnp.where(lane == jnp.where(right, -1, 0), halo, before)
        mean_w = sums[0] * scale
        mean_f = fixed_sums_ref[z] * scale
        cov = sums[2] * scale - mean_f * mean_w
        var_f = fixed_sums_ref[NZ + z] * scale - mean_f * mean_f + 1e-5
        var_w = sums[1] * scale - mean_w * mean_w + 1e-5
        image = fixed_ref[z].astype(F32)
        deriv = 2.0 * cov / (var_f * var_w) * ((image - mean_f) - cov / var_w * (own - mean_w))
        half = 0.5 * deriv
        above, below = ext_ref[z + RAD + 1, RAD : RAD + NY, :], ext_ref[z + RAD - 1, RAD : RAD + NY, :]
        force_ref[0, z] = half * (above - below)
        force_ref[1, z] = half * (ext_ref[z + RAD, RAD + 1 : RAD + 1 + NY, :] - ext_ref[z + RAD, RAD - 1 : RAD - 1 + NY, :])
        force_ref[2, z] = half * (after - before)
        return 0

    lax.fori_loop(0, NZ, plane, 0)


def force_of(place, sums, sums_f, fixed, ext, warped_halos, fixed_halos):
    count = len(warped_halos)
    return pl.pallas_call(
        lambda *refs: force_kernel(count, *refs),
        out_shape=jax.ShapeDtypeStruct((3, NZ, NY, NX), F32),
        in_specs=[SMEM] + [VMEM] * (4 + 2 * count),
        out_specs=VMEM,
        scratch_shapes=[pltpu.VMEM((4 * count, NY, NX), F32)],
        name="force",
    )(place, sums, sums_f, fixed, ext, *warped_halos, *fixed_halos)


def pairings(size):
    even = [(i, i ^ 1) for i in range(size) if (i ^ 1) < size]
    odd = [(i, i + 1 if i % 2 else i - 1) for i in range(1, size)]
    odd = [(i, j) for i, j in odd if j < size]
    return [pairs for pairs in (even, odd) if pairs]


def halos(place, own, side):
    side = lax.ppermute(side, "gz", pairings(lax.axis_size("gz"))[0])
    along_y = pairings(lax.axis_size("gy"))
    sent = ysend(place, own, side, len(along_y) == 2)
    received = [lax.ppermute(s, "gy", pairs) for s, pairs in reversed(list(zip(sent, along_y)))][::-1]
    along_x = pairings(lax.axis_size("gx"))
    ext, *columns = extend(place, own, side, received, len(along_x))
    return ext, [lax.ppermute(c, "gx", pairs) for c, pairs in zip(columns, along_x)]


def per_device(fixed, moving, owners, block_ids, counts, mix_yx, mix_z):
    place = jnp.stack([lax.axis_index("gz"), lax.axis_index("gy") % 2, lax.axis_index("gx") % 2]).astype(jnp.int32)
    warped, side = fetch_and_mix(place, moving, owners, block_ids, counts, mix_yx, mix_z)
    image = fixed.astype(F32).reshape(NZ * NY, NX)
    start = jnp.where(place[0] == 0, (NZ - RAD) * NY, 0)
    fixed_ext, fixed_columns = halos(place, image, lax.dynamic_slice_in_dim(image, start, RAD * NY, 0))
    sums_f = fixed_sums(place, fixed_ext, fixed_columns)
    ext, columns = halos(place, warped, side)
    sums = warped_sums(ext, fixed_ext)
    force = force_of(place, sums, sums_f, fixed, ext, columns, fixed_columns)
    return warped.reshape(NZ, NY, NX), force


def solution(mesh):
    return jax.shard_map(
        per_device,
        mesh=mesh,
        in_specs=(
            P("gz", "gy", "gx"),
            P("gz", "gy", "gx"),
            P("gz", "gy", "gx", None, None),
            P("gz", "gy", "gx", None),
            P("gz", "gy", "gx", None),
            P("gz", "gy", "gx", None, None, None),
            P("gz", "gy", "gx", None, None, None),
        ),
        out_specs=(P("gz", "gy", "gx"), P(None, "gz", "gy", "gx")),
        check_vma=False,
    )
```

```python
import jax
import jax.numpy as jnp
from jax import lax
from jax.experimental import pallas as pl
from jax.experimental.pallas import tpu as pltpu
from jax.sharding import PartitionSpec as P

VZ = 8
VY = 8
VX = 16
NBZ = 2
NBY = 8
NBX = 8
SOURCES = 2
RAD = 4
BV = VY * VX
BLOCKS = NBZ * NBY * NBX
SLOTS = BLOCKS * SOURCES
NZ = NBZ * VZ
NY = NBY * VY
NX = NBX * VX
GROUPS = NBZ * NBY
PER = NBX * SOURCES
ROWS = PER * VZ
BRICKS = ("gy", "gx")
F32 = jnp.float32
LIMIT = 12 * 2**20
BF16 = jnp.bfloat16

VMEM = pl.BlockSpec(memory_space=pltpu.VMEM)
SMEM = pl.BlockSpec(memory_space=pltpu.SMEM)


def iota(shape, dim):
    return lax.broadcasted_iota(jnp.int32, shape, dim)


def pieces(value, count):
    parts = []
    for _ in range(count - 1):
        part = value.astype(BF16)
        parts.append(part)
        value = value - part.astype(F32)
    parts.append(value.astype(BF16))
    return parts


def swap_chunks(rows):
    chunk = iota((VZ, BV), 1) // VX
    for k in (1, 2, 4):
        low = (chunk & k) == 0
        out = list(rows)
        for b in range(8):
            if b & k == 0:
                first, second = rows[b], rows[b + k]
                out[b] = jnp.where(low, first, pltpu.roll(second, k * VX, 1))
                out[b + k] = jnp.where(low, pltpu.roll(first, BV - k * VX, 1), second)
        rows = out
    return rows


def prepare_kernel(half_ref, moving_ref, owner_ref, ident_ref, blocks_ref, request_ref, flat_ref, wide):
    holders, _, width = request_ref.shape
    capacity = width // 2
    half = half_ref[0]
    owner = owner_ref[...]
    ident = ident_ref[...].astype(F32)
    groups = 2 * holders
    named = jnp.where(owner == iota((groups, SLOTS), 0), 1.0, 0.0)
    earlier = jnp.where(iota((SLOTS, SLOTS), 0) < iota((SLOTS, SLOTS), 1), 1.0, 0.0).astype(BF16)
    before = jnp.dot(named.astype(BF16), earlier, preferred_element_type=F32)
    rank = jnp.sum(named * before, axis=0, keepdims=True).astype(jnp.int32)
    upper = jnp.where(owner >= holders, 1, 0)
    holder = owner - upper * holders
    place = jnp.where(upper == half, 0, capacity) + rank
    flat_ref[...] = holder * width + place
    wanted = jnp.where(holder == iota((holders, SLOTS), 0), ident, 0.0).astype(BF16)
    at = jnp.where(place == iota((width, SLOTS), 0), 1.0, 0.0).astype(BF16)
    request = lax.dot_general(wanted, at, (((1,), (1,)), ((), ())), preferred_element_type=F32).astype(jnp.int32)
    for h in range(holders):
        request_ref[h] = request[h : h + 1, :]
    for z in range(NZ):
        wide[z * NY : (z + 1) * NY, :] = moving_ref[z].astype(F32)

    def group(g, _):
        start = (g // NBY) * (VZ * NY) + (g % NBY) * VY
        rows = [wide[pl.ds(start + y, VZ, stride=NY), :] for y in range(VY)]
        for x, block in enumerate(swap_chunks(rows)):
            blocks_ref[g * NBX + x] = block.astype(BF16)
        return 0

    lax.fori_loop(0, GROUPS, group, 0, unroll=4)


def prepare(half, moving, owner, ident, groups, capacity):
    holders = groups // 2
    return pl.pallas_call(
        prepare_kernel,
        out_shape=(
            jax.ShapeDtypeStruct((BLOCKS, VZ, BV), BF16),
            jax.ShapeDtypeStruct((holders, 1, 2 * capacity), jnp.int32),
            jax.ShapeDtypeStruct((1, SLOTS), jnp.int32),
        ),
        in_specs=[SMEM, VMEM, VMEM, VMEM],
        out_specs=(VMEM, VMEM, VMEM),
        scratch_shapes=[pltpu.VMEM((NZ * NY, NX), F32)],
        compiler_params=pltpu.CompilerParams(vmem_limit_bytes=LIMIT),
        name="prepare",
    )(half, moving, owner, ident)


def pick_kernel(capacity, request_ref, near_ref, far_ref, out_ref):
    width = 2 * capacity

    def holder(h, _):
        for k in range(width):
            source = near_ref if k < capacity else far_ref
            out_ref[h * width + k] = source[request_ref[h, 0, k]]
        return 0

    lax.fori_loop(0, out_ref.shape[0] // width, holder, 0)


def pick(request, near, far, capacity):
    return pl.pallas_call(
        lambda *refs: pick_kernel(capacity, *refs),
        out_shape=jax.ShapeDtypeStruct((request.size, VZ, BV), BF16),
        in_specs=[SMEM, VMEM, VMEM],
        out_specs=VMEM,
        compiler_params=pltpu.CompilerParams(vmem_limit_bytes=LIMIT),
        name="pick",
    )(request, near, far)


def spread_kernel(mix_ref, out_ref):
    pick_lane = jnp.where(iota((VZ, ROWS), 1) % VZ == iota((VZ, ROWS), 0), 1.0, 0.0).astype(BF16)
    same = iota((ROWS, ROWS), 0) // VZ == iota((ROWS, ROWS), 1) // VZ

    def group(g, _):
        weights = mix_ref[pl.ds(pl.multiple_of(g * ROWS, ROWS), ROWS), :]
        for k, part in enumerate(pieces(weights, 3)):
            tiled = jnp.dot(part, pick_lane, preferred_element_type=F32)
            out_ref[g, k * ROWS : (k + 1) * ROWS, :] = jnp.where(same, tiled, 0.0).astype(BF16)
        return 0

    lax.fori_loop(0, GROUPS, group, 0, unroll=4)


def spread(mix_z):
    return pl.pallas_call(
        spread_kernel,
        out_shape=jax.ShapeDtypeStruct((GROUPS, 3 * ROWS, ROWS), BF16),
        in_specs=[VMEM],
        out_specs=VMEM,
        compiler_params=pltpu.CompilerParams(vmem_limit_bytes=LIMIT),
        name="spread",
    )(mix_z)


STEP = 4


def mix_kernel(flat_ref, place_ref, received_ref, spread_ref, mix_ref, warped_ref, side_ref, face_ref):
    step = pl.program_id(0)
    for q in range(STEP):
        g = step * STEP + q
        source = jnp.concatenate([received_ref[flat_ref[g * PER + i]].astype(F32) for i in range(PER)], 0)
        parts = jnp.dot(spread_ref[q], source.astype(BF16), preferred_element_type=F32)
        mixed = parts[:ROWS] + parts[ROWS : 2 * ROWS] + parts[2 * ROWS :]
        high = mixed.astype(BF16).astype(F32)
        low = mixed - high
        rows = []
        for j in range(NBX):
            a = slice(2 * j * VZ, (2 * j + 1) * VZ)
            b = slice((2 * j + 1) * VZ, (2 * j + 2) * VZ)
            left = jnp.concatenate(
                [jnp.concatenate([high[a], high[b]], 1), jnp.concatenate([low[a], low[b]], 1)], 0
            ).astype(BF16)
            right = mix_ref[q * PER + 2 * j : q * PER + 2 * j + 2].reshape(2 * BV, BV)
            both = jnp.dot(left, right, preferred_element_type=F32)
            rows.append(both[:VZ] + both[VZ:])
        start = (g // NBY) * (VZ * NY) + (g % NBY) * VY
        for y, row in enumerate(swap_chunks(rows)):
            warped_ref[pl.ds(start + y, VZ, stride=NY), :] = row

    @pl.when(step == pl.num_programs(0) - 1)
    def _():
        outer(place_ref, warped_ref, side_ref, face_ref)


def outer(place_ref, own_ref, side_ref, face_ref):
    first = jnp.where(place_ref[0] == 0, (NZ - RAD) * NY, 0)
    side_ref[...] = own_ref[pl.ds(pl.multiple_of(first, NY), RAD * NY), :]
    low = iota((VY, NX), 0) < RAD
    for z in range(NZ):
        face_ref[z] = jnp.where(low, own_ref[z * NY : z * NY + VY, :], own_ref[(z + 1) * NY - VY : (z + 1) * NY, :])


OUTER = (
    jax.ShapeDtypeStruct((NZ * NY, NX), F32),
    jax.ShapeDtypeStruct((RAD * NY, NX), F32),
    jax.ShapeDtypeStruct((NZ, VY, NX), F32),
)


def mix(flat, place, received, spread_z, mix_yx):
    return pl.pallas_call(
        mix_kernel,
        grid_spec=pltpu.PrefetchScalarGridSpec(
            num_scalar_prefetch=2,
            grid=(GROUPS // STEP,),
            in_specs=[
                pl.BlockSpec(received.shape, lambda i, f, p: (0, 0, 0)),
                pl.BlockSpec((STEP, 3 * ROWS, ROWS), lambda i, f, p: (i, 0, 0)),
                pl.BlockSpec((STEP * PER, BV, BV), lambda i, f, p: (i, 0, 0)),
            ],
            out_specs=(
                pl.BlockSpec((NZ * NY, NX), lambda i, f, p: (0, 0)),
                pl.BlockSpec((RAD * NY, NX), lambda i, f, p: (0, 0)),
                pl.BlockSpec((NZ, VY, NX), lambda i, f, p: (0, 0, 0)),
            ),
        ),
        out_shape=OUTER,
        compiler_params=pltpu.CompilerParams(vmem_limit_bytes=LIMIT),
        name="mix",
    )(flat, place, received, spread_z, mix_yx)


def image_kernel(place_ref, fixed_ref, own_ref, side_ref, face_ref):
    for z in range(NZ):
        own_ref[z * NY : (z + 1) * NY, :] = fixed_ref[z].astype(F32)
    outer(place_ref, own_ref, side_ref, face_ref)


def fetch(moving, owners, block_ids):
    rows_gy = lax.axis_size("gy")
    groups = rows_gy * lax.axis_size("gx")
    holders = groups // 2
    capacity = max(2, 2 * SLOTS // groups)
    halves = [list(range(holders)), list(range(holders, groups))]
    half = (lax.axis_index("gy") >= rows_gy // 2).astype(jnp.int32).reshape(1)
    near, request, flat = prepare(half, moving, owners.reshape(1, SLOTS), block_ids.reshape(1, SLOTS), groups, capacity)
    far = lax.ppermute(near, "gy", [(i, (i + rows_gy // 2) % rows_gy) for i in range(rows_gy)])
    request = lax.all_to_all(request, BRICKS, split_axis=0, concat_axis=0, tiled=True, axis_index_groups=halves)
    picked = pick(request, near, far, capacity).reshape(holders, 2 * capacity, VZ, BV)
    received = lax.all_to_all(picked, BRICKS, split_axis=0, concat_axis=0, tiled=True, axis_index_groups=halves)
    return received.reshape(groups * capacity, VZ, BV), flat.reshape(-1)


def spread_weights(counts, mix_z):
    slot_pos = jnp.arange(SLOTS, dtype=jnp.int32)
    keep = slot_pos % SOURCES < jnp.repeat(counts.reshape(-1), SOURCES)
    return spread(jnp.where(keep[:, None, None], mix_z.reshape(SLOTS, VZ, VZ), 0.0).reshape(SLOTS * VZ, VZ))


REACH = 2 * RAD
EZ = NZ + REACH
EY = NY + REACH
COUNT = float((REACH + 1) ** 3)


def call(kernel, name, outs, *args, scratch=()):
    return pl.pallas_call(
        kernel,
        out_shape=outs,
        in_specs=[SMEM] + [VMEM] * (len(args) - 1),
        out_specs=jax.tree.map(lambda _: VMEM, outs),
        scratch_shapes=scratch,
        compiler_params=pltpu.CompilerParams(vmem_limit_bytes=LIMIT),
        name=name,
    )(*args)


def array(*shape):
    return jax.ShapeDtypeStruct(shape, F32)


def rows_kernel(place_ref, face_ref, side_ref, *outs):
    even = place_ref[1] == 0
    low = iota((VY, NX), 0) < RAD
    for p in range(NZ + RAD):
        if p < NZ:
            face = face_ref[p]
        else:
            at = (p - NZ) * NY
            face = jnp.where(low, side_ref[at : at + VY, :], side_ref[at + NY - VY : at + NY, :])
        outs[0][p] = jnp.where(even, face[RAD:], face[:RAD])
        if len(outs) == 2:
            outs[1][p] = jnp.where(even, face[:RAD], face[RAD:])


def extended_planes(place_ref, own, side):
    low = place_ref[0] == 0
    empty = jnp.zeros_like(side[0])
    before = [jnp.where(low, empty, s) for s in side]
    after = [jnp.where(low, s, empty) for s in side]
    return before + own + after


def pack(place_ref, planes, k):
    even = place_ref[2] == 0
    lift = jnp.where(even, RAD, 0) if k == 0 else jnp.where(even, 0, RAD)
    slot = iota((VY, NX), 1) // RAD
    packed = jnp.zeros((VY, NX), F32)
    for p, rows in enumerate(planes):
        packed = jnp.where(slot == p, pltpu.roll(rows, lift + p * RAD, 1), packed)
    return packed


def window(parts, length):
    two = [parts[i] + parts[i + 1] for i in range(len(parts) - 1)]
    four = [two[i] + two[i + 2] for i in range(len(two) - 2)]
    eight = [four[i] + four[i + 4] for i in range(len(four) - 4)]
    return [eight[i] + parts[i + 8] for i in range(length)]


def own_kernel(x_count, with_image, place_ref, own_ref, side_ref, *refs):
    image_ref, sums_ref, *columns = refs

    def rows_of(q, _):
        at = pl.multiple_of(q * VY, VY)
        rows = pl.ds(at, VY)
        own = [own_ref[pl.ds(pl.multiple_of(z * NY + at, VY), VY), :] for z in range(NZ)]
        side = [side_ref[pl.ds(pl.multiple_of(z * NY + at, VY), VY), :] for z in range(RAD)]
        planes = extended_planes(place_ref, own, side)
        for k in range(x_count):
            columns[k][rows, :] = pack(place_ref, planes, k)
        fields = [planes, [v * v for v in planes]]
        if with_image:
            fields.append([image_ref[p, rows, :] * v for p, v in enumerate(planes)])
        else:
            for p, v in enumerate(planes):
                image_ref[p, rows, :] = v
        for f, parts in enumerate(fields):
            for z, total in enumerate(window(parts, NZ)):
                sums_ref[f * NZ + z, rows, :] = total
        return 0

    lax.fori_loop(0, NBY, rows_of, 0)


def columns_kernel(y_count, x_count, place_ref, *refs):
    halos, packed, (rows_ref, *columns) = refs[:y_count], refs[y_count : y_count + x_count], refs[y_count + x_count :]
    even = place_ref[1] == 0
    planes = []
    for p in range(NZ + RAD):
        first = halos[0][p]
        second = halos[1][p] if y_count == 2 else jnp.zeros_like(first)
        planes.append(jnp.concatenate([jnp.where(even, first, second), jnp.where(even, second, first)], 0))
    planes = extended_planes(place_ref, planes[:NZ], planes[NZ:])
    for p, rows in enumerate(planes):
        rows_ref[p] = rows
    for k in range(x_count):
        columns[k][:NY] = packed[k][...]
        columns[k][NY:] = pack(place_ref, planes, k)


def window_rows(value):
    two = value + pltpu.roll(value, EY - 1, 0)
    four = two + pltpu.roll(two, EY - 2, 0)
    return (value + pltpu.roll(four, RAD, 0) + pltpu.roll(four, EY - 1, 0))[:NY]


def split_dot(value, table):
    total = None
    for part in pieces(value, 3):
        term = jnp.dot(part, table, preferred_element_type=F32)
        total = term if total is None else total + term
    return total


def edge_table(right):
    row, col = iota((NX, NX), 0), iota((NX, NX), 1)
    plane, i = row // RAD, row % RAD
    z, j = col // RAD, col % RAD
    reach = jnp.where(right, j - i, i - j)
    inside = (plane >= z) & (plane <= z + REACH) & (z < NZ) & (plane < EZ) & (reach >= 0)
    return jnp.where(inside, 1.0, 0.0).astype(BF16)


def at_edge(right):
    return iota((NY, NX), 1) // RAD == jnp.where(right, NX // RAD - 1, 0)


def edge_part(sums, z, right, mask):
    base = jnp.where(right, NX - RAD, 0)
    return jnp.where(mask, pltpu.roll(sums, lax.rem(base + NX - RAD * z, NX), 1), 0.0)


def side_is_right(place_ref, k):
    even = place_ref[2] == 0
    return even if k == 0 else jnp.logical_not(even)


def sums_kernel(kinds, place_ref, own_sums_ref, *refs):
    halo_refs, out_ref, outer_sums = refs[:-2], refs[-2], refs[-1]
    first = [halo_refs[0][p] for p in range(EZ)]
    fields = [first, [v * v for v in first]]
    if kinds == 3:
        fields.append([halo_refs[1][p] * v for p, v in enumerate(first)])
    for f, parts in enumerate(fields):
        for z, total in enumerate(window(parts, NZ)):
            outer_sums[f * NZ + z] = total
    near = jnp.where(jnp.abs(iota((NX, NX), 0) - iota((NX, NX), 1)) <= RAD, 1.0, 0.0).astype(BF16)

    def one(i, _):
        out_ref[i] = split_dot(window_rows(jnp.concatenate([own_sums_ref[i], outer_sums[i]], 0)), near)
        return 0

    lax.fori_loop(0, kinds * NZ, one, 0, unroll=4)


def sums(kinds, place, own_sums, *halo_rows):
    return call(
        lambda *refs: sums_kernel(kinds, *refs),
        "sums",
        array(kinds * NZ, NY, NX),
        place,
        own_sums,
        *halo_rows,
        scratch=(pltpu.VMEM((kinds * NZ, VY, NX), F32),),
    )


def force_kernel(x_count, place_ref, sums_ref, fixed_sums_ref, fixed_ref, own_ref, side_ref, rows_ref, *refs):
    warped_halos, fixed_halos = refs[:x_count], refs[x_count : 2 * x_count]
    force_ref, edges = refs[2 * x_count], refs[2 * x_count + 1]
    for k in range(x_count):
        table = edge_table(side_is_right(place_ref, k))
        w, f = warped_halos[k][...], fixed_halos[k][...]
        for i, field in enumerate([w, w * w, f * w, f, f * f]):
            edges[6 * k + i] = split_dot(window_rows(field), table)
        edges[6 * k + 5] = w[:NY]
    scale = 1.0 / COUNT
    lane = iota((NY, NX), 1)
    low = place_ref[0] == 0

    def plane(z, _):
        at = pl.multiple_of(z * NY, NY)
        box = [sums_ref[f * NZ + z] for f in range(3)] + [fixed_sums_ref[f * NZ + z] for f in range(2)]
        own = own_ref[pl.ds(at, NY), :]
        after = jnp.where(lane == NX - 1, 0.0, pltpu.roll(own, NX - 1, 1))
        before = jnp.where(lane == 0, 0.0, pltpu.roll(own, 1, 1))
        for k in range(x_count):
            right = side_is_right(place_ref, k)
            mask = at_edge(right)
            box = [total + edge_part(edges[6 * k + i], z, right, mask) for i, total in enumerate(box)]
            turn = jnp.where(right, NX - 1, NX + 1 - RAD) + NX - RAD * (z + RAD)
            halo = pltpu.roll(edges[6 * k + 5], lax.rem(turn, NX), 1)
            after = jnp.where(lane == jnp.where(right, NX - 1, -1), halo, after)
            before = jnp.where(lane == jnp.where(right, -1, 0), halo, before)
        sum_w, sum_ww, sum_fw, sum_f, sum_ff = box
        mean_w = sum_w * scale
        mean_f = sum_f * scale
        cov = sum_fw * scale - mean_f * mean_w
        var_f = sum_ff * scale - mean_f * mean_f + 1e-5
        var_w = sum_ww * scale - mean_w * mean_w + 1e-5
        image = fixed_ref[z].astype(F32)
        deriv = 2.0 * cov / (var_f * var_w) * ((image - mean_f) - cov / var_w * (own - mean_w))
        half = 0.5 * deriv
        up = own_ref[pl.ds(pl.multiple_of(jnp.minimum(at + NY, (NZ - 1) * NY), NY), NY), :]
        down = own_ref[pl.ds(pl.multiple_of(jnp.maximum(at - NY, 0), NY), NY), :]
        up = jnp.where(z == NZ - 1, jnp.where(low, side_ref[:NY, :], 0.0), up)
        down = jnp.where(z == 0, jnp.where(low, 0.0, side_ref[(RAD - 1) * NY :, :]), down)
        force_ref[0, z] = half * (up - down)
        tall = jnp.concatenate([own, rows_ref[z + RAD]], 0)
        force_ref[1, z] = half * (pltpu.roll(tall, EY - 1, 0) - pltpu.roll(tall, 1, 0))[:NY]
        force_ref[2, z] = half * (after - before)
        return 0

    lax.fori_loop(0, NZ, plane, 0, unroll=2)


def pairings(size):
    even = [(i, i ^ 1) for i in range(size) if (i ^ 1) < size]
    odd = [(i, i + 1 if i % 2 else i - 1) for i in range(1, size)]
    odd = [(i, j) for i, j in odd if j < size]
    return [pairs for pairs in (even, odd) if pairs]


def exchange_rows(place, face, side):
    side = lax.ppermute(side, "gz", pairings(lax.axis_size("gz"))[0])
    along = pairings(lax.axis_size("gy"))
    sent = call(rows_kernel, "rows", (array(NZ + RAD, RAD, NX),) * len(along), place, face, side)
    received = [lax.ppermute(s, "gy", pairs) for s, pairs in reversed(list(zip(sent, along)))][::-1]
    return side, received


def pack_columns(place, received, packed):
    count = len(packed)
    rows, *columns = call(
        lambda *refs: columns_kernel(len(received), count, *refs),
        "columns",
        (array(EZ, VY, NX),) + (array(EY, NX),) * count,
        place,
        *received,
        *packed,
    )
    return rows, columns


def per_device(fixed, moving, owners, block_ids, counts, mix_yx, mix_z):
    place = jnp.stack([lax.axis_index("gz"), lax.axis_index("gy") % 2, lax.axis_index("gx") % 2]).astype(jnp.int32)
    along = pairings(lax.axis_size("gx"))
    count = len(along)
    received, flat = fetch(moving, owners, block_ids)
    weights = spread_weights(counts, mix_z)
    image, image_side, image_face = call(image_kernel, "image", OUTER, place, fixed)
    image_side, image_halos = exchange_rows(place, image_face, image_side)
    image_sums, image_planes, *image_packed = call(
        lambda place_ref, own_ref, side_ref, sums_ref, image_ref, *columns: own_kernel(
            count, False, place_ref, own_ref, side_ref, image_ref, sums_ref, *columns
        ),
        "image_own",
        (array(2 * NZ, NY, NX), array(EZ, NY, NX)) + (array(NY, NX),) * count,
        place,
        image,
        image_side,
    )
    image_rows, image_columns = pack_columns(place, image_halos, image_packed)
    received, image_columns, weights = lax.optimization_barrier((received, image_columns, weights))
    image_columns = [lax.ppermute(c, "gx", pairs) for c, pairs in zip(image_columns, along)]
    warped, side, face = mix(flat, place, received, weights, mix_yx.reshape(SLOTS, BV, BV))
    side, row_halos = exchange_rows(place, face, side)
    own_sums, *packed = call(
        lambda *refs: own_kernel(count, True, *refs),
        "own",
        (array(3 * NZ, NY, NX),) + (array(NY, NX),) * count,
        place,
        warped,
        side,
        image_planes,
    )
    box_f = sums(2, place, image_sums, image_rows)
    rows, columns = pack_columns(place, row_halos, packed)
    columns = [lax.ppermute(c, "gx", pairs) for c, pairs in zip(columns, along)]
    box = sums(3, place, own_sums, rows, image_rows)
    force = call(
        lambda *refs: force_kernel(count, *refs),
        "force",
        array(3, NZ, NY, NX),
        place,
        box,
        box_f,
        fixed,
        warped,
        side,
        rows,
        *columns,
        *image_columns,
        scratch=(pltpu.VMEM((6 * count, NY, NX), F32),),
    )
    return warped.reshape(NZ, NY, NX), force


def solution(mesh):
    return jax.shard_map(
        per_device,
        mesh=mesh,
        in_specs=(
            P("gz", "gy", "gx"),
            P("gz", "gy", "gx"),
            P("gz", "gy", "gx", None, None),
            P("gz", "gy", "gx", None),
            P("gz", "gy", "gx", None),
            P("gz", "gy", "gx", None, None, None),
            P("gz", "gy", "gx", None, None, None),
        ),
        out_specs=(P("gz", "gy", "gx"), P(None, "gz", "gy", "gx")),
        check_vma=False,
    )
```

```python
import jax
import jax.numpy as jnp
from jax import lax
from jax.experimental import pallas as pl
from jax.experimental.pallas import tpu as pltpu
from jax.sharding import PartitionSpec as P


VZ = 8
VY = 8
VX = 16
NBZ = 2
NBY = 8
NBX = 8
SOURCES = 2
RAD = 4
BV = VY * VX
BLOCKS = NBZ * NBY * NBX
SLOTS = BLOCKS * SOURCES
NZ = NBZ * VZ
NY = NBY * VY
NX = NBX * VX
GROUPS = NBZ * NBY
PER = NBX * SOURCES
ROWS = PER * VZ
BRICKS = ("gy", "gx")
F32 = jnp.float32
LIMIT = 12 * 2**20
WIDE = 20 * 2**20
BF16 = jnp.bfloat16

VMEM = pl.BlockSpec(memory_space=pltpu.VMEM)
SMEM = pl.BlockSpec(memory_space=pltpu.SMEM)


OUTER = (
    jax.ShapeDtypeStruct((NZ * NY, NX), F32),
    jax.ShapeDtypeStruct((RAD * NY, NX), F32),
    jax.ShapeDtypeStruct((NZ, VY, NX), F32),
)


def iota(shape, dim):
    return lax.broadcasted_iota(jnp.int32, shape, dim)


def pieces(value, count):
    parts = []
    for _ in range(count - 1):
        part = value.astype(BF16)
        parts.append(part)
        value = value - part.astype(F32)
    parts.append(value.astype(BF16))
    return parts


def swap_chunks(rows):
    chunk = iota((VZ, BV), 1) // VX
    for k in (1, 2, 4):
        low = (chunk & k) == 0
        out = list(rows)
        for b in range(8):
            if b & k == 0:
                first, second = rows[b], rows[b + k]
                out[b] = jnp.where(low, first, pltpu.roll(second, k * VX, 1))
                out[b + k] = jnp.where(low, pltpu.roll(first, BV - k * VX, 1), second)
        rows = out
    return rows


def prepare_kernel(
    half_ref, place_ref, moving_hbm, fixed_hbm, owner_hbm, ident_hbm,
    blocks_ref, request_ref, flat_ref, image_ref, side_ref, face_ref,
    moving_ref, fixed_ref, owner_ref, ident_ref, wide, sems,
):
    pairs = [(owner_hbm, owner_ref), (ident_hbm, ident_ref), (moving_hbm, moving_ref), (fixed_hbm, fixed_ref)]
    copies = [pltpu.make_async_copy(source, target, sems.at[i]) for i, (source, target) in enumerate(pairs)]
    for copy in copies:
        copy.start()
    holders, _, width = request_ref.shape
    capacity = width // 2
    half = half_ref[0]
    copies[0].wait()
    copies[1].wait()
    owner = owner_ref[...]
    ident = ident_ref[...].astype(F32)
    groups = 2 * holders
    named = jnp.where(owner == iota((groups, SLOTS), 0), 1.0, 0.0)
    earlier = jnp.where(iota((SLOTS, SLOTS), 0) < iota((SLOTS, SLOTS), 1), 1.0, 0.0).astype(BF16)
    before = jnp.dot(named.astype(BF16), earlier, preferred_element_type=F32)
    rank = jnp.sum(named * before, axis=0, keepdims=True).astype(jnp.int32)
    upper = jnp.where(owner >= holders, 1, 0)
    holder = owner - upper * holders
    place = jnp.where(upper == half, 0, capacity) + rank
    flat_ref[...] = holder * width + place
    wanted = jnp.where(holder == iota((holders, SLOTS), 0), ident, 0.0).astype(BF16)
    at = jnp.where(place == iota((width, SLOTS), 0), 1.0, 0.0).astype(BF16)
    request = lax.dot_general(wanted, at, (((1,), (1,)), ((), ())), preferred_element_type=F32).astype(jnp.int32)
    for h in range(holders):
        request_ref[h] = request[h : h + 1, :]
    copies[2].wait()
    for z in range(NZ):
        wide[z * NY : (z + 1) * NY, :] = moving_ref[z].astype(F32)

    def group(g, _):
        start = (g // NBY) * (VZ * NY) + (g % NBY) * VY
        rows = [wide[pl.ds(start + y, VZ, stride=NY), :] for y in range(VY)]
        for x, block in enumerate(swap_chunks(rows)):
            blocks_ref[g * NBX + x] = block.astype(BF16)
        return 0

    lax.fori_loop(0, GROUPS, group, 0, unroll=4)
    copies[3].wait()
    for z in range(NZ):
        image_ref[z * NY : (z + 1) * NY, :] = fixed_ref[z].astype(F32)
    outer(place_ref, image_ref, side_ref, face_ref)


def prepare(half, place, moving, fixed, owner, ident, groups, capacity):
    holders = groups // 2
    hbm = pl.BlockSpec(memory_space=pltpu.HBM)
    return pl.pallas_call(
        prepare_kernel,
        out_shape=(
            jax.ShapeDtypeStruct((BLOCKS, VZ, BV), BF16),
            jax.ShapeDtypeStruct((holders, 1, 2 * capacity), jnp.int32),
            jax.ShapeDtypeStruct((1, SLOTS), jnp.int32),
        )
        + OUTER,
        in_specs=[SMEM, SMEM, hbm, hbm, hbm, hbm],
        out_specs=(VMEM,) * 6,
        scratch_shapes=[
            pltpu.VMEM((NZ, NY, NX), BF16),
            pltpu.VMEM((NZ, NY, NX), BF16),
            pltpu.VMEM((1, SLOTS), jnp.int32),
            pltpu.VMEM((1, SLOTS), jnp.int32),
            pltpu.VMEM((NZ * NY, NX), F32),
            pltpu.SemaphoreType.DMA((4,)),
        ],
        compiler_params=pltpu.CompilerParams(vmem_limit_bytes=LIMIT),
        name="prepare",
    )(half, place, *[pltpu.with_memory_space_constraint(a, pltpu.HBM) for a in (moving, fixed, owner, ident)])


def pick_kernel(capacity, request_ref, near_ref, far_ref, out_ref):
    width = 2 * capacity

    def holder(h, _):
        for k in range(width):
            source = near_ref if k < capacity else far_ref
            out_ref[h * width + k] = source[request_ref[h, 0, k]]
        return 0

    lax.fori_loop(0, out_ref.shape[0] // width, holder, 0)


def pick(request, near, far, capacity):
    return pl.pallas_call(
        lambda *refs: pick_kernel(capacity, *refs),
        out_shape=jax.ShapeDtypeStruct((request.size, VZ, BV), BF16),
        in_specs=[SMEM, VMEM, VMEM],
        out_specs=VMEM,
        compiler_params=pltpu.CompilerParams(vmem_limit_bytes=LIMIT),
        name="pick",
    )(request, near, far)


def spread_kernel(mix_ref, out_ref):
    pick_lane = jnp.where(iota((VZ, ROWS), 1) % VZ == iota((VZ, ROWS), 0), 1.0, 0.0).astype(BF16)
    same = iota((ROWS, ROWS), 0) // VZ == iota((ROWS, ROWS), 1) // VZ

    def group(g, _):
        weights = mix_ref[pl.ds(pl.multiple_of(g * ROWS, ROWS), ROWS), :]
        for k, part in enumerate(pieces(weights, 3)):
            tiled = jnp.dot(part, pick_lane, preferred_element_type=F32)
            out_ref[g, k * ROWS : (k + 1) * ROWS, :] = jnp.where(same, tiled, 0.0).astype(BF16)
        return 0

    lax.fori_loop(0, GROUPS, group, 0, unroll=4)


def spread(mix_z):
    return pl.pallas_call(
        spread_kernel,
        out_shape=jax.ShapeDtypeStruct((GROUPS, 3 * ROWS, ROWS), BF16),
        in_specs=[VMEM],
        out_specs=VMEM,
        compiler_params=pltpu.CompilerParams(vmem_limit_bytes=LIMIT),
        name="spread",
    )(mix_z)


STEP = 4


def mix_kernel(
    place_ref, flat_ref, received_ref, spread_ref, mix_hbm, warped_ref, side_ref, face_ref, weights_ref, sems
):
    share = STEP * PER

    def weights(step):
        rows = pl.ds(step * share, share)
        return pltpu.make_async_copy(mix_hbm.at[rows], weights_ref.at[rows], sems.at[step])

    for step in range(GROUPS // STEP):
        weights(step).start()

    def across_planes(g):
        source = jnp.concatenate([received_ref[flat_ref[g * PER + i]].astype(F32) for i in range(PER)], 0)
        parts = jnp.dot(spread_ref[g], source.astype(BF16), preferred_element_type=F32)
        mixed = parts[:ROWS] + parts[ROWS : 2 * ROWS] + parts[2 * ROWS :]
        high = mixed.astype(BF16).astype(F32)
        return high, mixed - high

    def in_plane(g, high, low):
        rows = []
        for j in range(NBX):
            a = slice(2 * j * VZ, (2 * j + 1) * VZ)
            b = slice((2 * j + 1) * VZ, (2 * j + 2) * VZ)
            left = jnp.concatenate(
                [jnp.concatenate([high[a], high[b]], 1), jnp.concatenate([low[a], low[b]], 1)], 0
            ).astype(BF16)
            right = weights_ref[pl.ds(g * PER + 2 * j, 2)].reshape(2 * BV, BV)
            both = jnp.dot(left, right, preferred_element_type=F32)
            rows.append(both[:VZ] + both[VZ:])
        return rows

    def place_rows(g, rows):
        start = (g // NBY) * (VZ * NY) + (g % NBY) * VY
        for y, row in enumerate(swap_chunks(rows)):
            warped_ref[pl.ds(start + y, VZ, stride=NY), :] = row

    def some(step, _):
        weights(step).wait()
        first = step * STEP
        mixed, done = {}, {}
        for t in range(STEP + 2):
            if t < STEP:
                mixed[t] = across_planes(first + t)
            if 0 <= t - 1 < STEP:
                done[t - 1] = in_plane(first + t - 1, *mixed.pop(t - 1))
            if 0 <= t - 2:
                place_rows(first + t - 2, done.pop(t - 2))
        return 0

    lax.fori_loop(0, GROUPS // STEP, some, 0)
    outer(place_ref, warped_ref, side_ref, face_ref)


def outer(place_ref, own_ref, side_ref, face_ref):
    first = jnp.where(place_ref[0] == 0, (NZ - RAD) * NY, 0)
    side_ref[...] = own_ref[pl.ds(pl.multiple_of(first, NY), RAD * NY), :]
    low = iota((VY, NX), 0) < RAD
    for z in range(NZ):
        face_ref[z] = jnp.where(low, own_ref[z * NY : z * NY + VY, :], own_ref[(z + 1) * NY - VY : (z + 1) * NY, :])


def mix(flat, place, received, spread_z, mix_yx):
    return pl.pallas_call(
        mix_kernel,
        out_shape=OUTER,
        in_specs=[SMEM, SMEM, VMEM, VMEM, pl.BlockSpec(memory_space=pltpu.HBM)],
        out_specs=(VMEM,) * 3,
        scratch_shapes=[
            pltpu.VMEM((SLOTS, BV, BV), BF16),
            pltpu.SemaphoreType.DMA((GROUPS // STEP,)),
        ],
        compiler_params=pltpu.CompilerParams(vmem_limit_bytes=WIDE),
        name="mix",
    )(place, flat, received, spread_z, pltpu.with_memory_space_constraint(mix_yx, pltpu.HBM))


def halves_of_gy():
    groups = lax.axis_size("gy") * lax.axis_size("gx")
    holders = groups // 2
    return groups, max(2, 2 * SLOTS // groups), [list(range(holders)), list(range(holders, groups))]


def exchange_in_half(array):
    _, _, halves = halves_of_gy()
    return lax.all_to_all(array, BRICKS, split_axis=0, concat_axis=0, tiled=True, axis_index_groups=halves)


def ask(place, moving, fixed, owners, block_ids):
    rows_gy = lax.axis_size("gy")
    groups, capacity, _ = halves_of_gy()
    half = (lax.axis_index("gy") >= rows_gy // 2).astype(jnp.int32).reshape(1)
    near, request, flat, *image = prepare(
        half, place, moving, fixed, owners.reshape(1, SLOTS), block_ids.reshape(1, SLOTS), groups, capacity
    )
    far = lax.ppermute(near, "gy", [(i, (i + rows_gy // 2) % rows_gy) for i in range(rows_gy)])
    request = exchange_in_half(request)
    return request, near, far, flat.reshape(-1), image


def answer(request, near, far):
    groups, capacity, _ = halves_of_gy()
    picked = pick(request, near, far, capacity).reshape(groups // 2, 2 * capacity, VZ, BV)
    return exchange_in_half(picked).reshape(groups * capacity, VZ, BV)


def spread_weights(counts, mix_z):
    slot_pos = jnp.arange(SLOTS, dtype=jnp.int32)
    keep = slot_pos % SOURCES < jnp.repeat(counts.reshape(-1), SOURCES)
    return spread(jnp.where(keep[:, None, None], mix_z.reshape(SLOTS, VZ, VZ), 0.0).reshape(SLOTS * VZ, VZ))


REACH = 2 * RAD
EZ = NZ + REACH
EY = NY + REACH
COUNT = float((REACH + 1) ** 3)


def call(kernel, outs, *args, scratch=()):
    return pl.pallas_call(
        kernel,
        out_shape=outs,
        in_specs=[SMEM] + [VMEM] * (len(args) - 1),
        out_specs=jax.tree.map(lambda _: VMEM, outs),
        scratch_shapes=scratch,
        compiler_params=pltpu.CompilerParams(vmem_limit_bytes=LIMIT),
    )(*args)


def array(*shape):
    return jax.ShapeDtypeStruct(shape, F32)


def rows_kernel(packed_count, place_ref, face_ref, side_ref, *refs):
    packed, outs = refs[:packed_count], refs[packed_count:]
    even = place_ref[1] == 0
    low = iota((VY, NX), 0) < RAD
    faces = [face_ref[p] for p in range(NZ)]
    for ref, at in [(side_ref, p * NY) for p in range(RAD)] + [(ref, 0) for ref in packed]:
        faces.append(jnp.where(low, ref[at : at + VY, :], ref[at + NY - VY : at + NY, :]))
    for p, face in enumerate(faces):
        outs[0][p] = jnp.where(even, face[RAD:], face[:RAD])
        if len(outs) == 2:
            outs[1][p] = jnp.where(even, face[:RAD], face[RAD:])


def extended_planes(place_ref, own, side):
    low = place_ref[0] == 0
    empty = jnp.zeros_like(side[0])
    before = [jnp.where(low, empty, s) for s in side]
    after = [jnp.where(low, s, empty) for s in side]
    return before + own + after


def pack(place_ref, planes, k):
    even = place_ref[2] == 0
    lift = jnp.where(even, RAD, 0) if k == 0 else jnp.where(even, 0, RAD)
    slot = iota((VY, NX), 1) // RAD
    packed = jnp.zeros((VY, NX), F32)
    for p, rows in enumerate(planes):
        packed = jnp.where(slot == p, pltpu.roll(rows, lift + p * RAD, 1), packed)
    return packed


def window(parts, length):
    two = [parts[i] + parts[i + 1] for i in range(len(parts) - 1)]
    four = [two[i] + two[i + 2] for i in range(len(two) - 2)]
    eight = [four[i] + four[i + 4] for i in range(len(four) - 4)]
    return [eight[i] + parts[i + 8] for i in range(length)]


def pack_kernel(place_ref, own_ref, side_ref, *columns):
    def rows_of(q, _):
        at = pl.multiple_of(q * VY, VY)
        planes = own_planes(place_ref, own_ref, side_ref, at)
        for k, column in enumerate(columns):
            column[pl.ds(at, VY), :] = pack(place_ref, planes, k)
        return 0

    lax.fori_loop(0, NBY, rows_of, 0, unroll=2)


def own_planes(place_ref, own_ref, side_ref, at):
    own = [own_ref[pl.ds(pl.multiple_of(z * NY + at, VY), VY), :] for z in range(NZ)]
    side = [side_ref[pl.ds(pl.multiple_of(z * NY + at, VY), VY), :] for z in range(RAD)]
    return extended_planes(place_ref, own, side)


def own_kernel(with_image, place_ref, own_ref, side_ref, *refs):
    image_ref, sums_ref, *columns = refs
    if with_image:
        out_ref = columns.pop(0)
        for z in range(NZ):
            out_ref[z] = own_ref[z * NY : (z + 1) * NY, :]

    def rows_of(q, _):
        at = pl.multiple_of(q * VY, VY)
        rows = pl.ds(at, VY)
        planes = own_planes(place_ref, own_ref, side_ref, at)
        for k, column in enumerate(columns):
            column[rows, :] = pack(place_ref, planes, k)
        fields = [planes, [v * v for v in planes]]
        if with_image:
            fields.append([image_ref[p, rows, :] * v for p, v in enumerate(planes)])
        else:
            for p, v in enumerate(planes):
                image_ref[p, rows, :] = v
        for f, parts in enumerate(fields):
            for z, total in enumerate(window(parts, NZ)):
                sums_ref[f * NZ + z, rows, :] = total
        return 0

    lax.fori_loop(0, NBY, rows_of, 0)


def columns_kernel(y_count, x_count, place_ref, *refs):
    halos, packed, (rows_ref, *columns) = refs[:y_count], refs[y_count : y_count + x_count], refs[y_count + x_count :]
    even = place_ref[1] == 0
    planes = []
    for p in range(halos[0].shape[0]):
        first = halos[0][p]
        second = halos[1][p] if y_count == 2 else jnp.zeros_like(first)
        planes.append(jnp.concatenate([jnp.where(even, first, second), jnp.where(even, second, first)], 0))
    come = planes[NZ + RAD :]
    planes = extended_planes(place_ref, planes[:NZ], planes[NZ : NZ + RAD])
    for p, rows in enumerate(planes):
        rows_ref[p] = rows
    for k in range(x_count):
        columns[k][:NY] = packed[k][...]
        columns[k][NY:] = come[k] if come else pack(place_ref, planes, k)


def window_rows(value):
    two = value + pltpu.roll(value, EY - 1, 0)
    four = two + pltpu.roll(two, EY - 2, 0)
    return (value + pltpu.roll(four, RAD, 0) + pltpu.roll(four, EY - 1, 0))[:NY]


def split_dot(value, table):
    total = None
    for part in pieces(value, 3):
        term = jnp.dot(part, table, preferred_element_type=F32)
        total = term if total is None else total + term
    return total


def edge_table(right):
    row, col = iota((NX, NX), 0), iota((NX, NX), 1)
    plane, i = row // RAD, row % RAD
    z, j = col // RAD, col % RAD
    reach = jnp.where(right, j - i, i - j)
    inside = (plane >= z) & (plane <= z + REACH) & (z < NZ) & (plane < EZ) & (reach >= 0)
    return jnp.where(inside, 1.0, 0.0).astype(BF16)


def at_edge(right, rows):
    return iota((rows, NX), 1) // RAD == jnp.where(right, NX // RAD - 1, 0)


def edge_part(sums, z, right, mask):
    base = jnp.where(right, NX - RAD, 0)
    return jnp.where(mask, pltpu.roll(sums, lax.rem(base + NX - RAD * z, NX), 1), 0.0)


def side_is_right(place_ref, k):
    even = place_ref[2] == 0
    return even if k == 0 else jnp.logical_not(even)


def near_columns():
    return jnp.where(jnp.abs(iota((NX, NX), 0) - iota((NX, NX), 1)) <= RAD, 1.0, 0.0).astype(BF16)


def brick_sums(count, load, out_ref, line, pair, four):
    near = near_columns()
    lanes = line.shape[0]

    def some(step, _):
        for k in range(lanes):
            i = step * lanes + k
            own, halo = load(i)
            line[k, :RAD] = halo[RAD:]
            line[k, RAD : RAD + NY] = own
            line[k, RAD + NY : EY] = halo[:RAD]
            pair[k, :EY] = line[k, :EY] + line[k, 1 : EY + 1]
            four[k, :EY] = pair[k, :EY] + pair[k, 2 : EY + 2]
            total = four[k, :NY] + four[k, RAD : RAD + NY] + line[k, REACH : REACH + NY]
            out_ref[i] = split_dot(total, near)
        return 0

    lax.fori_loop(0, count // lanes, some, 0)


LINES = (pltpu.VMEM((4, EY + VY, NX), F32),) * 3


def image_sums_kernel(place_ref, own_sums_ref, out_ref, *lines):
    brick_sums(2 * NZ, lambda i: (own_sums_ref[i], jnp.zeros((VY, NX), F32)), out_ref, *lines)


def halo_sums(fields, outer_sums):
    for f, parts in enumerate(fields):
        for z, total in enumerate(window(parts, NZ)):
            outer_sums[f * NZ + z] = total


def warped_sums_kernel(place_ref, own_sums_ref, rows_ref, image_rows_ref, out_ref, outer_sums, *lines):
    w = [rows_ref[p] for p in range(EZ)]
    halo_sums([w, [v * v for v in w], [image_rows_ref[p] * v for p, v in enumerate(w)]], outer_sums)
    brick_sums(3 * NZ, lambda i: (own_sums_ref[i], outer_sums[i]), out_ref, *lines)


def halo_part(total):
    row = iota(total.shape, 0) % VY
    size = total.shape[0]
    turned = jnp.where(row < RAD, pltpu.roll(total, size - RAD, 0), pltpu.roll(total, RAD, 0))
    for k in (1, 2):
        up, down = pltpu.roll(turned, size - k, 0), pltpu.roll(turned, k, 0)
        turned = turned + jnp.where(row < RAD - k, up, jnp.where(row >= RAD + k, down, 0.0))
    return turned


def add_edges(x_count, place_ref, z, box, edges, stride, start):
    rows = box[0].shape[0]
    for k in range(x_count):
        right = side_is_right(place_ref, k)
        mask = at_edge(right, rows)
        box = [
            total + edge_part(edges[stride * k + i, start : start + rows, :], z, right, mask)
            for i, total in enumerate(box)
        ]
    return box


def image_box_kernel(x_count, place_ref, sums_ref, image_ref, rows_ref, *refs):
    halos, (out_ref, edges, outer_sums) = refs[:x_count], refs[x_count:]
    for k in range(x_count):
        table = edge_table(side_is_right(place_ref, k))
        f = halos[k][...]
        for i, field in enumerate([f, f * f]):
            edges[2 * k + i] = split_dot(window_rows(field), table)
    f = [rows_ref[p] for p in range(EZ)]
    halo_sums([f, [v * v for v in f]], outer_sums)
    outer = split_dot(halo_part(outer_sums[...].reshape(2 * NZ * VY, NX)), near_columns())
    outer_sums[...] = outer.reshape(2 * NZ, VY, NX)
    first = iota((VY, NX), 0) < RAD
    scale = 1.0 / COUNT

    def plane(z, _):
        box = []
        for f in range(2):
            total, rows = sums_ref[f * NZ + z], outer_sums[f * NZ + z]
            box.append(
                jnp.concatenate(
                    [
                        total[:VY] + jnp.where(first, rows, 0.0),
                        total[VY : NY - VY],
                        total[NY - VY :] + jnp.where(first, 0.0, rows),
                    ],
                    0,
                )
            )
        box = add_edges(x_count, place_ref, z, box, edges, 2, 0)
        mean = box[0] * scale
        out_ref[z] = mean
        out_ref[NZ + z] = image_ref[pl.ds(pl.multiple_of(z * NY, NY), NY), :] - mean
        out_ref[2 * NZ + z] = 1.0 / (box[1] * scale - mean * mean + 1e-5)
        return 0

    lax.fori_loop(0, NZ, plane, 0, unroll=2)


HALF = NY // 2


def force_kernel(x_count, place_ref, sums_ref, image_ref, own_ref, side_ref, rows_ref, *refs):
    warped_halos, fixed_halos = refs[:x_count], refs[x_count : 2 * x_count]
    force_ref, edges = refs[2 * x_count], refs[2 * x_count + 1]
    for k in range(x_count):
        table = edge_table(side_is_right(place_ref, k))
        w, f = warped_halos[k][...], fixed_halos[k][...]
        for i, field in enumerate([w, w * w, f * w]):
            edges[4 * k + i] = split_dot(window_rows(field), table)
        edges[4 * k + 3] = w[:NY]
    scale = 1.0 / COUNT
    lane = iota((HALF, NX), 1)
    low = place_ref[0] == 0

    def plane(z, _):
        at = pl.multiple_of(z * NY, NY)
        tall = jnp.concatenate([own_ref[pl.ds(at, NY), :], rows_ref[z + RAD]], 0)
        force_ref[1, z] = (pltpu.roll(tall, EY - 1, 0) - pltpu.roll(tall, 1, 0))[:NY]
        above = pl.multiple_of(jnp.minimum(at + NY, (NZ - 1) * NY), NY)
        below = pl.multiple_of(jnp.maximum(at - NY, 0), NY)
        for h in range(0, NY, HALF):
            part = slice(h, h + HALF)
            own = own_ref[pl.ds(at + h, HALF), :]
            box = [sums_ref[f * NZ + z, part, :] for f in range(3)]
            box = add_edges(x_count, place_ref, z, box, edges, 4, h)
            mean_w = box[0] * scale
            cov = box[2] * scale - image_ref[z, part, :] * mean_w
            ratio = cov / (box[1] * scale - mean_w * mean_w + 1e-5)
            half = (ratio * image_ref[2 * NZ + z, part, :]) * (image_ref[NZ + z, part, :] - ratio * (own - mean_w))
            up, down = own_ref[pl.ds(above + h, HALF), :], own_ref[pl.ds(below + h, HALF), :]
            up = jnp.where(z == NZ - 1, jnp.where(low, side_ref[part, :], 0.0), up)
            down = jnp.where(z == 0, jnp.where(low, 0.0, side_ref[(RAD - 1) * NY + h : (RAD - 1) * NY + h + HALF, :]), down)
            force_ref[0, z, part, :] = half * (up - down)
            force_ref[1, z, part, :] = half * force_ref[1, z, part, :]
            after = jnp.where(lane == NX - 1, 0.0, pltpu.roll(own, NX - 1, 1))
            before = jnp.where(lane == 0, 0.0, pltpu.roll(own, 1, 1))
            for k in range(x_count):
                right = side_is_right(place_ref, k)
                turn = jnp.where(right, NX - 1, NX + 1 - RAD) + NX - RAD * (z + RAD)
                halo = pltpu.roll(edges[4 * k + 3, part, :], lax.rem(turn, NX), 1)
                after = jnp.where(lane == jnp.where(right, NX - 1, -1), halo, after)
                before = jnp.where(lane == jnp.where(right, -1, 0), halo, before)
            force_ref[2, z, part, :] = half * (after - before)
        return 0

    lax.fori_loop(0, NZ, plane, 0)


def pairings(size):
    even = [(i, i ^ 1) for i in range(size) if (i ^ 1) < size]
    odd = [(i, i + 1 if i % 2 else i - 1) for i in range(1, size)]
    odd = [(i, j) for i, j in odd if j < size]
    return [pairs for pairs in (even, odd) if pairs]


def exchange_planes(side):
    return lax.ppermute(side, "gz", pairings(lax.axis_size("gz"))[0])


def rows_to_send(place, face, side, *packed):
    count = len(pairings(lax.axis_size("gy")))
    return call(
        lambda *refs: rows_kernel(len(packed), *refs),
        (array(NZ + RAD + len(packed), RAD, NX),) * count,
        place,
        face,
        side,
        *packed,
    )


def exchange_rows(sent):
    along = pairings(lax.axis_size("gy"))
    return [lax.ppermute(s, "gy", pairs) for s, pairs in reversed(list(zip(sent, along)))][::-1]


def exchange_columns(columns):
    along = pairings(lax.axis_size("gx"))
    return [lax.ppermute(c, "gx", pairs) for c, pairs in zip(columns, along)]


def pack_columns(place, received, packed):
    count = len(packed)
    rows, *columns = call(
        lambda *refs: columns_kernel(len(received), count, *refs),
        (array(EZ, VY, NX),) + (array(EY, NX),) * count,
        place,
        *received,
        *packed,
    )
    return rows, columns


def per_device(fixed, moving, owners, block_ids, counts, mix_yx, mix_z):
    place = jnp.stack([lax.axis_index("gz"), lax.axis_index("gy") % 2, lax.axis_index("gx") % 2]).astype(jnp.int32)
    count = len(pairings(lax.axis_size("gx")))
    request, near, far, flat, (image, image_side, image_face) = ask(place, moving, fixed, owners, block_ids)
    image_side = exchange_planes(image_side)
    image_packed = call(pack_kernel, (array(NY, NX),) * count, place, image, image_side)
    image_packed = exchange_columns(image_packed)
    request, image_packed = lax.optimization_barrier((request, image_packed))
    received = answer(request, near, far)
    image_sent = rows_to_send(place, image_face, image_side, *image_packed)
    image_halos = exchange_rows(image_sent)
    weights = spread_weights(counts, mix_z)
    image_sums, image_planes = call(
        lambda place_ref, own_ref, side_ref, sums_ref, image_ref: own_kernel(
            False, place_ref, own_ref, side_ref, image_ref, sums_ref
        ),
        (array(2 * NZ, NY, NX), array(EZ, NY, NX)),
        place,
        image,
        image_side,
    )
    image_sums = call(image_sums_kernel, array(2 * NZ, NY, NX), place, image_sums, scratch=LINES)
    received, weights, image_sums = lax.optimization_barrier((received, weights, image_sums))
    warped, side, face = mix(flat, place, received, weights, mix_yx.reshape(SLOTS, BV, BV))
    side = exchange_planes(side)
    row_halos = exchange_rows(rows_to_send(place, face, side))
    own_sums, out, *packed = call(
        lambda *refs: own_kernel(True, *refs),
        (array(3 * NZ, NY, NX), array(NZ, NY, NX)) + (array(NY, NX),) * count,
        place,
        warped,
        side,
        image_planes,
    )
    image_rows, image_columns = pack_columns(place, image_halos, image_packed)
    image_box = call(
        lambda *refs: image_box_kernel(count, *refs),
        array(3 * NZ, NY, NX),
        place,
        image_sums,
        image,
        image_rows,
        *image_columns,
        scratch=(pltpu.VMEM((2 * count, NY, NX), F32), pltpu.VMEM((2 * NZ, VY, NX), F32)),
    )
    rows, columns = pack_columns(place, row_halos, packed)
    columns = exchange_columns(columns)
    box = call(
        warped_sums_kernel,
        array(3 * NZ, NY, NX),
        place,
        own_sums,
        rows,
        image_rows,
        scratch=(pltpu.VMEM((3 * NZ, VY, NX), F32),) + LINES,
    )
    force = call(
        lambda *refs: force_kernel(count, *refs),
        array(3, NZ, NY, NX),
        place,
        box,
        image_box,
        warped,
        side,
        rows,
        *columns,
        *image_columns,
        scratch=(pltpu.VMEM((4 * count, NY, NX), F32),),
    )
    return out, force


def solution(mesh):
    return jax.shard_map(
        per_device,
        mesh=mesh,
        in_specs=(
            P("gz", "gy", "gx"),
            P("gz", "gy", "gx"),
            P("gz", "gy", "gx", None, None),
            P("gz", "gy", "gx", None),
            P("gz", "gy", "gx", None),
            P("gz", "gy", "gx", None, None, None),
            P("gz", "gy", "gx", None, None, None),
        ),
        out_specs=(P("gz", "gy", "gx"), P(None, "gz", "gy", "gx")),
        check_vma=False,
    )
```

```python
import jax
import jax.numpy as jnp
from jax import lax
from jax.experimental import pallas as pl
from jax.experimental.pallas import tpu as pltpu
from jax.sharding import PartitionSpec as P


VZ = 8
VY = 8
VX = 16
NBZ = 2
NBY = 8
NBX = 8
SOURCES = 2
RAD = 4
BV = VY * VX
BLOCKS = NBZ * NBY * NBX
SLOTS = BLOCKS * SOURCES
NZ = NBZ * VZ
NY = NBY * VY
NX = NBX * VX
GROUPS = NBZ * NBY
PER = NBX * SOURCES
ROWS = PER * VZ
BRICKS = ("gy", "gx")
F32 = jnp.float32
LIMIT = 12 * 2**20
WIDE = 20 * 2**20
BF16 = jnp.bfloat16

VMEM = pl.BlockSpec(memory_space=pltpu.VMEM)
SMEM = pl.BlockSpec(memory_space=pltpu.SMEM)


OUTER = (
    jax.ShapeDtypeStruct((NZ * NY, NX), F32),
    jax.ShapeDtypeStruct((RAD * NY, NX), F32),
    jax.ShapeDtypeStruct((NZ, VY, NX), F32),
)


def iota(shape, dim):
    return lax.broadcasted_iota(jnp.int32, shape, dim)


def pieces(value, count):
    parts = []
    for _ in range(count - 1):
        part = value.astype(BF16)
        parts.append(part)
        value = value - part.astype(F32)
    parts.append(value.astype(BF16))
    return parts


def swap_chunks(rows):
    chunk = iota((VZ, BV), 1) // VX
    for k in (1, 2, 4):
        low = (chunk & k) == 0
        out = list(rows)
        for b in range(8):
            if b & k == 0:
                first, second = rows[b], rows[b + k]
                out[b] = jnp.where(low, first, pltpu.roll(second, k * VX, 1))
                out[b + k] = jnp.where(low, pltpu.roll(first, BV - k * VX, 1), second)
        rows = out
    return rows


def prepare_kernel(
    half_ref, place_ref, moving_hbm, fixed_hbm, owner_hbm, ident_hbm,
    blocks_ref, request_ref, flat_ref, image_ref, side_ref, face_ref,
    moving_ref, fixed_ref, owner_ref, ident_ref, wide, sems,
):
    pairs = [(owner_hbm, owner_ref), (ident_hbm, ident_ref), (moving_hbm, moving_ref), (fixed_hbm, fixed_ref)]
    copies = [pltpu.make_async_copy(source, target, sems.at[i]) for i, (source, target) in enumerate(pairs)]
    for copy in copies:
        copy.start()
    holders, _, width = request_ref.shape
    capacity = width // 2
    half = half_ref[0]
    copies[0].wait()
    copies[1].wait()
    owner = owner_ref[...]
    ident = ident_ref[...].astype(F32)
    groups = 2 * holders
    named = jnp.where(owner == iota((groups, SLOTS), 0), 1.0, 0.0)
    earlier = jnp.where(iota((SLOTS, SLOTS), 0) < iota((SLOTS, SLOTS), 1), 1.0, 0.0).astype(BF16)
    before = jnp.dot(named.astype(BF16), earlier, preferred_element_type=F32)
    rank = jnp.sum(named * before, axis=0, keepdims=True).astype(jnp.int32)
    upper = jnp.where(owner >= holders, 1, 0)
    holder = owner - upper * holders
    place = jnp.where(upper == half, 0, capacity) + rank
    flat_ref[...] = holder * width + place
    wanted = jnp.where(holder == iota((holders, SLOTS), 0), ident, 0.0).astype(BF16)
    at = jnp.where(place == iota((width, SLOTS), 0), 1.0, 0.0).astype(BF16)
    request = lax.dot_general(wanted, at, (((1,), (1,)), ((), ())), preferred_element_type=F32).astype(jnp.int32)
    for h in range(holders):
        request_ref[h] = request[h : h + 1, :]
    copies[2].wait()
    for z in range(NZ):
        wide[z * NY : (z + 1) * NY, :] = moving_ref[z].astype(F32)

    def group(g, _):
        start = (g // NBY) * (VZ * NY) + (g % NBY) * VY
        rows = [wide[pl.ds(start + y, VZ, stride=NY), :] for y in range(VY)]
        for x, block in enumerate(swap_chunks(rows)):
            blocks_ref[g * NBX + x] = block.astype(BF16)
        return 0

    lax.fori_loop(0, GROUPS, group, 0, unroll=4)
    copies[3].wait()
    for z in range(NZ):
        image_ref[z * NY : (z + 1) * NY, :] = fixed_ref[z].astype(F32)
    outer(place_ref, image_ref, side_ref, face_ref)


def prepare(half, place, moving, fixed, owner, ident, groups, capacity):
    holders = groups // 2
    hbm = pl.BlockSpec(memory_space=pltpu.HBM)
    return pl.pallas_call(
        prepare_kernel,
        out_shape=(
            jax.ShapeDtypeStruct((BLOCKS, VZ, BV), BF16),
            jax.ShapeDtypeStruct((holders, 1, 2 * capacity), jnp.int32),
            jax.ShapeDtypeStruct((1, SLOTS), jnp.int32),
        )
        + OUTER,
        in_specs=[SMEM, SMEM, hbm, hbm, hbm, hbm],
        out_specs=(VMEM,) * 6,
        scratch_shapes=[
            pltpu.VMEM((NZ, NY, NX), BF16),
            pltpu.VMEM((NZ, NY, NX), BF16),
            pltpu.VMEM((1, SLOTS), jnp.int32),
            pltpu.VMEM((1, SLOTS), jnp.int32),
            pltpu.VMEM((NZ * NY, NX), F32),
            pltpu.SemaphoreType.DMA((4,)),
        ],
        compiler_params=pltpu.CompilerParams(vmem_limit_bytes=LIMIT),
        name="prepare",
    )(half, place, *[pltpu.with_memory_space_constraint(a, pltpu.HBM) for a in (moving, fixed, owner, ident)])


def pick_kernel(capacity, request_ref, near_ref, far_ref, out_ref):
    width = 2 * capacity

    for h in range(out_ref.shape[0] // width):
        for k in range(width):
            source = near_ref if k < capacity else far_ref
            out_ref[h * width + k] = source[request_ref[h, 0, k]]


def pick(request, near, far, capacity):
    return pl.pallas_call(
        lambda *refs: pick_kernel(capacity, *refs),
        out_shape=jax.ShapeDtypeStruct((request.size, VZ, BV), BF16),
        in_specs=[SMEM, VMEM, VMEM],
        out_specs=VMEM,
        compiler_params=pltpu.CompilerParams(vmem_limit_bytes=LIMIT),
        name="pick",
    )(request, near, far)


def spread_kernel(mix_ref, out_ref):
    pick_lane = jnp.where(iota((VZ, ROWS), 1) % VZ == iota((VZ, ROWS), 0), 1.0, 0.0).astype(BF16)
    same = iota((ROWS, ROWS), 0) // VZ == iota((ROWS, ROWS), 1) // VZ

    def group(g, _):
        weights = mix_ref[pl.ds(pl.multiple_of(g * ROWS, ROWS), ROWS), :]
        for k, part in enumerate(pieces(weights, 3)):
            tiled = jnp.dot(part, pick_lane, preferred_element_type=F32)
            out_ref[g, k * ROWS : (k + 1) * ROWS, :] = jnp.where(same, tiled, 0.0).astype(BF16)
        return 0

    lax.fori_loop(0, GROUPS, group, 0, unroll=4)


def spread(mix_z):
    return pl.pallas_call(
        spread_kernel,
        out_shape=jax.ShapeDtypeStruct((GROUPS, 3 * ROWS, ROWS), BF16),
        in_specs=[VMEM],
        out_specs=VMEM,
        compiler_params=pltpu.CompilerParams(vmem_limit_bytes=LIMIT),
        name="spread",
    )(mix_z)


STEP = 4


def mix_kernel(
    place_ref, flat_ref, received_ref, spread_ref, mix_hbm, warped_ref, side_ref, face_ref,
    weights_ref, left_ref, blocks_ref, sems,
):
    share = STEP * PER
    steps = GROUPS // STEP

    def weights(step):
        rows = pl.ds(step * share, share)
        return pltpu.make_async_copy(mix_hbm.at[rows], weights_ref.at[rows], sems.at[step])

    for step in range(steps):
        weights(step).start()

    def across_planes(g):
        source = jnp.concatenate([received_ref[flat_ref[g * PER + i]].astype(F32) for i in range(PER)], 0)
        parts = jnp.dot(spread_ref[g], source.astype(BF16), preferred_element_type=F32)
        mixed = parts[:ROWS] + parts[ROWS : 2 * ROWS] + parts[2 * ROWS :]
        high = mixed.astype(BF16).astype(F32)
        low = mixed - high
        for j in range(NBX):
            a = slice(2 * j * VZ, (2 * j + 1) * VZ)
            b = slice((2 * j + 1) * VZ, (2 * j + 2) * VZ)
            left_ref[g * NBX + j] = jnp.concatenate(
                [jnp.concatenate([high[a], high[b]], 1), jnp.concatenate([low[a], low[b]], 1)], 0
            ).astype(BF16)

    def in_plane(g):
        for j in range(NBX):
            right = weights_ref[g * PER + 2 * j : g * PER + 2 * j + 2].reshape(2 * BV, BV)
            both = jnp.dot(left_ref[g * NBX + j], right, preferred_element_type=F32)
            blocks_ref[g * NBX + j] = both[:VZ] + both[VZ:]

    def into_rows(g):
        start = (g // NBY) * (VZ * NY) + (g % NBY) * VY
        for y, row in enumerate(swap_chunks([blocks_ref[g * NBX + j] for j in range(NBX)])):
            warped_ref[pl.ds(start + y, VZ, stride=NY), :] = row

    for step in range(-1, steps + 1):
        if 0 <= step < steps:
            weights(step).wait()
        for q in range(STEP):
            if step + 1 < steps:
                across_planes((step + 1) * STEP + q)
            if 0 <= step < steps:
                in_plane(step * STEP + q)
            if step >= 1:
                into_rows((step - 1) * STEP + q)
    outer(place_ref, warped_ref, side_ref, face_ref)


def outer(place_ref, own_ref, side_ref, face_ref):
    first = jnp.where(place_ref[0] == 0, (NZ - RAD) * NY, 0)
    side_ref[...] = own_ref[pl.ds(pl.multiple_of(first, NY), RAD * NY), :]
    low = iota((VY, NX), 0) < RAD
    for z in range(NZ):
        face_ref[z] = jnp.where(low, own_ref[z * NY : z * NY + VY, :], own_ref[(z + 1) * NY - VY : (z + 1) * NY, :])


def mix(flat, place, received, spread_z, mix_yx):
    return pl.pallas_call(
        mix_kernel,
        out_shape=OUTER,
        in_specs=[SMEM, SMEM, VMEM, VMEM, pl.BlockSpec(memory_space=pltpu.HBM)],
        out_specs=(VMEM,) * 3,
        scratch_shapes=[
            pltpu.VMEM((SLOTS, BV, BV), BF16),
            pltpu.VMEM((BLOCKS, 2 * VZ, 2 * BV), BF16),
            pltpu.VMEM((BLOCKS, VZ, BV), F32),
            pltpu.SemaphoreType.DMA((GROUPS // STEP,)),
        ],
        compiler_params=pltpu.CompilerParams(vmem_limit_bytes=WIDE),
        name="mix",
    )(place, flat, received, spread_z, pltpu.with_memory_space_constraint(mix_yx, pltpu.HBM))


def halves_of_gy():
    groups = lax.axis_size("gy") * lax.axis_size("gx")
    holders = groups // 2
    return groups, max(2, 2 * SLOTS // groups), [list(range(holders)), list(range(holders, groups))]


def exchange_in_half(array):
    _, _, halves = halves_of_gy()
    return lax.all_to_all(array, BRICKS, split_axis=0, concat_axis=0, tiled=True, axis_index_groups=halves)


def ask(place, moving, fixed, owners, block_ids):
    rows_gy = lax.axis_size("gy")
    groups, capacity, _ = halves_of_gy()
    half = (lax.axis_index("gy") >= rows_gy // 2).astype(jnp.int32).reshape(1)
    near, request, flat, *image = prepare(
        half, place, moving, fixed, owners.reshape(1, SLOTS), block_ids.reshape(1, SLOTS), groups, capacity
    )
    far = lax.ppermute(near, "gy", [(i, (i + rows_gy // 2) % rows_gy) for i in range(rows_gy)])
    request = exchange_in_half(request)
    return request, near, far, flat.reshape(-1), image


def answer(request, near, far):
    groups, capacity, _ = halves_of_gy()
    picked = pick(request, near, far, capacity).reshape(groups // 2, 2 * capacity, VZ, BV)
    return exchange_in_half(picked).reshape(groups * capacity, VZ, BV)


def spread_weights(counts, mix_z):
    slot_pos = jnp.arange(SLOTS, dtype=jnp.int32)
    keep = slot_pos % SOURCES < jnp.repeat(counts.reshape(-1), SOURCES)
    return spread(jnp.where(keep[:, None, None], mix_z.reshape(SLOTS, VZ, VZ), 0.0).reshape(SLOTS * VZ, VZ))


REACH = 2 * RAD
EZ = NZ + REACH
EY = NY + REACH
COUNT = float((REACH + 1) ** 3)


def call(kernel, outs, *args, scratch=(), out_hbm=None):
    specs = jax.tree.map(lambda _: VMEM, outs)
    if out_hbm is not None:
        specs = tuple(pl.BlockSpec(memory_space=pltpu.HBM) if i == out_hbm else VMEM for i in range(len(outs)))
    return pl.pallas_call(
        kernel,
        out_shape=outs,
        in_specs=[SMEM] + [VMEM] * (len(args) - 1),
        out_specs=specs,
        scratch_shapes=scratch,
        compiler_params=pltpu.CompilerParams(vmem_limit_bytes=LIMIT),
    )(*args)


def array(*shape):
    return jax.ShapeDtypeStruct(shape, F32)


def rows_kernel(packed_count, place_ref, face_ref, side_ref, *refs):
    packed, outs = refs[:packed_count], refs[packed_count:]
    even = place_ref[1] == 0
    low = iota((VY, NX), 0) < RAD
    faces = [face_ref[p] for p in range(NZ)]
    for ref, at in [(side_ref, p * NY) for p in range(RAD)] + [(ref, 0) for ref in packed]:
        faces.append(jnp.where(low, ref[at : at + VY, :], ref[at + NY - VY : at + NY, :]))
    for p, face in enumerate(faces):
        outs[0][p] = jnp.where(even, face[RAD:], face[:RAD])
        if len(outs) == 2:
            outs[1][p] = jnp.where(even, face[:RAD], face[RAD:])


def extended_planes(place_ref, own, side):
    low = place_ref[0] == 0
    empty = jnp.zeros_like(side[0])
    before = [jnp.where(low, empty, s) for s in side]
    after = [jnp.where(low, s, empty) for s in side]
    return before + own + after


def pack(place_ref, planes, k):
    even = place_ref[2] == 0
    lift = jnp.where(even, RAD, 0) if k == 0 else jnp.where(even, 0, RAD)
    slot = iota((VY, NX), 1) // RAD
    packed = jnp.zeros((VY, NX), F32)
    for p, rows in enumerate(planes):
        packed = jnp.where(slot == p, pltpu.roll(rows, lift + p * RAD, 1), packed)
    return packed


def window(parts, length):
    two = [parts[i] + parts[i + 1] for i in range(len(parts) - 1)]
    four = [two[i] + two[i + 2] for i in range(len(two) - 2)]
    eight = [four[i] + four[i + 4] for i in range(len(four) - 4)]
    return [eight[i] + parts[i + 8] for i in range(length)]


def pack_kernel(place_ref, own_ref, side_ref, *columns):
    def rows_of(q, _):
        at = pl.multiple_of(q * VY, VY)
        planes = own_planes(place_ref, own_ref, side_ref, at)
        for k, column in enumerate(columns):
            column[pl.ds(at, VY), :] = pack(place_ref, planes, k)
        return 0

    lax.fori_loop(0, NBY, rows_of, 0, unroll=2)


def own_planes(place_ref, own_ref, side_ref, at):
    own = [own_ref[pl.ds(pl.multiple_of(z * NY + at, VY), VY), :] for z in range(NZ)]
    side = [side_ref[pl.ds(pl.multiple_of(z * NY + at, VY), VY), :] for z in range(RAD)]
    return extended_planes(place_ref, own, side)


def own_kernel(with_image, place_ref, own_ref, side_ref, *refs):
    image_ref, sums_ref, *columns = refs
    if with_image:
        out_hbm, sem = columns.pop(0), columns.pop()
        copy = pltpu.make_async_copy(own_ref, out_hbm, sem)
        copy.start()

    def rows_of(q, _):
        at = pl.multiple_of(q * VY, VY)
        rows = pl.ds(at, VY)
        planes = own_planes(place_ref, own_ref, side_ref, at)
        for k, column in enumerate(columns):
            column[rows, :] = pack(place_ref, planes, k)
        fields = [planes, [v * v for v in planes]]
        if with_image:
            fields.append([image_ref[p, rows, :] * v for p, v in enumerate(planes)])
        else:
            for p, v in enumerate(planes):
                image_ref[p, rows, :] = v
        for f, parts in enumerate(fields):
            for z, total in enumerate(window(parts, NZ)):
                sums_ref[f * NZ + z, rows, :] = total
        return 0

    lax.fori_loop(0, NBY, rows_of, 0)
    if with_image:
        copy.wait()


def columns_kernel(y_count, x_count, place_ref, *refs):
    halos, packed, (rows_ref, *columns) = refs[:y_count], refs[y_count : y_count + x_count], refs[y_count + x_count :]
    even = place_ref[1] == 0
    planes = []
    for p in range(halos[0].shape[0]):
        first = halos[0][p]
        second = halos[1][p] if y_count == 2 else jnp.zeros_like(first)
        planes.append(jnp.concatenate([jnp.where(even, first, second), jnp.where(even, second, first)], 0))
    come = planes[NZ + RAD :]
    planes = extended_planes(place_ref, planes[:NZ], planes[NZ : NZ + RAD])
    for p, rows in enumerate(planes):
        rows_ref[p] = rows
    for k in range(x_count):
        columns[k][:NY] = packed[k][...]
        columns[k][NY:] = come[k] if come else pack(place_ref, planes, k)


def window_rows(value):
    two = value + pltpu.roll(value, EY - 1, 0)
    four = two + pltpu.roll(two, EY - 2, 0)
    return (value + pltpu.roll(four, RAD, 0) + pltpu.roll(four, EY - 1, 0))[:NY]


def split_dot(value, table):
    total = None
    for part in pieces(value, 3):
        term = jnp.dot(part, table, preferred_element_type=F32)
        total = term if total is None else total + term
    return total


def edge_table(right):
    row, col = iota((NX, NX), 0), iota((NX, NX), 1)
    plane, i = row // RAD, row % RAD
    z, j = col // RAD, col % RAD
    reach = jnp.where(right, j - i, i - j)
    inside = (plane >= z) & (plane <= z + REACH) & (z < NZ) & (plane < EZ) & (reach >= 0)
    return jnp.where(inside, 1.0, 0.0).astype(BF16)


def at_edge(right, rows):
    return iota((rows, NX), 1) // RAD == jnp.where(right, NX // RAD - 1, 0)


def edge_part(sums, z, right, mask):
    base = jnp.where(right, NX - RAD, 0)
    return jnp.where(mask, pltpu.roll(sums, lax.rem(base + NX - RAD * z, NX), 1), 0.0)


def side_is_right(place_ref, k):
    even = place_ref[2] == 0
    return even if k == 0 else jnp.logical_not(even)


def near_columns():
    return jnp.where(jnp.abs(iota((NX, NX), 0) - iota((NX, NX), 1)) <= RAD, 1.0, 0.0).astype(BF16)


def brick_sums(count, load, out_ref, line, pair, four):
    near = near_columns()
    lanes = line.shape[0]

    def some(step, _):
        totals = []
        for k in range(lanes):
            own, halo = load(step * lanes + k)
            line[k, :RAD] = halo[RAD:]
            line[k, RAD : RAD + NY] = own
            line[k, RAD + NY : EY] = halo[:RAD]
            pair[k, :EY] = line[k, :EY] + line[k, 1 : EY + 1]
            four[k, :EY] = pair[k, :EY] + pair[k, 2 : EY + 2]
            totals.append(four[k, :NY] + four[k, RAD : RAD + NY] + line[k, REACH : REACH + NY])
        parts = [pieces(total, 3) for total in totals]
        sums = jnp.dot(jnp.concatenate([p for part in parts for p in part], 0), near, preferred_element_type=F32)
        for k in range(lanes):
            at = 3 * k * NY
            out_ref[step * lanes + k] = sums[at : at + NY] + sums[at + NY : at + 2 * NY] + sums[at + 2 * NY : at + 3 * NY]
        return 0

    lax.fori_loop(0, count // lanes, some, 0)


LINES = (pltpu.VMEM((4, EY + VY, NX), F32),) * 3


def image_sums_kernel(place_ref, own_sums_ref, out_ref, *lines):
    brick_sums(2 * NZ, lambda i: (own_sums_ref[i], jnp.zeros((VY, NX), F32)), out_ref, *lines)


def halo_sums(fields, outer_sums):
    for f, parts in enumerate(fields):
        for z, total in enumerate(window(parts, NZ)):
            outer_sums[f * NZ + z] = total


def warped_sums_kernel(own_sums_ref, rows_ref, image_rows_ref, out_ref, outer_sums, *lines):
    w = [rows_ref[p] for p in range(EZ)]
    halo_sums([w, [v * v for v in w], [image_rows_ref[p] * v for p, v in enumerate(w)]], outer_sums)
    brick_sums(3 * NZ, lambda i: (own_sums_ref[i], outer_sums[i]), out_ref, *lines)


def halo_part(total):
    row = iota(total.shape, 0) % VY
    size = total.shape[0]
    turned = jnp.where(row < RAD, pltpu.roll(total, size - RAD, 0), pltpu.roll(total, RAD, 0))
    for k in (1, 2):
        up, down = pltpu.roll(turned, size - k, 0), pltpu.roll(turned, k, 0)
        turned = turned + jnp.where(row < RAD - k, up, jnp.where(row >= RAD + k, down, 0.0))
    return turned


def add_edges(x_count, place_ref, z, box, edges, stride, start):
    rows = box[0].shape[0]
    for k in range(x_count):
        right = side_is_right(place_ref, k)
        mask = at_edge(right, rows)
        box = [
            total + edge_part(edges[stride * k + i, start : start + rows, :], z, right, mask)
            for i, total in enumerate(box)
        ]
    return box


def image_box_kernel(x_count, place_ref, sums_ref, image_ref, rows_ref, *refs):
    halos, (out_ref, edges, outer_sums) = refs[:x_count], refs[x_count:]
    for k in range(x_count):
        table = edge_table(side_is_right(place_ref, k))
        f = halos[k][...]
        for i, field in enumerate([f, f * f]):
            edges[2 * k + i] = split_dot(window_rows(field), table)
    f = [rows_ref[p] for p in range(EZ)]
    halo_sums([f, [v * v for v in f]], outer_sums)
    outer = split_dot(halo_part(outer_sums[...].reshape(2 * NZ * VY, NX)), near_columns())
    outer_sums[...] = outer.reshape(2 * NZ, VY, NX)
    first = iota((VY, NX), 0) < RAD
    scale = 1.0 / COUNT

    def plane(z, _):
        box = []
        for f in range(2):
            total, rows = sums_ref[f * NZ + z], outer_sums[f * NZ + z]
            box.append(
                jnp.concatenate(
                    [
                        total[:VY] + jnp.where(first, rows, 0.0),
                        total[VY : NY - VY],
                        total[NY - VY :] + jnp.where(first, 0.0, rows),
                    ],
                    0,
                )
            )
        box = add_edges(x_count, place_ref, z, box, edges, 2, 0)
        mean = box[0] * scale
        out_ref[z] = mean
        out_ref[NZ + z] = image_ref[pl.ds(pl.multiple_of(z * NY, NY), NY), :] - mean
        out_ref[2 * NZ + z] = 1.0 / (box[1] * scale - mean * mean + 1e-5)
        return 0

    lax.fori_loop(0, NZ, plane, 0, unroll=2)


def finish_kernel(y_count, x_count, place_ref, *refs):
    halos, refs = refs[: y_count + x_count], refs[y_count + x_count :]
    sums_ref, image_ref, own_sums_ref, rows_ref, box_ref, out_ref = refs[:6]
    columns, (image_rows, edges, image_outer, outer_sums, *lines) = refs[6 : 6 + x_count], refs[6 + x_count :]
    columns_kernel(y_count, x_count, place_ref, *halos, image_rows, *columns)
    image_box_kernel(x_count, place_ref, sums_ref, image_ref, image_rows, *columns, box_ref, edges, image_outer)
    warped_sums_kernel(own_sums_ref, rows_ref, image_rows, out_ref, outer_sums, *lines)


HALF = NY // 2


def force_kernel(x_count, place_ref, sums_ref, image_ref, own_ref, side_ref, rows_ref, *refs):
    warped_halos, fixed_halos = refs[:x_count], refs[x_count : 2 * x_count]
    force_hbm, edges, force_ref, sems = refs[2 * x_count :]
    for k in range(x_count):
        table = edge_table(side_is_right(place_ref, k))
        w, f = warped_halos[k][...], fixed_halos[k][...]
        for i, field in enumerate([w, w * w, f * w]):
            edges[4 * k + i] = split_dot(window_rows(field), table)
        edges[4 * k + 3] = w[:NY]
    scale = 1.0 / COUNT
    lane = iota((HALF, NX), 1)
    low = place_ref[0] == 0

    def plane(z, _):
        at = pl.multiple_of(z * NY, NY)
        tall = jnp.concatenate([own_ref[pl.ds(at, NY), :], rows_ref[z + RAD]], 0)
        force_ref[1, z] = (pltpu.roll(tall, EY - 1, 0) - pltpu.roll(tall, 1, 0))[:NY]
        above = pl.multiple_of(jnp.minimum(at + NY, (NZ - 1) * NY), NY)
        below = pl.multiple_of(jnp.maximum(at - NY, 0), NY)
        for h in range(0, NY, HALF):
            part = slice(h, h + HALF)
            own = own_ref[pl.ds(at + h, HALF), :]
            box = [sums_ref[f * NZ + z, part, :] for f in range(3)]
            box = add_edges(x_count, place_ref, z, box, edges, 4, h)
            mean_w = box[0] * scale
            cov = box[2] * scale - image_ref[z, part, :] * mean_w
            ratio = cov / (box[1] * scale - mean_w * mean_w + 1e-5)
            half = (ratio * image_ref[2 * NZ + z, part, :]) * (image_ref[NZ + z, part, :] - ratio * (own - mean_w))
            up, down = own_ref[pl.ds(above + h, HALF), :], own_ref[pl.ds(below + h, HALF), :]
            up = jnp.where(z == NZ - 1, jnp.where(low, side_ref[part, :], 0.0), up)
            down = jnp.where(z == 0, jnp.where(low, 0.0, side_ref[(RAD - 1) * NY + h : (RAD - 1) * NY + h + HALF, :]), down)
            force_ref[0, z, part, :] = half * (up - down)
            force_ref[1, z, part, :] = half * force_ref[1, z, part, :]
            after = jnp.where(lane == NX - 1, 0.0, pltpu.roll(own, NX - 1, 1))
            before = jnp.where(lane == 0, 0.0, pltpu.roll(own, 1, 1))
            for k in range(x_count):
                right = side_is_right(place_ref, k)
                turn = jnp.where(right, NX - 1, NX + 1 - RAD) + NX - RAD * (z + RAD)
                halo = pltpu.roll(edges[4 * k + 3, part, :], lax.rem(turn, NX), 1)
                after = jnp.where(lane == jnp.where(right, NX - 1, -1), halo, after)
                before = jnp.where(lane == jnp.where(right, -1, 0), halo, before)
            force_ref[2, z, part, :] = half * (after - before)
        return 0

    def out(group):
        rows = pl.ds(group * RAD, RAD)
        return [pltpu.make_async_copy(force_ref.at[d, rows], force_hbm.at[d, rows], sems.at[d, group]) for d in range(3)]

    for group in range(NZ // RAD):
        lax.fori_loop(group * RAD, (group + 1) * RAD, plane, 0)
        for copy in out(group):
            copy.start()
    for group in range(NZ // RAD):
        for copy in out(group):
            copy.wait()


def pairings(size):
    even = [(i, i ^ 1) for i in range(size) if (i ^ 1) < size]
    odd = [(i, i + 1 if i % 2 else i - 1) for i in range(1, size)]
    odd = [(i, j) for i, j in odd if j < size]
    return [pairs for pairs in (even, odd) if pairs]


def exchange_planes(side):
    return lax.ppermute(side, "gz", pairings(lax.axis_size("gz"))[0])


def rows_to_send(place, face, side, *packed):
    count = len(pairings(lax.axis_size("gy")))
    return call(
        lambda *refs: rows_kernel(len(packed), *refs),
        (array(NZ + RAD + len(packed), RAD, NX),) * count,
        place,
        face,
        side,
        *packed,
    )


def exchange_rows(sent):
    along = pairings(lax.axis_size("gy"))
    return [lax.ppermute(s, "gy", pairs) for s, pairs in reversed(list(zip(sent, along)))][::-1]


def exchange_columns(columns):
    along = pairings(lax.axis_size("gx"))
    return [lax.ppermute(c, "gx", pairs) for c, pairs in zip(columns, along)]


def pack_columns(place, received, packed):
    count = len(packed)
    rows, *columns = call(
        lambda *refs: columns_kernel(len(received), count, *refs),
        (array(EZ, VY, NX),) + (array(EY, NX),) * count,
        place,
        *received,
        *packed,
    )
    return rows, columns


def per_device(fixed, moving, owners, block_ids, counts, mix_yx, mix_z):
    place = jnp.stack([lax.axis_index("gz"), lax.axis_index("gy") % 2, lax.axis_index("gx") % 2]).astype(jnp.int32)
    count = len(pairings(lax.axis_size("gx")))
    request, near, far, flat, (image, image_side, image_face) = ask(place, moving, fixed, owners, block_ids)
    image_side = exchange_planes(image_side)
    image_packed = call(pack_kernel, (array(NY, NX),) * count, place, image, image_side)
    image_packed = exchange_columns(image_packed)
    request, image_packed = lax.optimization_barrier((request, image_packed))
    received = answer(request, near, far)
    image_sent = rows_to_send(place, image_face, image_side, *image_packed)
    image_halos = exchange_rows(image_sent)
    weights = spread_weights(counts, mix_z)
    image_sums, image_planes = call(
        lambda place_ref, own_ref, side_ref, sums_ref, image_ref: own_kernel(
            False, place_ref, own_ref, side_ref, image_ref, sums_ref
        ),
        (array(2 * NZ, NY, NX), array(EZ, NY, NX)),
        place,
        image,
        image_side,
    )
    image_sums = call(image_sums_kernel, array(2 * NZ, NY, NX), place, image_sums, scratch=LINES)
    received, weights, image_sums = lax.optimization_barrier((received, weights, image_sums))
    warped, side, face = mix(flat, place, received, weights, mix_yx.reshape(SLOTS, BV, BV))
    side = exchange_planes(side)
    row_halos = exchange_rows(rows_to_send(place, face, side))
    own_sums, out, *packed = call(
        lambda *refs: own_kernel(True, *refs),
        (array(3 * NZ, NY, NX), array(NZ * NY, NX)) + (array(NY, NX),) * count,
        place,
        warped,
        side,
        image_planes,
        scratch=(pltpu.SemaphoreType.DMA,),
        out_hbm=1,
    )
    rows, columns = pack_columns(place, row_halos, packed)
    columns = exchange_columns(columns)
    image_box, box, *image_columns = call(
        lambda *refs: finish_kernel(len(image_halos), count, *refs),
        (array(3 * NZ, NY, NX), array(3 * NZ, NY, NX)) + (array(EY, NX),) * count,
        place,
        *image_halos,
        *image_packed,
        image_sums,
        image,
        own_sums,
        rows,
        scratch=(
            pltpu.VMEM((EZ, VY, NX), F32),
            pltpu.VMEM((2 * count, NY, NX), F32),
            pltpu.VMEM((2 * NZ, VY, NX), F32),
            pltpu.VMEM((3 * NZ, VY, NX), F32),
        )
        + LINES,
    )
    (force,) = call(
        lambda *refs: force_kernel(count, *refs),
        (array(3, NZ, NY, NX),),
        place,
        box,
        image_box,
        warped,
        side,
        rows,
        *columns,
        *image_columns,
        scratch=(
            pltpu.VMEM((4 * count, NY, NX), F32),
            pltpu.VMEM((3, NZ, NY, NX), F32),
            pltpu.SemaphoreType.DMA((3, NZ // RAD)),
        ),
        out_hbm=0,
    )
    return out.reshape(NZ, NY, NX), force


def solution(mesh):
    return jax.shard_map(
        per_device,
        mesh=mesh,
        in_specs=(
            P("gz", "gy", "gx"),
            P("gz", "gy", "gx"),
            P("gz", "gy", "gx", None, None),
            P("gz", "gy", "gx", None),
            P("gz", "gy", "gx", None),
            P("gz", "gy", "gx", None, None, None),
            P("gz", "gy", "gx", None, None, None),
        ),
        out_specs=(P("gz", "gy", "gx"), P(None, "gz", "gy", "gx")),
        check_vma=False,
    )
```

```python
import jax
import jax.numpy as jnp
from jax import lax
from jax.experimental import pallas as pl
from jax.experimental.pallas import tpu as pltpu
from jax.sharding import PartitionSpec as P


VZ = 8
VY = 8
VX = 16
NBZ = 2
NBY = 8
NBX = 8
SOURCES = 2
RAD = 4
BV = VY * VX
BLOCKS = NBZ * NBY * NBX
SLOTS = BLOCKS * SOURCES
NZ = NBZ * VZ
NY = NBY * VY
NX = NBX * VX
GROUPS = NBZ * NBY
PER = NBX * SOURCES
ROWS = PER * VZ
BRICKS = ("gy", "gx")
F32 = jnp.float32
LIMIT = 12 * 2**20
WIDE = 20 * 2**20
BF16 = jnp.bfloat16

VMEM = pl.BlockSpec(memory_space=pltpu.VMEM)
SMEM = pl.BlockSpec(memory_space=pltpu.SMEM)


OUTER = (
    jax.ShapeDtypeStruct((NZ * NY, NX), F32),
    jax.ShapeDtypeStruct((RAD * NY, NX), F32),
    jax.ShapeDtypeStruct((NZ, VY, NX), F32),
)


def iota(shape, dim):
    return lax.broadcasted_iota(jnp.int32, shape, dim)


def pieces(value, count):
    parts = []
    for _ in range(count - 1):
        part = value.astype(BF16)
        parts.append(part)
        value = value - part.astype(F32)
    parts.append(value.astype(BF16))
    return parts


def swap_chunks(rows):
    chunk = iota((VZ, BV), 1) // VX
    for k in (1, 2, 4):
        low = (chunk & k) == 0
        out = list(rows)
        for b in range(8):
            if b & k == 0:
                first, second = rows[b], rows[b + k]
                out[b] = jnp.where(low, first, pltpu.roll(second, k * VX, 1))
                out[b + k] = jnp.where(low, pltpu.roll(first, BV - k * VX, 1), second)
        rows = out
    return rows


def prepare_kernel(
    half_ref, moving_hbm, owner_hbm, ident_hbm,
    blocks_ref, request_ref, flat_ref,
    moving_ref, owner_ref, ident_ref, wide, sems,
):
    pairs = [(owner_hbm, owner_ref), (ident_hbm, ident_ref), (moving_hbm, moving_ref)]
    copies = [pltpu.make_async_copy(source, target, sems.at[i]) for i, (source, target) in enumerate(pairs)]
    for copy in copies:
        copy.start()
    holders, _, width = request_ref.shape
    capacity = width // 2
    half = half_ref[0]
    copies[0].wait()
    copies[1].wait()
    owner = owner_ref[...]
    ident = ident_ref[...].astype(F32)
    groups = 2 * holders
    named = jnp.where(owner == iota((groups, SLOTS), 0), 1.0, 0.0)
    earlier = jnp.where(iota((SLOTS, SLOTS), 0) < iota((SLOTS, SLOTS), 1), 1.0, 0.0).astype(BF16)
    before = jnp.dot(named.astype(BF16), earlier, preferred_element_type=F32)
    rank = jnp.sum(named * before, axis=0, keepdims=True).astype(jnp.int32)
    upper = jnp.where(owner >= holders, 1, 0)
    holder = owner - upper * holders
    place = jnp.where(upper == half, 0, capacity) + rank
    flat_ref[...] = holder * width + place
    wanted = jnp.where(holder == iota((holders, SLOTS), 0), ident, 0.0).astype(BF16)
    at = jnp.where(place == iota((width, SLOTS), 0), 1.0, 0.0).astype(BF16)
    request = lax.dot_general(wanted, at, (((1,), (1,)), ((), ())), preferred_element_type=F32).astype(jnp.int32)
    for h in range(holders):
        request_ref[h] = request[h : h + 1, :]
    copies[2].wait()
    for z in range(NZ):
        wide[z * NY : (z + 1) * NY, :] = moving_ref[z].astype(F32)

    def group(g, _):
        start = (g // NBY) * (VZ * NY) + (g % NBY) * VY
        rows = [wide[pl.ds(start + y, VZ, stride=NY), :] for y in range(VY)]
        for x, block in enumerate(swap_chunks(rows)):
            blocks_ref[g * NBX + x] = block.astype(BF16)
        return 0

    lax.fori_loop(0, GROUPS, group, 0, unroll=4)


def image_kernel(place_ref, fixed_hbm, image_ref, side_ref, face_ref, fixed_ref, sem):
    copy = pltpu.make_async_copy(fixed_hbm, fixed_ref, sem)
    copy.start()
    copy.wait()
    for z in range(NZ):
        image_ref[z * NY : (z + 1) * NY, :] = fixed_ref[z].astype(F32)
    outer(place_ref, image_ref, side_ref, face_ref)


def widen(place, fixed):
    return pl.pallas_call(
        image_kernel,
        out_shape=OUTER,
        in_specs=[SMEM, pl.BlockSpec(memory_space=pltpu.HBM)],
        out_specs=(VMEM,) * 3,
        scratch_shapes=[pltpu.VMEM((NZ, NY, NX), BF16), pltpu.SemaphoreType.DMA],
        compiler_params=pltpu.CompilerParams(vmem_limit_bytes=LIMIT),
        name="image",
    )(place, pltpu.with_memory_space_constraint(fixed, pltpu.HBM))


def prepare(half, moving, owner, ident, groups, capacity):
    holders = groups // 2
    hbm = pl.BlockSpec(memory_space=pltpu.HBM)
    return pl.pallas_call(
        prepare_kernel,
        out_shape=(
            jax.ShapeDtypeStruct((BLOCKS, VZ, BV), BF16),
            jax.ShapeDtypeStruct((holders, 1, 2 * capacity), jnp.int32),
            jax.ShapeDtypeStruct((1, SLOTS), jnp.int32),
        ),
        in_specs=[SMEM, hbm, hbm, hbm],
        out_specs=(VMEM,) * 3,
        scratch_shapes=[
            pltpu.VMEM((NZ, NY, NX), BF16),
            pltpu.VMEM((1, SLOTS), jnp.int32),
            pltpu.VMEM((1, SLOTS), jnp.int32),
            pltpu.VMEM((NZ * NY, NX), F32),
            pltpu.SemaphoreType.DMA((3,)),
        ],
        compiler_params=pltpu.CompilerParams(vmem_limit_bytes=LIMIT),
        name="prepare",
    )(half, *[pltpu.with_memory_space_constraint(a, pltpu.HBM) for a in (moving, owner, ident)])


def pick_kernel(capacity, request_ref, near_ref, far_ref, out_ref):
    width = 2 * capacity

    for h in range(out_ref.shape[0] // width):
        for k in range(width):
            source = near_ref if k < capacity else far_ref
            out_ref[h * width + k] = source[request_ref[h, 0, k]]


def pick(request, near, far, capacity):
    return pl.pallas_call(
        lambda *refs: pick_kernel(capacity, *refs),
        out_shape=jax.ShapeDtypeStruct((request.size, VZ, BV), BF16),
        in_specs=[SMEM, VMEM, VMEM],
        out_specs=VMEM,
        compiler_params=pltpu.CompilerParams(vmem_limit_bytes=LIMIT),
        name="pick",
    )(request, near, far)


def spread_kernel(mix_ref, out_ref):
    pick_lane = jnp.where(iota((VZ, ROWS), 1) % VZ == iota((VZ, ROWS), 0), 1.0, 0.0).astype(BF16)
    same = iota((ROWS, ROWS), 0) // VZ == iota((ROWS, ROWS), 1) // VZ

    def group(g, _):
        weights = mix_ref[pl.ds(pl.multiple_of(g * ROWS, ROWS), ROWS), :]
        for k, part in enumerate(pieces(weights, 3)):
            tiled = jnp.dot(part, pick_lane, preferred_element_type=F32)
            out_ref[g, k * ROWS : (k + 1) * ROWS, :] = jnp.where(same, tiled, 0.0).astype(BF16)
        return 0

    lax.fori_loop(0, GROUPS, group, 0, unroll=4)


def spread(mix_z):
    return pl.pallas_call(
        spread_kernel,
        out_shape=jax.ShapeDtypeStruct((GROUPS, 3 * ROWS, ROWS), BF16),
        in_specs=[VMEM],
        out_specs=VMEM,
        compiler_params=pltpu.CompilerParams(vmem_limit_bytes=LIMIT),
        name="spread",
    )(mix_z)


STEP = 4


def mix_kernel(
    place_ref, flat_ref, received_ref, spread_ref, mix_hbm, warped_ref, side_ref, face_ref,
    weights_ref, left_ref, blocks_ref, sems,
):
    share = STEP * PER
    steps = GROUPS // STEP

    def weights(step):
        rows = pl.ds(step * share, share)
        return pltpu.make_async_copy(mix_hbm.at[rows], weights_ref.at[rows], sems.at[step])

    for step in range(steps):
        weights(step).start()

    def across_planes(g):
        source = jnp.concatenate([received_ref[flat_ref[g * PER + i]].astype(F32) for i in range(PER)], 0)
        parts = jnp.dot(spread_ref[g], source.astype(BF16), preferred_element_type=F32)
        mixed = parts[:ROWS] + parts[ROWS : 2 * ROWS] + parts[2 * ROWS :]
        high = mixed.astype(BF16).astype(F32)
        low = mixed - high
        for j in range(NBX):
            a = slice(2 * j * VZ, (2 * j + 1) * VZ)
            b = slice((2 * j + 1) * VZ, (2 * j + 2) * VZ)
            left_ref[g * NBX + j] = jnp.concatenate(
                [jnp.concatenate([high[a], high[b]], 1), jnp.concatenate([low[a], low[b]], 1)], 0
            ).astype(BF16)

    def in_plane(g):
        for j in range(NBX):
            right = weights_ref[g * PER + 2 * j : g * PER + 2 * j + 2].reshape(2 * BV, BV)
            both = jnp.dot(left_ref[g * NBX + j], right, preferred_element_type=F32)
            blocks_ref[g * NBX + j] = both[:VZ] + both[VZ:]

    def into_rows(g):
        start = (g // NBY) * (VZ * NY) + (g % NBY) * VY
        for y, row in enumerate(swap_chunks([blocks_ref[g * NBX + j] for j in range(NBX)])):
            warped_ref[pl.ds(start + y, VZ, stride=NY), :] = row

    for step in range(-1, steps + 1):
        if 0 <= step < steps:
            weights(step).wait()
        for q in range(STEP):
            if step + 1 < steps:
                across_planes((step + 1) * STEP + q)
            if 0 <= step < steps:
                in_plane(step * STEP + q)
            if step >= 1:
                into_rows((step - 1) * STEP + q)
    outer(place_ref, warped_ref, side_ref, face_ref)


def outer(place_ref, own_ref, side_ref, face_ref):
    first = jnp.where(place_ref[0] == 0, (NZ - RAD) * NY, 0)
    side_ref[...] = own_ref[pl.ds(pl.multiple_of(first, NY), RAD * NY), :]
    low = iota((VY, NX), 0) < RAD
    for z in range(NZ):
        face_ref[z] = jnp.where(low, own_ref[z * NY : z * NY + VY, :], own_ref[(z + 1) * NY - VY : (z + 1) * NY, :])


def mix(flat, place, received, spread_z, mix_yx):
    return pl.pallas_call(
        mix_kernel,
        out_shape=OUTER,
        in_specs=[SMEM, SMEM, VMEM, VMEM, pl.BlockSpec(memory_space=pltpu.HBM)],
        out_specs=(VMEM,) * 3,
        scratch_shapes=[
            pltpu.VMEM((SLOTS, BV, BV), BF16),
            pltpu.VMEM((BLOCKS, 2 * VZ, 2 * BV), BF16),
            pltpu.VMEM((BLOCKS, VZ, BV), F32),
            pltpu.SemaphoreType.DMA((GROUPS // STEP,)),
        ],
        compiler_params=pltpu.CompilerParams(vmem_limit_bytes=WIDE),
        name="mix",
    )(place, flat, received, spread_z, pltpu.with_memory_space_constraint(mix_yx, pltpu.HBM))


def halves_of_gy():
    groups = lax.axis_size("gy") * lax.axis_size("gx")
    holders = groups // 2
    return groups, max(2, 2 * SLOTS // groups), [list(range(holders)), list(range(holders, groups))]


def exchange_in_half(array):
    _, _, halves = halves_of_gy()
    return lax.all_to_all(array, BRICKS, split_axis=0, concat_axis=0, tiled=True, axis_index_groups=halves)


def ask(moving, owners, block_ids):
    rows_gy = lax.axis_size("gy")
    groups, capacity, _ = halves_of_gy()
    half = (lax.axis_index("gy") >= rows_gy // 2).astype(jnp.int32).reshape(1)
    near, request, flat = prepare(half, moving, owners.reshape(1, SLOTS), block_ids.reshape(1, SLOTS), groups, capacity)
    far = lax.ppermute(near, "gy", [(i, (i + rows_gy // 2) % rows_gy) for i in range(rows_gy)])
    request = exchange_in_half(request)
    return request, near, far, flat.reshape(-1)


def answer(request, near, far):
    groups, capacity, _ = halves_of_gy()
    picked = pick(request, near, far, capacity).reshape(groups // 2, 2 * capacity, VZ, BV)
    received = exchange_in_half(picked)
    return received.reshape(groups * capacity, VZ, BV)


def spread_weights(counts, mix_z):
    slot_pos = jnp.arange(SLOTS, dtype=jnp.int32)
    keep = slot_pos % SOURCES < jnp.repeat(counts.reshape(-1), SOURCES)
    return spread(jnp.where(keep[:, None, None], mix_z.reshape(SLOTS, VZ, VZ), 0.0).reshape(SLOTS * VZ, VZ))


REACH = 2 * RAD
EZ = NZ + REACH
EY = NY + REACH
COUNT = float((REACH + 1) ** 3)


def call(kernel, outs, *args, scratch=(), out_hbm=None):
    specs = jax.tree.map(lambda _: VMEM, outs)
    if out_hbm is not None:
        specs = tuple(pl.BlockSpec(memory_space=pltpu.HBM) if i == out_hbm else VMEM for i in range(len(outs)))
    return pl.pallas_call(
        kernel,
        out_shape=outs,
        in_specs=[SMEM] + [VMEM] * (len(args) - 1),
        out_specs=specs,
        scratch_shapes=scratch,
        compiler_params=pltpu.CompilerParams(vmem_limit_bytes=LIMIT),
    )(*args)


def array(*shape):
    return jax.ShapeDtypeStruct(shape, F32)


def rows_kernel(packed_count, place_ref, face_ref, side_ref, *refs):
    packed, outs = refs[:packed_count], refs[packed_count:]
    even = place_ref[1] == 0
    low = iota((VY, NX), 0) < RAD
    faces = [face_ref[p] for p in range(NZ)]
    for ref, at in [(side_ref, p * NY) for p in range(RAD)] + [(ref, 0) for ref in packed]:
        faces.append(jnp.where(low, ref[at : at + VY, :], ref[at + NY - VY : at + NY, :]))
    for p, face in enumerate(faces):
        outs[0][p] = jnp.where(even, face[RAD:], face[:RAD])
        if len(outs) == 2:
            outs[1][p] = jnp.where(even, face[:RAD], face[RAD:])


def extended_planes(place_ref, own, side):
    low = place_ref[0] == 0
    empty = jnp.zeros_like(side[0])
    before = [jnp.where(low, empty, s) for s in side]
    after = [jnp.where(low, s, empty) for s in side]
    return before + own + after


def pack(place_ref, planes, k):
    even = place_ref[2] == 0
    lift = jnp.where(even, RAD, 0) if k == 0 else jnp.where(even, 0, RAD)
    slot = iota((VY, NX), 1) // RAD
    packed = jnp.zeros((VY, NX), F32)
    for p, rows in enumerate(planes):
        packed = jnp.where(slot == p, pltpu.roll(rows, lift + p * RAD, 1), packed)
    return packed


def window(parts, length):
    two = [parts[i] + parts[i + 1] for i in range(len(parts) - 1)]
    four = [two[i] + two[i + 2] for i in range(len(two) - 2)]
    eight = [four[i] + four[i + 4] for i in range(len(four) - 4)]
    return [eight[i] + parts[i + 8] for i in range(length)]


def pack_kernel(place_ref, own_ref, side_ref, *columns):
    def rows_of(q, _):
        at = pl.multiple_of(q * VY, VY)
        planes = own_planes(place_ref, own_ref, side_ref, at)
        for k, column in enumerate(columns):
            column[pl.ds(at, VY), :] = pack(place_ref, planes, k)
        return 0

    lax.fori_loop(0, NBY, rows_of, 0, unroll=2)


def own_planes(place_ref, own_ref, side_ref, at):
    own = [own_ref[pl.ds(pl.multiple_of(z * NY + at, VY), VY), :] for z in range(NZ)]
    side = [side_ref[pl.ds(pl.multiple_of(z * NY + at, VY), VY), :] for z in range(RAD)]
    return extended_planes(place_ref, own, side)


def own_kernel(with_image, place_ref, own_ref, side_ref, *refs):
    image_ref, sums_ref, *columns = refs
    if with_image:
        out_hbm, sem = columns.pop(0), columns.pop()
        copy = pltpu.make_async_copy(own_ref, out_hbm, sem)
        copy.start()

    def rows_of(q, _):
        at = pl.multiple_of(q * VY, VY)
        rows = pl.ds(at, VY)
        planes = own_planes(place_ref, own_ref, side_ref, at)
        for k, column in enumerate(columns):
            column[rows, :] = pack(place_ref, planes, k)
        fields = [planes, [v * v for v in planes]]
        if with_image:
            fields.append([image_ref[p, rows, :] * v for p, v in enumerate(planes)])
        else:
            for p, v in enumerate(planes):
                image_ref[p, rows, :] = v
        for f, parts in enumerate(fields):
            for z, total in enumerate(window(parts, NZ)):
                sums_ref[f * NZ + z, rows, :] = total
        return 0

    lax.fori_loop(0, NBY, rows_of, 0)
    if with_image:
        copy.wait()


def columns_kernel(y_count, x_count, place_ref, *refs):
    halos, packed, (rows_ref, *columns) = refs[:y_count], refs[y_count : y_count + x_count], refs[y_count + x_count :]
    even = place_ref[1] == 0
    planes = []
    for p in range(halos[0].shape[0]):
        first = halos[0][p]
        second = halos[1][p] if y_count == 2 else jnp.zeros_like(first)
        planes.append(jnp.concatenate([jnp.where(even, first, second), jnp.where(even, second, first)], 0))
    come = planes[NZ + RAD :]
    planes = extended_planes(place_ref, planes[:NZ], planes[NZ : NZ + RAD])
    for p, rows in enumerate(planes):
        rows_ref[p] = rows
    for k in range(x_count):
        columns[k][:NY] = packed[k][...]
        columns[k][NY:] = come[k] if come else pack(place_ref, planes, k)


def window_rows(value):
    two = value + pltpu.roll(value, EY - 1, 0)
    four = two + pltpu.roll(two, EY - 2, 0)
    return (value + pltpu.roll(four, RAD, 0) + pltpu.roll(four, EY - 1, 0))[:NY]


def split_dot(value, table):
    total = None
    for part in pieces(value, 3):
        term = jnp.dot(part, table, preferred_element_type=F32)
        total = term if total is None else total + term
    return total


def edge_table(right):
    row, col = iota((NX, NX), 0), iota((NX, NX), 1)
    plane, i = row // RAD, row % RAD
    z, j = col // RAD, col % RAD
    reach = jnp.where(right, j - i, i - j)
    inside = (plane >= z) & (plane <= z + REACH) & (z < NZ) & (plane < EZ) & (reach >= 0)
    return jnp.where(inside, 1.0, 0.0).astype(BF16)


def at_edge(right, rows):
    return iota((rows, NX), 1) // RAD == jnp.where(right, NX // RAD - 1, 0)


def edge_part(sums, z, right, mask):
    base = jnp.where(right, NX - RAD, 0)
    return jnp.where(mask, pltpu.roll(sums, lax.rem(base + NX - RAD * z, NX), 1), 0.0)


def side_is_right(place_ref, k):
    even = place_ref[2] == 0
    return even if k == 0 else jnp.logical_not(even)


def near_columns():
    return jnp.where(jnp.abs(iota((NX, NX), 0) - iota((NX, NX), 1)) <= RAD, 1.0, 0.0).astype(BF16)


def brick_sums(count, load, out_ref, line, pair, four):
    near = near_columns()
    lanes = line.shape[0]

    def some(step, _):
        totals = []
        for k in range(lanes):
            own, halo = load(step * lanes + k)
            line[k, :RAD] = halo[RAD:]
            line[k, RAD : RAD + NY] = own
            line[k, RAD + NY : EY] = halo[:RAD]
            pair[k, :EY] = line[k, :EY] + line[k, 1 : EY + 1]
            four[k, :EY] = pair[k, :EY] + pair[k, 2 : EY + 2]
            totals.append(four[k, :NY] + four[k, RAD : RAD + NY] + line[k, REACH : REACH + NY])
        parts = [pieces(total, 3) for total in totals]
        sums = jnp.dot(jnp.concatenate([p for part in parts for p in part], 0), near, preferred_element_type=F32)
        for k in range(lanes):
            at = 3 * k * NY
            out_ref[step * lanes + k] = sums[at : at + NY] + sums[at + NY : at + 2 * NY] + sums[at + 2 * NY : at + 3 * NY]
        return 0

    lax.fori_loop(0, count // lanes, some, 0)


LINES = (pltpu.VMEM((4, EY + VY, NX), F32),) * 3


def image_sums_kernel(place_ref, own_sums_ref, out_ref, *lines):
    brick_sums(2 * NZ, lambda i: (own_sums_ref[i], jnp.zeros((VY, NX), F32)), out_ref, *lines)


def halo_sums(fields, outer_sums):
    for f, parts in enumerate(fields):
        for z, total in enumerate(window(parts, NZ)):
            outer_sums[f * NZ + z] = total


def warped_sums_kernel(own_sums_ref, rows_ref, image_rows_ref, out_ref, outer_sums, *lines):
    w = [rows_ref[p] for p in range(EZ)]
    halo_sums([w, [v * v for v in w], [image_rows_ref[p] * v for p, v in enumerate(w)]], outer_sums)
    brick_sums(3 * NZ, lambda i: (own_sums_ref[i], outer_sums[i]), out_ref, *lines)


def halo_part(total):
    row = iota(total.shape, 0) % VY
    size = total.shape[0]
    turned = jnp.where(row < RAD, pltpu.roll(total, size - RAD, 0), pltpu.roll(total, RAD, 0))
    for k in (1, 2):
        up, down = pltpu.roll(turned, size - k, 0), pltpu.roll(turned, k, 0)
        turned = turned + jnp.where(row < RAD - k, up, jnp.where(row >= RAD + k, down, 0.0))
    return turned


def add_edges(x_count, place_ref, z, box, edges, stride, start):
    rows = box[0].shape[0]
    for k in range(x_count):
        right = side_is_right(place_ref, k)
        mask = at_edge(right, rows)
        box = [
            total + edge_part(edges[stride * k + i, start : start + rows, :], z, right, mask)
            for i, total in enumerate(box)
        ]
    return box


def image_box_kernel(x_count, place_ref, sums_ref, image_ref, rows_ref, *refs):
    halos, (out_ref, edges, outer_sums) = refs[:x_count], refs[x_count:]
    for k in range(x_count):
        table = edge_table(side_is_right(place_ref, k))
        f = halos[k][...]
        for i, field in enumerate([f, f * f]):
            edges[2 * k + i] = split_dot(window_rows(field), table)
    f = [rows_ref[p] for p in range(EZ)]
    halo_sums([f, [v * v for v in f]], outer_sums)
    outer = split_dot(halo_part(outer_sums[...].reshape(2 * NZ * VY, NX)), near_columns())
    outer_sums[...] = outer.reshape(2 * NZ, VY, NX)
    first = iota((VY, NX), 0) < RAD
    scale = 1.0 / COUNT

    def plane(z, _):
        box = []
        for f in range(2):
            total, rows = sums_ref[f * NZ + z], outer_sums[f * NZ + z]
            box.append(
                jnp.concatenate(
                    [
                        total[:VY] + jnp.where(first, rows, 0.0),
                        total[VY : NY - VY],
                        total[NY - VY :] + jnp.where(first, 0.0, rows),
                    ],
                    0,
                )
            )
        box = add_edges(x_count, place_ref, z, box, edges, 2, 0)
        mean = box[0] * scale
        out_ref[z] = mean
        out_ref[NZ + z] = image_ref[pl.ds(pl.multiple_of(z * NY, NY), NY), :] - mean
        out_ref[2 * NZ + z] = 1.0 / (box[1] * scale - mean * mean + 1e-5)
        return 0

    lax.fori_loop(0, NZ, plane, 0, unroll=2)


def finish_kernel(y_count, x_count, place_ref, *refs):
    halos, refs = refs[: y_count + x_count], refs[y_count + x_count :]
    sums_ref, image_ref, own_sums_ref, rows_ref, box_ref, out_ref = refs[:6]
    columns, (image_rows, edges, image_outer, outer_sums, *lines) = refs[6 : 6 + x_count], refs[6 + x_count :]
    columns_kernel(y_count, x_count, place_ref, *halos, image_rows, *columns)
    image_box_kernel(x_count, place_ref, sums_ref, image_ref, image_rows, *columns, box_ref, edges, image_outer)
    warped_sums_kernel(own_sums_ref, rows_ref, image_rows, out_ref, outer_sums, *lines)


HALF = NY // 2


def force_kernel(x_count, place_ref, sums_ref, image_ref, own_ref, side_ref, rows_ref, *refs):
    warped_halos, fixed_halos = refs[:x_count], refs[x_count : 2 * x_count]
    force_hbm, edges, force_ref, sems = refs[2 * x_count :]
    for k in range(x_count):
        table = edge_table(side_is_right(place_ref, k))
        w, f = warped_halos[k][...], fixed_halos[k][...]
        for i, field in enumerate([w, w * w, f * w]):
            edges[4 * k + i] = split_dot(window_rows(field), table)
        edges[4 * k + 3] = w[:NY]
    scale = 1.0 / COUNT
    lane = iota((HALF, NX), 1)
    low = place_ref[0] == 0

    def plane(z, _):
        at = pl.multiple_of(z * NY, NY)
        tall = jnp.concatenate([own_ref[pl.ds(at, NY), :], rows_ref[z + RAD]], 0)
        force_ref[1, z] = (pltpu.roll(tall, EY - 1, 0) - pltpu.roll(tall, 1, 0))[:NY]
        above = pl.multiple_of(jnp.minimum(at + NY, (NZ - 1) * NY), NY)
        below = pl.multiple_of(jnp.maximum(at - NY, 0), NY)
        for h in range(0, NY, HALF):
            part = slice(h, h + HALF)
            own = own_ref[pl.ds(at + h, HALF), :]
            box = [sums_ref[f * NZ + z, part, :] for f in range(3)]
            box = add_edges(x_count, place_ref, z, box, edges, 4, h)
            mean_w = box[0] * scale
            cov = box[2] * scale - image_ref[z, part, :] * mean_w
            ratio = cov / (box[1] * scale - mean_w * mean_w + 1e-5)
            half = (ratio * image_ref[2 * NZ + z, part, :]) * (image_ref[NZ + z, part, :] - ratio * (own - mean_w))
            up, down = own_ref[pl.ds(above + h, HALF), :], own_ref[pl.ds(below + h, HALF), :]
            up = jnp.where(z == NZ - 1, jnp.where(low, side_ref[part, :], 0.0), up)
            down = jnp.where(z == 0, jnp.where(low, 0.0, side_ref[(RAD - 1) * NY + h : (RAD - 1) * NY + h + HALF, :]), down)
            force_ref[0, z, part, :] = half * (up - down)
            force_ref[1, z, part, :] = half * force_ref[1, z, part, :]
            after = jnp.where(lane == NX - 1, 0.0, pltpu.roll(own, NX - 1, 1))
            before = jnp.where(lane == 0, 0.0, pltpu.roll(own, 1, 1))
            for k in range(x_count):
                right = side_is_right(place_ref, k)
                turn = jnp.where(right, NX - 1, NX + 1 - RAD) + NX - RAD * (z + RAD)
                halo = pltpu.roll(edges[4 * k + 3, part, :], lax.rem(turn, NX), 1)
                after = jnp.where(lane == jnp.where(right, NX - 1, -1), halo, after)
                before = jnp.where(lane == jnp.where(right, -1, 0), halo, before)
            force_ref[2, z, part, :] = half * (after - before)
        return 0

    def out(group):
        rows = pl.ds(group * RAD, RAD)
        return [pltpu.make_async_copy(force_ref.at[d, rows], force_hbm.at[d, rows], sems.at[d, group]) for d in range(3)]

    for group in range(NZ // RAD):
        lax.fori_loop(group * RAD, (group + 1) * RAD, plane, 0, unroll=2)
        for copy in out(group):
            copy.start()
    for group in range(NZ // RAD):
        for copy in out(group):
            copy.wait()


def pairings(size):
    even = [(i, i ^ 1) for i in range(size) if (i ^ 1) < size]
    odd = [(i, i + 1 if i % 2 else i - 1) for i in range(1, size)]
    odd = [(i, j) for i, j in odd if j < size]
    return [pairs for pairs in (even, odd) if pairs]


def exchange_planes(side):
    return lax.ppermute(side, "gz", pairings(lax.axis_size("gz"))[0])


def rows_to_send(place, face, side, *packed):
    count = len(pairings(lax.axis_size("gy")))
    return call(
        lambda *refs: rows_kernel(len(packed), *refs),
        (array(NZ + RAD + len(packed), RAD, NX),) * count,
        place,
        face,
        side,
        *packed,
    )


def exchange_rows(sent):
    along = pairings(lax.axis_size("gy"))
    return [lax.ppermute(s, "gy", pairs) for s, pairs in reversed(list(zip(sent, along)))][::-1]


def exchange_columns(columns):
    along = pairings(lax.axis_size("gx"))
    return [lax.ppermute(c, "gx", pairs) for c, pairs in zip(columns, along)]


def pack_columns(place, received, packed):
    count = len(packed)
    rows, *columns = call(
        lambda *refs: columns_kernel(len(received), count, *refs),
        (array(EZ, VY, NX),) + (array(EY, NX),) * count,
        place,
        *received,
        *packed,
    )
    return rows, columns


def per_device(fixed, moving, owners, block_ids, counts, mix_yx, mix_z):
    place = jnp.stack([lax.axis_index("gz"), lax.axis_index("gy") % 2, lax.axis_index("gx") % 2]).astype(jnp.int32)
    count = len(pairings(lax.axis_size("gx")))
    request, near, far, flat = ask(moving, owners, block_ids)
    image, image_side, image_face = widen(place, fixed)
    image_side = exchange_planes(image_side)
    image_packed = call(pack_kernel, (array(NY, NX),) * count, place, image, image_side)
    image_packed = exchange_columns(image_packed)
    received = answer(request, near, far)
    image_sent = rows_to_send(place, image_face, image_side, *image_packed)
    image_halos = exchange_rows(image_sent)
    weights = spread_weights(counts, mix_z)
    image_sums, image_planes = call(
        lambda place_ref, own_ref, side_ref, sums_ref, image_ref: own_kernel(
            False, place_ref, own_ref, side_ref, image_ref, sums_ref
        ),
        (array(2 * NZ, NY, NX), array(EZ, NY, NX)),
        place,
        image,
        image_side,
    )
    image_sums = call(image_sums_kernel, array(2 * NZ, NY, NX), place, image_sums, scratch=LINES)
    received, weights, image_sums = lax.optimization_barrier((received, weights, image_sums))
    warped, side, face = mix(flat, place, received, weights, mix_yx.reshape(SLOTS, BV, BV))
    side = exchange_planes(side)
    row_halos = exchange_rows(rows_to_send(place, face, side))
    own_sums, out, *packed = call(
        lambda *refs: own_kernel(True, *refs),
        (array(3 * NZ, NY, NX), array(NZ * NY, NX)) + (array(NY, NX),) * count,
        place,
        warped,
        side,
        image_planes,
        scratch=(pltpu.SemaphoreType.DMA,),
        out_hbm=1,
    )
    rows, columns = pack_columns(place, row_halos, packed)
    columns = exchange_columns(columns)
    image_box, box, *image_columns = call(
        lambda *refs: finish_kernel(len(image_halos), count, *refs),
        (array(3 * NZ, NY, NX), array(3 * NZ, NY, NX)) + (array(EY, NX),) * count,
        place,
        *image_halos,
        *image_packed,
        image_sums,
        image,
        own_sums,
        rows,
        scratch=(
            pltpu.VMEM((EZ, VY, NX), F32),
            pltpu.VMEM((2 * count, NY, NX), F32),
            pltpu.VMEM((2 * NZ, VY, NX), F32),
            pltpu.VMEM((3 * NZ, VY, NX), F32),
        )
        + LINES,
    )
    (force,) = call(
        lambda *refs: force_kernel(count, *refs),
        (array(3, NZ, NY, NX),),
        place,
        box,
        image_box,
        warped,
        side,
        rows,
        *columns,
        *image_columns,
        scratch=(
            pltpu.VMEM((4 * count, NY, NX), F32),
            pltpu.VMEM((3, NZ, NY, NX), F32),
            pltpu.SemaphoreType.DMA((3, NZ // RAD)),
        ),
        out_hbm=0,
    )
    return out.reshape(NZ, NY, NX), force


def solution(mesh):
    return jax.shard_map(
        per_device,
        mesh=mesh,
        in_specs=(
            P("gz", "gy", "gx"),
            P("gz", "gy", "gx"),
            P("gz", "gy", "gx", None, None),
            P("gz", "gy", "gx", None),
            P("gz", "gy", "gx", None),
            P("gz", "gy", "gx", None, None, None),
            P("gz", "gy", "gx", None, None, None),
        ),
        out_specs=(P("gz", "gy", "gx"), P(None, "gz", "gy", "gx")),
        check_vma=False,
    )
```

```python
import jax
import jax.numpy as jnp
from jax import lax
from jax.experimental import pallas as pl
from jax.experimental.pallas import tpu as pltpu
from jax.sharding import PartitionSpec as P


VZ = 8
VY = 8
VX = 16
NBZ = 2
NBY = 8
NBX = 8
SOURCES = 2
RAD = 4
BV = VY * VX
BLOCKS = NBZ * NBY * NBX
SLOTS = BLOCKS * SOURCES
NZ = NBZ * VZ
NY = NBY * VY
NX = NBX * VX
GROUPS = NBZ * NBY
PER = NBX * SOURCES
ROWS = PER * VZ
BRICKS = ("gy", "gx")
F32 = jnp.float32
LIMIT = 12 * 2**20
WIDE = 20 * 2**20
BF16 = jnp.bfloat16

VMEM = pl.BlockSpec(memory_space=pltpu.VMEM)
SMEM = pl.BlockSpec(memory_space=pltpu.SMEM)


OUTER = (
    jax.ShapeDtypeStruct((NZ * NY, NX), F32),
    jax.ShapeDtypeStruct((RAD * NY, NX), F32),
    jax.ShapeDtypeStruct((NZ, VY, NX), F32),
)


def iota(shape, dim):
    return lax.broadcasted_iota(jnp.int32, shape, dim)


def pieces(value, count):
    parts = []
    for _ in range(count - 1):
        part = value.astype(BF16)
        parts.append(part)
        value = value - part.astype(F32)
    parts.append(value.astype(BF16))
    return parts


def swap_chunks(rows):
    chunk = iota((VZ, BV), 1) // VX
    for k in (1, 2, 4):
        low = (chunk & k) == 0
        out = list(rows)
        for b in range(8):
            if b & k == 0:
                first, second = rows[b], rows[b + k]
                out[b] = jnp.where(low, first, pltpu.roll(second, k * VX, 1))
                out[b + k] = jnp.where(low, pltpu.roll(first, BV - k * VX, 1), second)
        rows = out
    return rows


def prepare_kernel(
    half_ref, moving_hbm, owner_hbm, ident_hbm,
    blocks_ref, request_ref, flat_ref,
    moving_ref, owner_ref, ident_ref, wide, sems,
):
    pairs = [(owner_hbm, owner_ref), (ident_hbm, ident_ref), (moving_hbm, moving_ref)]
    copies = [pltpu.make_async_copy(source, target, sems.at[i]) for i, (source, target) in enumerate(pairs)]
    for copy in copies:
        copy.start()
    holders, _, width = request_ref.shape
    capacity = width // 2
    half = half_ref[0]
    copies[0].wait()
    copies[1].wait()
    owner = owner_ref[...]
    ident = ident_ref[...].astype(F32)
    groups = 2 * holders
    named = jnp.where(owner == iota((groups, SLOTS), 0), 1.0, 0.0)
    earlier = jnp.where(iota((SLOTS, SLOTS), 0) < iota((SLOTS, SLOTS), 1), 1.0, 0.0).astype(BF16)
    before = jnp.dot(named.astype(BF16), earlier, preferred_element_type=F32)
    rank = jnp.sum(named * before, axis=0, keepdims=True).astype(jnp.int32)
    upper = jnp.where(owner >= holders, 1, 0)
    holder = owner - upper * holders
    place = jnp.where(upper == half, 0, capacity) + rank
    flat_ref[...] = holder * width + place
    wanted = jnp.where(holder == iota((holders, SLOTS), 0), ident, 0.0).astype(BF16)
    at = jnp.where(place == iota((width, SLOTS), 0), 1.0, 0.0).astype(BF16)
    request = lax.dot_general(wanted, at, (((1,), (1,)), ((), ())), preferred_element_type=F32).astype(jnp.int32)
    for h in range(holders):
        request_ref[h] = request[h : h + 1, :]
    copies[2].wait()
    for z in range(NZ):
        wide[z * NY : (z + 1) * NY, :] = moving_ref[z].astype(F32)

    def group(g, _):
        start = (g // NBY) * (VZ * NY) + (g % NBY) * VY
        rows = [wide[pl.ds(start + y, VZ, stride=NY), :] for y in range(VY)]
        for x, block in enumerate(swap_chunks(rows)):
            blocks_ref[g * NBX + x] = block.astype(BF16)
        return 0

    lax.fori_loop(0, GROUPS, group, 0, unroll=4)


def image_kernel(place_ref, fixed_hbm, image_ref, side_ref, face_ref, fixed_ref, sem):
    copy = pltpu.make_async_copy(fixed_hbm, fixed_ref, sem)
    copy.start()
    copy.wait()
    for z in range(NZ):
        image_ref[z * NY : (z + 1) * NY, :] = fixed_ref[z].astype(F32)
    outer(place_ref, image_ref, side_ref, face_ref)


def widen(place, fixed):
    return pl.pallas_call(
        image_kernel,
        out_shape=OUTER,
        in_specs=[SMEM, pl.BlockSpec(memory_space=pltpu.HBM)],
        out_specs=(VMEM,) * 3,
        scratch_shapes=[pltpu.VMEM((NZ, NY, NX), BF16), pltpu.SemaphoreType.DMA],
        compiler_params=pltpu.CompilerParams(vmem_limit_bytes=LIMIT),
        name="image",
    )(place, pltpu.with_memory_space_constraint(fixed, pltpu.HBM))


def prepare(half, moving, owner, ident, groups, capacity):
    holders = groups // 2
    hbm = pl.BlockSpec(memory_space=pltpu.HBM)
    return pl.pallas_call(
        prepare_kernel,
        out_shape=(
            jax.ShapeDtypeStruct((BLOCKS, VZ, BV), BF16),
            jax.ShapeDtypeStruct((holders, 1, 2 * capacity), jnp.int32),
            jax.ShapeDtypeStruct((1, SLOTS), jnp.int32),
        ),
        in_specs=[SMEM, hbm, hbm, hbm],
        out_specs=(VMEM,) * 3,
        scratch_shapes=[
            pltpu.VMEM((NZ, NY, NX), BF16),
            pltpu.VMEM((1, SLOTS), jnp.int32),
            pltpu.VMEM((1, SLOTS), jnp.int32),
            pltpu.VMEM((NZ * NY, NX), F32),
            pltpu.SemaphoreType.DMA((3,)),
        ],
        compiler_params=pltpu.CompilerParams(vmem_limit_bytes=LIMIT),
        name="prepare",
    )(half, *[pltpu.with_memory_space_constraint(a, pltpu.HBM) for a in (moving, owner, ident)])


def pick_kernel(capacity, request_ref, near_ref, far_ref, out_ref):
    width = 2 * capacity

    for h in range(out_ref.shape[0] // width):
        for k in range(width):
            source = near_ref if k < capacity else far_ref
            out_ref[h * width + k] = source[request_ref[h, 0, k]]


def pick(request, near, far, capacity):
    return pl.pallas_call(
        lambda *refs: pick_kernel(capacity, *refs),
        out_shape=jax.ShapeDtypeStruct((request.size, VZ, BV), BF16),
        in_specs=[SMEM, VMEM, VMEM],
        out_specs=VMEM,
        compiler_params=pltpu.CompilerParams(vmem_limit_bytes=LIMIT),
        name="pick",
    )(request, near, far)


def spread_kernel(mix_ref, out_ref):
    pick_lane = jnp.where(iota((VZ, ROWS), 1) % VZ == iota((VZ, ROWS), 0), 1.0, 0.0).astype(BF16)
    same = iota((ROWS, ROWS), 0) // VZ == iota((ROWS, ROWS), 1) // VZ

    def group(g, _):
        weights = mix_ref[pl.ds(pl.multiple_of(g * ROWS, ROWS), ROWS), :]
        for k, part in enumerate(pieces(weights, 3)):
            tiled = jnp.dot(part, pick_lane, preferred_element_type=F32)
            out_ref[g, k * ROWS : (k + 1) * ROWS, :] = jnp.where(same, tiled, 0.0).astype(BF16)
        return 0

    lax.fori_loop(0, GROUPS, group, 0, unroll=4)


def spread(mix_z):
    return pl.pallas_call(
        spread_kernel,
        out_shape=jax.ShapeDtypeStruct((GROUPS, 3 * ROWS, ROWS), BF16),
        in_specs=[VMEM],
        out_specs=VMEM,
        compiler_params=pltpu.CompilerParams(vmem_limit_bytes=LIMIT),
        name="spread",
    )(mix_z)


STEP = 4


def mix_kernel(
    place_ref, flat_ref, received_ref, spread_ref, mix_hbm, warped_ref, side_ref, face_ref,
    weights_ref, left_ref, blocks_ref, sems,
):
    share = STEP * PER
    steps = GROUPS // STEP

    def weights(step):
        rows = pl.ds(step * share, share)
        return pltpu.make_async_copy(mix_hbm.at[rows], weights_ref.at[rows], sems.at[step])

    for step in range(steps):
        weights(step).start()

    def across_planes(g):
        source = jnp.concatenate([received_ref[flat_ref[g * PER + i]].astype(F32) for i in range(PER)], 0)
        parts = jnp.dot(spread_ref[g], source.astype(BF16), preferred_element_type=F32)
        mixed = parts[:ROWS] + parts[ROWS : 2 * ROWS] + parts[2 * ROWS :]
        high = mixed.astype(BF16).astype(F32)
        low = mixed - high
        for j in range(NBX):
            a = slice(2 * j * VZ, (2 * j + 1) * VZ)
            b = slice((2 * j + 1) * VZ, (2 * j + 2) * VZ)
            left_ref[g * NBX + j] = jnp.concatenate(
                [jnp.concatenate([high[a], high[b]], 1), jnp.concatenate([low[a], low[b]], 1)], 0
            ).astype(BF16)

    def in_plane(g):
        for j in range(NBX):
            right = weights_ref[g * PER + 2 * j : g * PER + 2 * j + 2].reshape(2 * BV, BV)
            both = jnp.dot(left_ref[g * NBX + j], right, preferred_element_type=F32)
            blocks_ref[g * NBX + j] = both[:VZ] + both[VZ:]

    def into_rows(g):
        start = (g // NBY) * (VZ * NY) + (g % NBY) * VY
        for y, row in enumerate(swap_chunks([blocks_ref[g * NBX + j] for j in range(NBX)])):
            warped_ref[pl.ds(start + y, VZ, stride=NY), :] = row

    for step in range(-1, steps + 1):
        if 0 <= step < steps:
            weights(step).wait()
        for q in range(STEP):
            if step + 1 < steps:
                across_planes((step + 1) * STEP + q)
            if 0 <= step < steps:
                in_plane(step * STEP + q)
            if step >= 1:
                into_rows((step - 1) * STEP + q)
    outer(place_ref, warped_ref, side_ref, face_ref)


def outer(place_ref, own_ref, side_ref, face_ref):
    first = jnp.where(place_ref[0] == 0, (NZ - RAD) * NY, 0)
    side_ref[...] = own_ref[pl.ds(pl.multiple_of(first, NY), RAD * NY), :]
    low = iota((VY, NX), 0) < RAD
    for z in range(NZ):
        face_ref[z] = jnp.where(low, own_ref[z * NY : z * NY + VY, :], own_ref[(z + 1) * NY - VY : (z + 1) * NY, :])


def mix(flat, place, received, spread_z, mix_yx):
    return pl.pallas_call(
        mix_kernel,
        out_shape=OUTER,
        in_specs=[SMEM, SMEM, VMEM, VMEM, pl.BlockSpec(memory_space=pltpu.HBM)],
        out_specs=(VMEM,) * 3,
        scratch_shapes=[
            pltpu.VMEM((SLOTS, BV, BV), BF16),
            pltpu.VMEM((BLOCKS, 2 * VZ, 2 * BV), BF16),
            pltpu.VMEM((BLOCKS, VZ, BV), F32),
            pltpu.SemaphoreType.DMA((GROUPS // STEP,)),
        ],
        compiler_params=pltpu.CompilerParams(vmem_limit_bytes=WIDE),
        name="mix",
    )(place, flat, received, spread_z, pltpu.with_memory_space_constraint(mix_yx, pltpu.HBM))


def halves_of_gy():
    groups = lax.axis_size("gy") * lax.axis_size("gx")
    holders = groups // 2
    return groups, max(2, 2 * SLOTS // groups), [list(range(holders)), list(range(holders, groups))]


def exchange_in_half(array):
    _, _, halves = halves_of_gy()
    return lax.all_to_all(array, BRICKS, split_axis=0, concat_axis=0, tiled=True, axis_index_groups=halves)


def ask(moving, owners, block_ids):
    rows_gy = lax.axis_size("gy")
    groups, capacity, _ = halves_of_gy()
    half = (lax.axis_index("gy") >= rows_gy // 2).astype(jnp.int32).reshape(1)
    near, request, flat = prepare(half, moving, owners.reshape(1, SLOTS), block_ids.reshape(1, SLOTS), groups, capacity)
    far = lax.ppermute(near, "gy", [(i, (i + rows_gy // 2) % rows_gy) for i in range(rows_gy)])
    request = exchange_in_half(request)
    return request, near, far, flat.reshape(-1)


def answer(request, near, far):
    groups, capacity, _ = halves_of_gy()
    picked = pick(request, near, far, capacity).reshape(groups // 2, 2 * capacity, VZ, BV)
    received = exchange_in_half(picked)
    return received.reshape(groups * capacity, VZ, BV)


def spread_weights(counts, mix_z):
    slot_pos = jnp.arange(SLOTS, dtype=jnp.int32)
    keep = slot_pos % SOURCES < jnp.repeat(counts.reshape(-1), SOURCES)
    return spread(jnp.where(keep[:, None, None], mix_z.reshape(SLOTS, VZ, VZ), 0.0).reshape(SLOTS * VZ, VZ))


REACH = 2 * RAD
EZ = NZ + REACH
EY = NY + REACH
COUNT = float((REACH + 1) ** 3)


def call(kernel, outs, *args, scratch=(), out_hbm=None):
    specs = jax.tree.map(lambda _: VMEM, outs)
    if out_hbm is not None:
        specs = tuple(pl.BlockSpec(memory_space=pltpu.HBM) if i == out_hbm else VMEM for i in range(len(outs)))
    return pl.pallas_call(
        kernel,
        out_shape=outs,
        in_specs=[SMEM] + [VMEM] * (len(args) - 1),
        out_specs=specs,
        scratch_shapes=scratch,
        compiler_params=pltpu.CompilerParams(vmem_limit_bytes=LIMIT),
    )(*args)


def array(*shape):
    return jax.ShapeDtypeStruct(shape, F32)


def rows_kernel(packed_count, place_ref, face_ref, side_ref, *refs):
    packed, outs = refs[:packed_count], refs[packed_count:]
    even = place_ref[1] == 0
    low = iota((VY, NX), 0) < RAD
    faces = [face_ref[p] for p in range(NZ)]
    for ref, at in [(side_ref, p * NY) for p in range(RAD)] + [(ref, 0) for ref in packed]:
        faces.append(jnp.where(low, ref[at : at + VY, :], ref[at + NY - VY : at + NY, :]))
    for p, face in enumerate(faces):
        outs[0][p] = jnp.where(even, face[RAD:], face[:RAD])
        if len(outs) == 2:
            outs[1][p] = jnp.where(even, face[:RAD], face[RAD:])


def extended_planes(place_ref, own, side):
    low = place_ref[0] == 0
    empty = jnp.zeros_like(side[0])
    before = [jnp.where(low, empty, s) for s in side]
    after = [jnp.where(low, s, empty) for s in side]
    return before + own + after


def pack(place_ref, planes, k):
    even = place_ref[2] == 0
    lift = jnp.where(even, RAD, 0) if k == 0 else jnp.where(even, 0, RAD)
    slot = iota((VY, NX), 1) // RAD
    packed = jnp.zeros((VY, NX), F32)
    for p, rows in enumerate(planes):
        packed = jnp.where(slot == p, pltpu.roll(rows, lift + p * RAD, 1), packed)
    return packed


def window(parts, length):
    two = [parts[i] + parts[i + 1] for i in range(len(parts) - 1)]
    four = [two[i] + two[i + 2] for i in range(len(two) - 2)]
    eight = [four[i] + four[i + 4] for i in range(len(four) - 4)]
    return [eight[i] + parts[i + 8] for i in range(length)]


def pack_kernel(place_ref, own_ref, side_ref, *columns):
    def rows_of(q, _):
        at = pl.multiple_of(q * VY, VY)
        planes = own_planes(place_ref, own_ref, side_ref, at)
        for k, column in enumerate(columns):
            column[pl.ds(at, VY), :] = pack(place_ref, planes, k)
        return 0

    lax.fori_loop(0, NBY, rows_of, 0, unroll=2)


def own_planes(place_ref, own_ref, side_ref, at):
    own = [own_ref[pl.ds(pl.multiple_of(z * NY + at, VY), VY), :] for z in range(NZ)]
    side = [side_ref[pl.ds(pl.multiple_of(z * NY + at, VY), VY), :] for z in range(RAD)]
    return extended_planes(place_ref, own, side)


def plane_sums(place_ref, refs, fields_of, sums_ref, columns=()):
    def rows_of(q, _):
        at = pl.multiple_of(q * VY, VY)
        rows = pl.ds(at, VY)
        planes = [own_planes(place_ref, own_ref, side_ref, at) for own_ref, side_ref in refs]
        for k, column in enumerate(columns):
            column[rows, :] = pack(place_ref, planes[0], k)
        for f, parts in enumerate(fields_of(*planes)):
            for z, total in enumerate(window(parts, NZ)):
                sums_ref[f * NZ + z, rows, :] = total
        return 0

    lax.fori_loop(0, NBY, rows_of, 0)


def own_kernel(place_ref, own_ref, side_ref, image_ref, image_side_ref, sums_ref, out_hbm, *rest):
    columns, sem = rest[:-1], rest[-1]
    copy = pltpu.make_async_copy(own_ref, out_hbm, sem)
    copy.start()
    plane_sums(
        place_ref,
        [(own_ref, side_ref), (image_ref, image_side_ref)],
        lambda w, f: [w, [v * v for v in w], [u * v for u, v in zip(f, w)]],
        sums_ref,
        columns,
    )
    copy.wait()


def columns_kernel(y_count, x_count, place_ref, *refs):
    halos, packed, (rows_ref, *columns) = refs[:y_count], refs[y_count : y_count + x_count], refs[y_count + x_count :]
    even = place_ref[1] == 0
    planes = []
    for p in range(halos[0].shape[0]):
        first = halos[0][p]
        second = halos[1][p] if y_count == 2 else jnp.zeros_like(first)
        planes.append(jnp.concatenate([jnp.where(even, first, second), jnp.where(even, second, first)], 0))
    come = planes[NZ + RAD :]
    planes = extended_planes(place_ref, planes[:NZ], planes[NZ : NZ + RAD])
    for p, rows in enumerate(planes):
        rows_ref[p] = rows
    for k in range(x_count):
        columns[k][:NY] = packed[k][...]
        columns[k][NY:] = come[k] if come else pack(place_ref, planes, k)


def window_rows(value):
    two = value + pltpu.roll(value, EY - 1, 0)
    four = two + pltpu.roll(two, EY - 2, 0)
    return (value + pltpu.roll(four, RAD, 0) + pltpu.roll(four, EY - 1, 0))[:NY]


def split_dot(value, table):
    total = None
    for part in pieces(value, 3):
        term = jnp.dot(part, table, preferred_element_type=F32)
        total = term if total is None else total + term
    return total


def edge_table(right):
    row, col = iota((NX, NX), 0), iota((NX, NX), 1)
    plane, i = row // RAD, row % RAD
    z, j = col // RAD, col % RAD
    reach = jnp.where(right, j - i, i - j)
    inside = (plane >= z) & (plane <= z + REACH) & (z < NZ) & (plane < EZ) & (reach >= 0)
    return jnp.where(inside, 1.0, 0.0).astype(BF16)


def at_edge(right, rows):
    return iota((rows, NX), 1) // RAD == jnp.where(right, NX // RAD - 1, 0)


def edge_part(sums, z, right, mask):
    base = jnp.where(right, NX - RAD, 0)
    return jnp.where(mask, pltpu.roll(sums, lax.rem(base + NX - RAD * z, NX), 1), 0.0)


def side_is_right(place_ref, k):
    even = place_ref[2] == 0
    return even if k == 0 else jnp.logical_not(even)


def near_columns():
    return jnp.where(jnp.abs(iota((NX, NX), 0) - iota((NX, NX), 1)) <= RAD, 1.0, 0.0).astype(BF16)


def brick_sums(count, load, out_ref, line, pair, four):
    near = near_columns()
    lanes = line.shape[0]

    def some(step, _):
        totals = []
        for k in range(lanes):
            own, halo = load(step * lanes + k)
            line[k, :RAD] = halo[RAD:]
            line[k, RAD : RAD + NY] = own
            line[k, RAD + NY : EY] = halo[:RAD]
            pair[k, :EY] = line[k, :EY] + line[k, 1 : EY + 1]
            four[k, :EY] = pair[k, :EY] + pair[k, 2 : EY + 2]
            totals.append(four[k, :NY] + four[k, RAD : RAD + NY] + line[k, REACH : REACH + NY])
        parts = [pieces(total, 3) for total in totals]
        sums = jnp.dot(jnp.concatenate([p for part in parts for p in part], 0), near, preferred_element_type=F32)
        for k in range(lanes):
            at = 3 * k * NY
            out_ref[step * lanes + k] = sums[at : at + NY] + sums[at + NY : at + 2 * NY] + sums[at + 2 * NY : at + 3 * NY]
        return 0

    lax.fori_loop(0, count // lanes, some, 0)


LINES = (pltpu.VMEM((4, EY + VY, NX), F32),) * 3


def halo_sums(fields, outer_sums):
    for f, parts in enumerate(fields):
        for z, total in enumerate(window(parts, NZ)):
            outer_sums[f * NZ + z] = total


def warped_sums_kernel(own_sums_ref, rows_ref, image_rows_ref, out_ref, outer_sums, *lines):
    w = [rows_ref[p] for p in range(EZ)]
    halo_sums([w, [v * v for v in w], [image_rows_ref[p] * v for p, v in enumerate(w)]], outer_sums)
    brick_sums(3 * NZ, lambda i: (own_sums_ref[i], outer_sums[i]), out_ref, *lines)


def halo_part(total):
    row = iota(total.shape, 0) % VY
    size = total.shape[0]
    turned = jnp.where(row < RAD, pltpu.roll(total, size - RAD, 0), pltpu.roll(total, RAD, 0))
    for k in (1, 2):
        up, down = pltpu.roll(turned, size - k, 0), pltpu.roll(turned, k, 0)
        turned = turned + jnp.where(row < RAD - k, up, jnp.where(row >= RAD + k, down, 0.0))
    return turned


def add_edges(x_count, place_ref, z, box, edges, stride, start):
    rows = box[0].shape[0]
    for k in range(x_count):
        right = side_is_right(place_ref, k)
        mask = at_edge(right, rows)
        box = [
            total + edge_part(edges[stride * k + i, start : start + rows, :], z, right, mask)
            for i, total in enumerate(box)
        ]
    return box


def image_values(out_ref, z, box, image):
    mean = box[0] * (1.0 / COUNT)
    out_ref[z] = mean
    out_ref[NZ + z] = image - mean
    out_ref[2 * NZ + z] = 1.0 / (box[1] * (1.0 / COUNT) - mean * mean + 1e-5)


def image_early_kernel(x_count, place_ref, image_ref, side_ref, *refs):
    packed, (out_ref, outer_ref, planes, sums_ref, edges, *lines) = refs[:x_count], refs[x_count:]
    plane_sums(place_ref, [(image_ref, side_ref)], lambda f: [f, [v * v for v in f]], planes)
    brick_sums(2 * NZ, lambda i: (planes[i], jnp.zeros((VY, NX), F32)), sums_ref, *lines)
    for k in range(x_count):
        table = edge_table(side_is_right(place_ref, k))
        f = jnp.concatenate([packed[k][...], jnp.zeros((VY, NX), F32)], 0)
        for i, field in enumerate([f, f * f]):
            edges[2 * k + i] = split_dot(window_rows(field), table)

    def plane(z, _):
        box = [sums_ref[z], sums_ref[NZ + z]]
        for f in range(2):
            outer_ref[f * NZ + z] = outer_rows(box[f][:VY], box[f][NY - VY :])
        box = add_edges(x_count, place_ref, z, box, edges, 2, 0)
        image_values(out_ref, z, box, image_ref[pl.ds(pl.multiple_of(z * NY, NY), NY), :])
        return 0

    lax.fori_loop(0, NZ, plane, 0, unroll=2)


def outer_rows(first, last):
    return jnp.concatenate([first, last], 0)


def image_late_kernel(x_count, place_ref, sums_ref, image_ref, rows_ref, *refs):
    halos, (out_ref, edges, outer_sums) = refs[:x_count], refs[x_count:]
    for k in range(x_count):
        table = edge_table(side_is_right(place_ref, k))
        f = halos[k][...]
        for i, field in enumerate([f, f * f]):
            rows = window_rows(field)
            edges[2 * k + i] = split_dot(outer_rows(rows[:VY], rows[NY - VY :]), table)
    f = [rows_ref[p] for p in range(EZ)]
    halo_sums([f, [v * v for v in f]], outer_sums)
    outer = split_dot(halo_part(outer_sums[...].reshape(2 * NZ * VY, NX)), near_columns())
    outer_sums[...] = outer.reshape(2 * NZ, VY, NX)
    first = iota((VY, NX), 0) < RAD

    def plane(z, _):
        box = []
        for f in range(2):
            rows = outer_sums[f * NZ + z]
            before = sums_ref[f * NZ + z, :VY, :] + jnp.where(first, rows, 0.0)
            box.append(outer_rows(before, sums_ref[f * NZ + z, VY:, :] + jnp.where(first, 0.0, rows)))
        box = add_edges(x_count, place_ref, z, box, edges, 2, 0)
        at = pl.multiple_of(z * NY, NY)
        image_values(out_ref, z, box, outer_rows(image_ref[pl.ds(at, VY), :], image_ref[pl.ds(at + NY - VY, VY), :]))
        return 0

    lax.fori_loop(0, NZ, plane, 0, unroll=4)


def finish_kernel(y_count, x_count, place_ref, *refs):
    halos, refs = refs[: y_count + x_count], refs[y_count + x_count :]
    sums_ref, image_ref, own_sums_ref, rows_ref, box_ref, out_ref = refs[:6]
    columns, (image_rows, edges, image_outer, outer_sums, *lines) = refs[6 : 6 + x_count], refs[6 + x_count :]
    columns_kernel(y_count, x_count, place_ref, *halos, image_rows, *columns)
    image_late_kernel(x_count, place_ref, sums_ref, image_ref, image_rows, *columns, box_ref, edges, image_outer)
    warped_sums_kernel(own_sums_ref, rows_ref, image_rows, out_ref, outer_sums, *lines)


HALF = NY // 2


def force_kernel(x_count, place_ref, sums_ref, image_ref, patch_ref, own_ref, side_ref, rows_ref, *refs):
    warped_halos, fixed_halos = refs[:x_count], refs[x_count : 2 * x_count]
    force_hbm, edges, force_ref, sems = refs[2 * x_count :]
    for k in range(x_count):
        table = edge_table(side_is_right(place_ref, k))
        w, f = warped_halos[k][...], fixed_halos[k][...]
        for i, field in enumerate([w, w * w, f * w]):
            edges[4 * k + i] = split_dot(window_rows(field), table)
        edges[4 * k + 3] = w[:NY]
    scale = 1.0 / COUNT
    lane = iota((HALF, NX), 1)
    low = place_ref[0] == 0

    def plane(z, _):
        at = pl.multiple_of(z * NY, NY)
        tall = jnp.concatenate([own_ref[pl.ds(at, NY), :], rows_ref[z + RAD]], 0)
        force_ref[1, z] = (pltpu.roll(tall, EY - 1, 0) - pltpu.roll(tall, 1, 0))[:NY]
        above = pl.multiple_of(jnp.minimum(at + NY, (NZ - 1) * NY), NY)
        below = pl.multiple_of(jnp.maximum(at - NY, 0), NY)
        for h in range(0, NY, HALF):
            part = slice(h, h + HALF)
            own = own_ref[pl.ds(at + h, HALF), :]
            box = [sums_ref[f * NZ + z, part, :] for f in range(3)]
            box = add_edges(x_count, place_ref, z, box, edges, 4, h)
            mean_f, image, inverse_f = [
                jnp.concatenate([patch_ref[f * NZ + z, :VY, :], image_ref[f * NZ + z, VY:HALF, :]], 0)
                if h == 0
                else jnp.concatenate([image_ref[f * NZ + z, HALF : NY - VY, :], patch_ref[f * NZ + z, VY:, :]], 0)
                for f in range(3)
            ]
            mean_w = box[0] * scale
            cov = box[2] * scale - mean_f * mean_w
            ratio = cov / (box[1] * scale - mean_w * mean_w + 1e-5)
            half = (ratio * inverse_f) * (image - ratio * (own - mean_w))
            up, down = own_ref[pl.ds(above + h, HALF), :], own_ref[pl.ds(below + h, HALF), :]
            up = jnp.where(z == NZ - 1, jnp.where(low, side_ref[part, :], 0.0), up)
            down = jnp.where(z == 0, jnp.where(low, 0.0, side_ref[(RAD - 1) * NY + h : (RAD - 1) * NY + h + HALF, :]), down)
            force_ref[0, z, part, :] = half * (up - down)
            force_ref[1, z, part, :] = half * force_ref[1, z, part, :]
            after = jnp.where(lane == NX - 1, 0.0, pltpu.roll(own, NX - 1, 1))
            before = jnp.where(lane == 0, 0.0, pltpu.roll(own, 1, 1))
            for k in range(x_count):
                right = side_is_right(place_ref, k)
                turn = jnp.where(right, NX - 1, NX + 1 - RAD) + NX - RAD * (z + RAD)
                halo = pltpu.roll(edges[4 * k + 3, part, :], lax.rem(turn, NX), 1)
                after = jnp.where(lane == jnp.where(right, NX - 1, -1), halo, after)
                before = jnp.where(lane == jnp.where(right, -1, 0), halo, before)
            force_ref[2, z, part, :] = half * (after - before)
        return 0

    def out(group):
        rows = pl.ds(group * RAD, RAD)
        return [pltpu.make_async_copy(force_ref.at[d, rows], force_hbm.at[d, rows], sems.at[d, group]) for d in range(3)]

    for group in range(NZ // RAD):
        lax.fori_loop(group * RAD, (group + 1) * RAD, plane, 0, unroll=2)
        for copy in out(group):
            copy.start()
    for group in range(NZ // RAD):
        for copy in out(group):
            copy.wait()


def pairings(size):
    even = [(i, i ^ 1) for i in range(size) if (i ^ 1) < size]
    odd = [(i, i + 1 if i % 2 else i - 1) for i in range(1, size)]
    odd = [(i, j) for i, j in odd if j < size]
    return [pairs for pairs in (even, odd) if pairs]


def exchange_planes(side):
    return lax.ppermute(side, "gz", pairings(lax.axis_size("gz"))[0])


def rows_to_send(place, face, side, *packed):
    count = len(pairings(lax.axis_size("gy")))
    return call(
        lambda *refs: rows_kernel(len(packed), *refs),
        (array(NZ + RAD + len(packed), RAD, NX),) * count,
        place,
        face,
        side,
        *packed,
    )


def exchange_rows(sent):
    along = pairings(lax.axis_size("gy"))
    return [lax.ppermute(s, "gy", pairs) for s, pairs in reversed(list(zip(sent, along)))][::-1]


def exchange_columns(columns):
    along = pairings(lax.axis_size("gx"))
    return [lax.ppermute(c, "gx", pairs) for c, pairs in zip(columns, along)]


def pack_columns(place, received, packed):
    count = len(packed)
    rows, *columns = call(
        lambda *refs: columns_kernel(len(received), count, *refs),
        (array(EZ, VY, NX),) + (array(EY, NX),) * count,
        place,
        *received,
        *packed,
    )
    return rows, columns


def per_device(fixed, moving, owners, block_ids, counts, mix_yx, mix_z):
    place = jnp.stack([lax.axis_index("gz"), lax.axis_index("gy") % 2, lax.axis_index("gx") % 2]).astype(jnp.int32)
    count = len(pairings(lax.axis_size("gx")))
    request, near, far, flat = ask(moving, owners, block_ids)
    image, image_side, image_face = widen(place, fixed)
    image_side = exchange_planes(image_side)
    image_packed = call(pack_kernel, (array(NY, NX),) * count, place, image, image_side)
    image_packed = exchange_columns(image_packed)
    received = answer(request, near, far)
    image_sent = rows_to_send(place, image_face, image_side, *image_packed)
    image_halos = exchange_rows(image_sent)
    weights = spread_weights(counts, mix_z)
    image_box, image_sums = call(
        lambda *refs: image_early_kernel(count, *refs),
        (array(3 * NZ, NY, NX), array(2 * NZ, 2 * VY, NX)),
        place,
        image,
        image_side,
        *image_packed,
        scratch=(
            pltpu.VMEM((2 * NZ, NY, NX), F32),
            pltpu.VMEM((2 * NZ, NY, NX), F32),
            pltpu.VMEM((2 * count, NY, NX), F32),
        )
        + LINES,
    )
    received, weights, image_box = lax.optimization_barrier((received, weights, image_box))
    warped, side, face = mix(flat, place, received, weights, mix_yx.reshape(SLOTS, BV, BV))
    side = exchange_planes(side)
    row_halos = exchange_rows(rows_to_send(place, face, side))
    own_sums, out, *packed = call(
        own_kernel,
        (array(3 * NZ, NY, NX), array(NZ * NY, NX)) + (array(NY, NX),) * count,
        place,
        warped,
        side,
        image,
        image_side,
        scratch=(pltpu.SemaphoreType.DMA,),
        out_hbm=1,
    )
    rows, columns = pack_columns(place, row_halos, packed)
    columns = exchange_columns(columns)
    image_patch, box, *image_columns = call(
        lambda *refs: finish_kernel(len(image_halos), count, *refs),
        (array(3 * NZ, 2 * VY, NX), array(3 * NZ, NY, NX)) + (array(EY, NX),) * count,
        place,
        *image_halos,
        *image_packed,
        image_sums,
        image,
        own_sums,
        rows,
        scratch=(
            pltpu.VMEM((EZ, VY, NX), F32),
            pltpu.VMEM((2 * count, 2 * VY, NX), F32),
            pltpu.VMEM((2 * NZ, VY, NX), F32),
            pltpu.VMEM((3 * NZ, VY, NX), F32),
        )
        + LINES,
    )
    (force,) = call(
        lambda *refs: force_kernel(count, *refs),
        (array(3, NZ, NY, NX),),
        place,
        box,
        image_box,
        image_patch,
        warped,
        side,
        rows,
        *columns,
        *image_columns,
        scratch=(
            pltpu.VMEM((4 * count, NY, NX), F32),
            pltpu.VMEM((3, NZ, NY, NX), F32),
            pltpu.SemaphoreType.DMA((3, NZ // RAD)),
        ),
        out_hbm=0,
    )
    return out.reshape(NZ, NY, NX), force


def solution(mesh):
    return jax.shard_map(
        per_device,
        mesh=mesh,
        in_specs=(
            P("gz", "gy", "gx"),
            P("gz", "gy", "gx"),
            P("gz", "gy", "gx", None, None),
            P("gz", "gy", "gx", None),
            P("gz", "gy", "gx", None),
            P("gz", "gy", "gx", None, None, None),
            P("gz", "gy", "gx", None, None, None),
        ),
        out_specs=(P("gz", "gy", "gx"), P(None, "gz", "gy", "gx")),
        check_vma=False,
    )
```
